128 devices in a mesh: row: 16 (over y, z_lo, core), col: 8 (over z_hi, x).
Axes of the slice: x: 4, y: 4, z: 4 (z_hi: 2, z_lo: 2; z = z_hi * 2 + z_lo), core: 2. Of those that a mesh axis runs over, the one named last changes fastest.
Arguments:
- samples: bfloat16 [32768, 8192], P(('row', 'col'))
- labels: int32 [32768], P(('row', 'col')), may hold values from 0 to 1
- basis_start: bfloat16 [8192, 256], replicated, may hold values from -0.0625 to 0.0625
- width_index: int32 [], replicated, may hold values from 0 to 2
Outputs:
- projected: bfloat16 [32768, 256], P(('row', 'col'))
- proof: float32 [32768], P(('row', 'col'))
- basis: bfloat16 [8192, 256], replicated
The draws below stay inside these ranges and needn't reach their ends.
All inputs are finite; a program needn't handle non-finite values.
Results may differ from the reference program's by a relative error of at most 0.011.
Values may be sent and summed in bfloat16 or wider, within the bound.
A program may use at most 128 MiB of HBM per device.

```python
import math
import jax
import jax.numpy as jnp
from jax import lax

D = 8192
K = 256
SAMPLES = 32768


def label_draw(key):
    return jax.random.randint(jax.random.fold_in(key, 11), (SAMPLES,), 0, 2).astype(jnp.int32)


def draw_labels(key, part):
    return label_draw(key)


def draw_samples(key, part):
    marks = label_draw(key).astype(jnp.float32)
    feature_scale = jnp.exp(jax.random.uniform(jax.random.fold_in(key, 12), (D,), jnp.float32, -1.2, 1.1))
    drift = 0.05 * jax.random.normal(jax.random.fold_in(key, 13), (D,), jnp.float32)
    noise = jax.random.normal(jax.random.fold_in(key, 14), (SAMPLES, D), jnp.float32)
    values = noise * feature_scale + marks[:, None] * drift
    return values.astype(jnp.bfloat16)


def bell_draw(own_key, extent, scale, bound, held_as=jnp.bfloat16):
    array = jax.random.normal(own_key, extent, jnp.float32) * scale
    return jnp.minimum(jnp.maximum(array, -bound), bound).astype(held_as)


def setup_inputs(seed: int = 0) -> dict:
    splits = jax.random.split(jax.random.key(seed), 5)
    samples = draw_samples(jax.random.fold_in(splits[4], 71), 0)
    labels = draw_labels(jax.random.fold_in(splits[4], 71), 0)
    basis_start = bell_draw(splits[2], (D, K), D ** -0.5, 0.0625)
    width_index = jax.random.randint(splits[3], (), 0, 3).astype(jnp.int32)
    return {"samples": samples, "labels": labels, "basis_start": basis_start, "width_index": width_index}


def kernel_sums(panel_rows, panel_cols, col_is_ref, width_sq):
    row_norms = jnp.sum(jnp.square(panel_rows.astype(jnp.float32)), 1)
    col_norms = jnp.sum(jnp.square(panel_cols.astype(jnp.float32)), 1)
    block_size = math.gcd(panel_rows.shape[0], 512)

    def block_sums(pieces):
        block_rows, block_norms = pieces
        inner_products = lax.dot_general(block_rows.astype(jnp.float32), panel_cols.astype(jnp.float32), (((1,), (1,)), ((), ())), preferred_element_type=jnp.float32)
        dist_sq = block_norms[:, None] + col_norms[None, :] - 2.0 * inner_products
        kernel = jnp.exp(-dist_sq / (2.0 * width_sq))
        return (jnp.sum(kernel * col_is_ref[None, :], 1), jnp.sum(kernel, 1))
    ref_sums, row_sums = lax.map(block_sums, (panel_rows.reshape(-1, block_size, panel_rows.shape[1]), row_norms.reshape(-1, block_size)))
    return (ref_sums.reshape(-1), row_sums.reshape(-1))

def reference(samples, labels, basis_start, width_index):
    n_total = jnp.float32(SAMPLES)
    is_ref = (labels == 0).astype(jnp.float32)
    n_ref = jnp.sum(is_ref)
    n_cur = n_total - n_ref
    sample_mean = jnp.sum(samples, 0, dtype=jnp.float32) / n_total
    centred = (samples - sample_mean).astype(jnp.bfloat16)
    first = jnp.dot(centred.astype(jnp.float32), basis_start.astype(jnp.float32), preferred_element_type=jnp.float32).astype(jnp.bfloat16)
    gram = lax.dot_general(centred.astype(jnp.float32), first.astype(jnp.float32), (((0,), (0,)), ((), ())), preferred_element_type=jnp.float32) / n_total
    square = jnp.dot(gram.T, gram, precision=lax.Precision.HIGHEST)
    factor = jnp.linalg.cholesky(square)
    basis = jax.scipy.linalg.solve_triangular(factor, gram.T, lower=True).T.astype(jnp.bfloat16)
    projected = jnp.dot(centred.astype(jnp.float32), basis.astype(jnp.float32), preferred_element_type=jnp.float32).astype(jnp.bfloat16)
    width_sq = 128.0 * jnp.exp2(width_index.astype(jnp.float32))
    ref_sums, row_sums = kernel_sums(projected, projected, is_ref, width_sq)
    proof = (ref_sums / n_ref - (row_sums - ref_sums) / n_cur) / (row_sums / n_total)
    return (projected, proof, basis)
```

```python
import functools

import jax
import jax.numpy as jnp
from jax import lax
from jax.experimental import pallas as pl
from jax.experimental.pallas import tpu as pltpu
from jax.sharding import PartitionSpec as P

MESH = pl.DeviceIdType.MESH
F32 = jnp.float32
BF16 = jnp.bfloat16
VMEM = pl.BlockSpec(memory_space=pltpu.VMEM)
HIGHEST = lax.Precision.HIGHEST
LIMIT = 60 * 1024 * 1024

PARTS = ((0, 48, (0, 1, 2)), (48, 48, (1, 2, 0)), (96, 32, (2, 0, 1)))
GATHER = ((0, 32, (2, 1, 0)), (32, 16, (0, 2, 1)), (48, 16, (1, 0, 2)))


def place():
    row, col = lax.axis_index("row"), lax.axis_index("col")
    y, z_lo, core = row // 4, (row // 2) % 2, row % 2
    z_hi, x = col // 4, col % 4
    return (x, y, z_hi * 2 + z_lo), core


def device(at, core):
    x, y, z = at
    return (y * 4 + (z % 2) * 2 + core, (z // 2) * 4 + x)


def moved(at, axis, offset):
    return tuple((c + offset) % 4 if a == axis else c for a, c in enumerate(at))


class Copies:
    def __init__(self, send, recv):
        self.send, self.recv, self.used = send, recv, 0

    def start(self, src, dst, target):
        n = self.used
        self.used += 1
        copy = pltpu.make_async_remote_copy(
            src_ref=src,
            dst_ref=dst,
            send_sem=self.send.at[n],
            recv_sem=self.recv.at[n],
            device_id=target,
            device_id_type=MESH,
        )
        copy.start()
        return copy


def greet(peers):
    barrier = pltpu.get_barrier_semaphore()
    for peer in peers:
        pl.semaphore_signal(barrier, inc=1, device_id=peer, device_id_type=MESH)
    pl.semaphore_wait(barrier, len(peers))


def axis_peers(at, core):
    return [device(moved(at, a, o), core) for a in range(3) for o in (1, 2, 3)]


def pick(axes, at, rows=None):
    index = tuple(at[a] if a in axes else slice(None) for a in range(3))
    return index if rows is None else (*index, rows)


def gram_kernel(
    n_total, x_ref, b_ref, g_ref, s_ref, mean_ref,
    c_ref, local_ref, mhalf, mrecv0, mrecv, daug, gt, half, recv0,
    r1a, r1b, r1c, t1a, t1b, t1c, r2a, r2b, r2c, t2a, t2b, t2c, r3a, r3b, r3c,
    gme, s_half, sr0, sr1, ss1, sr2, ss2, send, recv,
):
    at, core = place()
    x, y, z = at
    other = 1 - core
    copies = Copies(send, recv)
    partner = device(at, other)
    greet([partner, *axis_peers(at, core)])
    n_local, width = x_ref.shape

    @pl.loop(0, width // 256)
    def _(j):
        lanes = pl.ds(pl.multiple_of(j * 256, 256), 256)
        m = jnp.sum(x_ref[:, lanes].astype(F32), 0, keepdims=True) * (1.0 / n_local)
        local_ref[pl.ds(2 * j, 1), :] = m[:, :128]
        local_ref[pl.ds(2 * j + 1, 1), :] = m[:, 128:]

    mine = pl.ds(pl.multiple_of(core * 32, 32), 32)
    theirs = pl.ds(pl.multiple_of(other * 32, 32), 32)
    copy = copies.start(local_ref.at[theirs], mrecv0, partner)

    @pl.loop(0, width // 256)
    def _(j):
        lanes = pl.ds(pl.multiple_of(j * 256, 256), 256)
        rows = local_ref[pl.ds(2 * j, 2), :]
        m = jnp.concatenate([rows[0:1], rows[1:2]], 1)
        c_ref[:, lanes] = (x_ref[:, lanes].astype(F32) - m).astype(BF16)

    first = jnp.zeros((n_local, b_ref.shape[1]), F32)
    pieces = 4
    deep = width // pieces
    copy.wait()
    mhalf[0] = local_ref[mine, :] + mrecv0[...]
    for a in range(3):
        waits = [copies.start(mhalf.at[a], mrecv.at[a, o - 1], device(moved(at, a, o), core)) for o in (1, 2, 3)]
        first += jnp.dot(
            c_ref[:, a * deep : (a + 1) * deep], b_ref[a * deep : (a + 1) * deep, :], preferred_element_type=F32
        )
        for w in waits:
            w.wait()
        mhalf[a + 1] = mhalf[a] + mrecv[a, 0] + mrecv[a, 1] + mrecv[a, 2]
    mhalf[4] = mhalf[3] * (1.0 / 128.0)
    mean_ref[mine, :] = mhalf[4]
    copy = copies.start(mhalf.at[4], mean_ref.at[mine], partner)
    first += jnp.dot(c_ref[:, 3 * deep :], b_ref[3 * deep :, :], preferred_element_type=F32)
    first_t = first.T.astype(BF16)
    copy.wait()

    ids = lax.broadcasted_iota(jnp.int32, (16, 128), 0)

    @pl.loop(0, width // 128)
    def _(j):
        delta = local_ref[pl.ds(j, 1), :] - mean_ref[pl.ds(j, 1), :]
        high = delta.astype(BF16).astype(F32)
        low = delta - high
        tile = jnp.where(ids == 1, low, jnp.where((ids == 0) | (ids == 2), high, 0.0))
        daug[:, pl.ds(pl.multiple_of(j * 128, 128), 128)] = tile.astype(BF16)

    tau = jnp.dot(daug[...], b_ref[...], preferred_element_type=F32)
    tau = (tau[0:1] + tau[1:2]) * float(n_local)
    t_high = tau.astype(BF16).astype(F32)
    ids = lax.broadcasted_iota(jnp.int32, (16, 256), 0)
    taug = jnp.where(ids == 2, tau - t_high, jnp.where(ids < 2, t_high, 0.0))
    taug_t = taug.T.astype(BF16)

    @pl.loop(0, width // 256)
    def _(j):
        lanes = pl.ds(pl.multiple_of(j * 256, 256), 256)
        block = jnp.dot(first_t, c_ref[:, lanes], preferred_element_type=F32)
        block += jnp.dot(taug_t, daug[:, lanes], preferred_element_type=F32)
        block = block.astype(BF16)
        bx, by, bz = j // 8, (j // 2) % 4, (j % 2) * 2
        gt[bx, by, bz] = block[:, :128]
        gt[bx, by, bz + 1] = block[:, 128:]

    near = pl.ds(pl.multiple_of(core * 128, 128), 128)
    far = pl.ds(pl.multiple_of(other * 128, 128), 128)
    copies.start(gt.at[:, :, :, far, :], recv0, partner).wait()

    @pl.loop(0, 64)
    def _(j):
        bx, by, bz = j // 16, (j // 4) % 4, j % 4
        half[bx, by, bz] = (gt[bx, by, bz, near, :].astype(F32) + recv0[bx, by, bz].astype(F32)).astype(BF16)

    parts = list(zip(PARTS, (r1a, r1b, r1c), (t1a, t1b, t1c), (r2a, r2b, r2c), (t2a, t2b, t2c), (r3a, r3b, r3c)))
    waits = []
    for (start, size, order), r1, _, _, _, _ in parts:
        rows = slice(start, start + size)
        for o in (1, 2, 3):
            to = moved(at, order[0], o)
            waits.append(copies.start(half.at[pick(order[:1], to, rows)], r1.at[o - 1], device(to, core)))
    for w in waits:
        w.wait()
    waits = []
    for (start, size, order), r1, t1, r2, _, _ in parts:
        rows = slice(start, start + size)
        own = half.at[pick(order[:1], at, rows)]

        @pl.loop(0, 16)
        def _(j):
            u, v = j // 4, j % 4
            t1[u, v] = (own[u, v].astype(F32) + r1[0, u, v].astype(F32)) + (
                r1[1, u, v].astype(F32) + r1[2, u, v].astype(F32)
            )

        left = [a for a in range(3) if a != order[0]]
        for o in (1, 2, 3):
            to = moved(at, order[1], o)
            index = (to[order[1]],) if left[0] == order[1] else (slice(None), to[order[1]])
            waits.append(copies.start(t1.at[index], r2.at[o - 1], device(to, core)))
    for w in waits:
        w.wait()
    waits = []
    for (start, size, order), _, t1, r2, t2, r3 in parts:
        left = [a for a in range(3) if a != order[0]]
        first_left = left[0] == order[1]
        for k in range(4):
            own = t1[at[order[1]], k] if first_left else t1[k, at[order[1]]]
            t2[k] = (own + r2[0, k]) + (r2[1, k] + r2[2, k])
        for o in (1, 2, 3):
            to = moved(at, order[2], o)
            waits.append(copies.start(t2.at[to[order[2]]], r3.at[o - 1], device(to, core)))
    for w in waits:
        w.wait()
    for (start, size, order), _, _, _, t2, r3 in parts:
        total = (t2[at[order[2]]] + r3[0]) + (r3[1] + r3[2])
        gme[start : start + size, :] = total * (1.0 / n_total)
    g_ref[near, :] = gme[...]
    copies.start(gme, g_ref.at[near], partner).wait()

    square = lax.dot_general(
        gme[...], g_ref[...], (((1,), (1,)), ((), ())), precision=HIGHEST, preferred_element_type=F32
    )
    s_half[0] = square[:, :128]
    s_half[1] = square[:, 128:]
    waits = []
    for o in (1, 2, 3):
        to = moved(at, 0, o)
        rows = pl.ds(pl.multiple_of(to[0] * 32, 32), 32)
        waits.append(copies.start(s_half.at[:, rows, :], sr0.at[o - 1], device(to, core)))
    for w in waits:
        w.wait()
    ss1[...] = (s_half[:, pl.ds(pl.multiple_of(x * 32, 32), 32), :] + sr0[0]) + (sr0[1] + sr0[2])
    waits = []
    for o in (1, 2, 3):
        to = moved(at, 1, o)
        rows = pl.ds(pl.multiple_of(to[1] * 8, 8), 8)
        waits.append(copies.start(ss1.at[:, rows, :], sr1.at[o - 1], device(to, core)))
    for w in waits:
        w.wait()
    ss2[...] = (ss1[:, pl.ds(pl.multiple_of(y * 8, 8), 8), :] + sr1[0]) + (sr1[1] + sr1[2])
    waits = []
    for o in (1, 2, 3):
        waits.append(copies.start(ss2, sr2.at[z], device(moved(at, 2, o), core)))
    sr2[z] = ss2[...]
    for w in waits:
        w.wait()
    base = pl.multiple_of(core * 128 + x * 32 + y * 8, 8)
    s_ref[:, pl.ds(base, 8), :] = (sr2[0] + sr2[1]) + (sr2[2] + sr2[3])
    for axis, rows in (
        (1, pl.ds(base, 8)),
        (0, pl.ds(pl.multiple_of(core * 128 + x * 32, 32), 32)),
    ):
        view = s_ref.at[:, rows, :]
        waits = [copies.start(view, view, device(moved(at, axis, o), core)) for o in (1, 2, 3)]
        for w in waits:
            w.wait()
    view = s_ref.at[:, near, :]
    copies.start(view, view, partner).wait()


def gram_and_square(samples, basis_start, n_total):
    scratch = [
        pltpu.VMEM((256, 8192), BF16),
        pltpu.VMEM((64, 128), F32),
        pltpu.VMEM((5, 32, 128), F32),
        pltpu.VMEM((32, 128), F32),
        pltpu.VMEM((3, 3, 32, 128), F32),
        pltpu.VMEM((16, 8192), BF16),
        pltpu.VMEM((4, 4, 4, 256, 128), BF16),
        pltpu.VMEM((4, 4, 4, 128, 128), BF16),
        pltpu.VMEM((4, 4, 4, 128, 128), BF16),
        *[pltpu.VMEM((3, 4, 4, size, 128), BF16) for _, size, _ in PARTS],
        *[pltpu.VMEM((4, 4, size, 128), F32) for _, size, _ in PARTS],
        *[pltpu.VMEM((3, 4, size, 128), F32) for _, size, _ in PARTS],
        *[pltpu.VMEM((4, size, 128), F32) for _, size, _ in PARTS],
        *[pltpu.VMEM((3, size, 128), F32) for _, size, _ in PARTS],
        pltpu.VMEM((128, 128), F32),
        pltpu.VMEM((2, 128, 128), F32),
        pltpu.VMEM((3, 2, 32, 128), F32),
        pltpu.VMEM((3, 2, 8, 128), F32),
        pltpu.VMEM((2, 32, 128), F32),
        pltpu.VMEM((4, 2, 8, 128), F32),
        pltpu.VMEM((2, 8, 128), F32),
        pltpu.SemaphoreType.DMA((56,)),
        pltpu.SemaphoreType.DMA((56,)),
    ]
    return pl.pallas_call(
        functools.partial(gram_kernel, n_total),
        out_shape=(
            jax.ShapeDtypeStruct((256, 128), F32),
            jax.ShapeDtypeStruct((2, 256, 128), F32),
            jax.ShapeDtypeStruct((64, 128), F32),
        ),
        in_specs=[VMEM, VMEM],
        out_specs=(VMEM, VMEM, VMEM),
        scratch_shapes=scratch,
        compiler_params=pltpu.CompilerParams(collective_id=0, has_side_effects=True, vmem_limit_bytes=LIMIT),
        name="gram",
    )(samples, basis_start)


def basis_kernel(g_ref, inv_ref, out_ref, send, recv):
    at, core = place()
    copies = Copies(send, recv)
    partner = device(at, 1 - core)
    greet([partner, *axis_peers(at, core)])
    block = lax.dot_general(
        g_ref[...], inv_ref[...], (((0,), (1,)), ((), ())), precision=HIGHEST, preferred_element_type=F32
    ).astype(BF16)
    out_ref[at[0], at[1], at[2], core] = jnp.where(core == 0, block[:64], block[64:])
    for step in range(3):
        waits = []
        for start, size, order in GATHER:
            fixed = order[step:]
            view = out_ref.at[(*pick(fixed, at), core, slice(start, start + size))]
            for o in (1, 2, 3):
                waits.append(copies.start(view, view, device(moved(at, order[step], o), core)))
        for w in waits:
            w.wait()
    waits = []
    for o in range(4):
        bx = (at[0] + o) % 4
        view = out_ref.at[bx, :, :, core]
        waits.append(copies.start(view, view, partner))
    for w in waits:
        w.wait()


def gather_basis(g, inverse):
    out = pl.pallas_call(
        basis_kernel,
        out_shape=jax.ShapeDtypeStruct((4, 4, 4, 2, 64, 256), BF16),
        in_specs=[VMEM, VMEM],
        out_specs=VMEM,
        scratch_shapes=[pltpu.SemaphoreType.DMA((31,)), pltpu.SemaphoreType.DMA((31,))],
        compiler_params=pltpu.CompilerParams(collective_id=1, has_side_effects=True, vmem_limit_bytes=LIMIT),
        name="basis",
    )(g, inverse)
    return out.reshape(8192, 256)


def proof_kernel(
    n_total, width_ref, p_ref, label_ref, out_ref,
    rowp, colp, negrow, acc_all, acc_ref, pay, got, send, recv,
):
    at, core = place()
    x, y, z = at
    z_lo, z_hi = z % 2, z // 2
    copies = Copies(send, recv)
    partner = device(at, 1 - core)
    me_row, me_col = lax.axis_index("row"), lax.axis_index("col")
    rows = [((x + o) % 4, (z_hi + h) % 2) for h in (0, 1) for o in (0, 1, 2, 3)]
    cols = [((y + o) % 4, (z_lo + h) % 2) for h in (0, 1) for o in (0, 1, 2, 3)]
    row_devices = [device((rx, y, rh * 2 + z_lo), core) for rx, rh in rows]
    col_devices = [device((x, cy, z_hi * 2 + cl), core) for cy, cl in cols]
    greet([partner, *row_devices[1:], *col_devices[1:]])

    is_ref = (label_ref[...] == 0).astype(F32)
    mine_row, mine_col = rowp.at[me_col], colp.at[me_row]
    tail = jnp.broadcast_to(is_ref, (16, 256)).astype(BF16)
    mine_row[0:256, :] = p_ref[...]
    mine_row[256:272, :] = tail
    mine_col[0:256, :] = p_ref[...]
    mine_col[256:272, :] = tail
    row_waits = [copies.start(mine_row, mine_row, d) for d in row_devices[1:]]
    col_waits = [copies.start(mine_col, mine_col, d) for d in col_devices[1:]]
    core_waits = [copies.start(mine_col, mine_col, partner)]
    for (cy, cl), o, h, w in zip(cols[1:], (1, 2, 3, 0, 1, 2, 3), (0, 0, 0, 1, 1, 1, 1), col_waits):
        w.wait()
        slot = ((y + 4 - o) % 4) * 4 + ((z_lo + h) % 2) * 2 + core
        view = colp.at[slot]
        core_waits.append(copies.start(view, view, partner))
    for w in row_waits:
        w.wait()

    scale = 1.4426950408889634 / (128.0 * jnp.exp2(jnp.full((1, 256), width_ref[0], jnp.int32).astype(F32)))
    ones = jnp.ones((8, 256), F32)
    for q in range(8):
        p = rowp[q, 0:256, :].astype(F32)
        norm = lax.dot_general(ones, p * p, (((1,), (1,)), ((), ())), precision=HIGHEST, preferred_element_type=F32)
        negrow[q] = norm * -0.5
        acc_all[q] = jnp.zeros((8, 256), F32)
        acc_ref[q] = jnp.zeros((8, 256), F32)
    for w in core_waits:
        w.wait()

    def column(r, count):
        block = colp[r, 0:256, :]
        p = block.astype(F32)
        half_norm = jnp.sum(p * p, 1, keepdims=True) * -0.5
        mark_row = colp[r, 256:272, :].astype(F32)[0:1]
        mark = jnp.concatenate(
            [jnp.broadcast_to(mark_row[:, :128], (128, 128)).T, jnp.broadcast_to(mark_row[:, 128:], (128, 128)).T], 0
        )
        mark = jnp.concatenate([mark, mark], 1)

        def row_block(q, carry):
            inner = lax.dot_general(
                block, rowp[q, 0:256, :], (((1,), (1,)), ((), ())), preferred_element_type=F32
            )
            value = jnp.exp2(((inner + half_norm) + negrow[q][0:1]) * scale)
            acc_all[q] += jnp.sum(value.reshape(32, 8, 256), 0)
            acc_ref[q] += jnp.sum((value * mark).reshape(32, 8, 256), 0)
            return carry

        lax.fori_loop(0, 8, row_block, 0)
        return count + mark_row

    count = lax.fori_loop(0, 16, column, jnp.zeros((1, 256), F32))
    ids = lax.broadcasted_iota(jnp.int32, (8, 256), 0)
    for q in range(8):
        total = jnp.sum(acc_all[q], 0, keepdims=True)
        refs = jnp.sum(acc_ref[q], 0, keepdims=True)
        pay[q] = jnp.where(ids == 0, total, jnp.where(ids == 1, refs, count))
    waits = []
    for (rx, rh), d in zip(rows[1:], row_devices[1:]):
        waits.append(copies.start(pay.at[rh * 4 + rx], got.at[me_col], d))
    got[me_col] = pay[me_col]
    for w in waits:
        w.wait()
    total = jnp.sum(got[...], 0)
    row_sums, ref_sums = total[0:1], total[1:2]
    n_ref = jnp.sum(total[2:3], 1, keepdims=True)
    n_cur = n_total - n_ref
    proof = (ref_sums / n_ref - (row_sums - ref_sums) / n_cur) / (row_sums / n_total)
    out_ref[...] = jnp.broadcast_to(proof, (8, 256))


def proof_values(projected, labels, width_index, n_total):
    out = pl.pallas_call(
        functools.partial(proof_kernel, n_total),
        out_shape=jax.ShapeDtypeStruct((8, 256), F32),
        in_specs=[pl.BlockSpec(memory_space=pltpu.SMEM), VMEM, VMEM],
        out_specs=VMEM,
        scratch_shapes=[
            pltpu.VMEM((8, 272, 256), BF16),
            pltpu.VMEM((16, 272, 256), BF16),
            pltpu.VMEM((8, 8, 256), F32),
            pltpu.VMEM((8, 8, 256), F32),
            pltpu.VMEM((8, 8, 256), F32),
            pltpu.VMEM((8, 8, 256), F32),
            pltpu.VMEM((8, 8, 256), F32),
            pltpu.SemaphoreType.DMA((29,)),
            pltpu.SemaphoreType.DMA((29,)),
        ],
        compiler_params=pltpu.CompilerParams(collective_id=2, has_side_effects=True, vmem_limit_bytes=LIMIT),
        name="proof",
    )(width_index.reshape(1), projected, labels.reshape(1, 256))
    return out[0]


def local(n_total, samples, labels, basis_start, width_index):
    g, square, mean = gram_and_square(samples, basis_start, n_total)
    square = jnp.concatenate([square[0], square[1]], 1)
    factor = jnp.linalg.cholesky(square)
    inverse = jax.scipy.linalg.solve_triangular(factor, jnp.eye(256, dtype=F32), lower=True)
    basis = gather_basis(g, inverse)
    centred = (samples - mean.reshape(1, 8192)).astype(BF16)
    projected = jnp.dot(centred, basis, preferred_element_type=F32).astype(BF16)
    proof = proof_values(projected, labels, width_index, n_total)
    return projected, proof, basis


def solution(mesh):
    n_total = float(256 * mesh.size)
    placed = (P(("row", "col"), None), P(("row", "col")), P(), P())
    return jax.shard_map(
        functools.partial(local, n_total),
        mesh=mesh,
        in_specs=placed,
        out_specs=(P(("row", "col"), None), P(("row", "col")), P()),
        check_vma=False,
    )
```

```python
import functools

import jax
import jax.numpy as jnp
from jax import lax
from jax.experimental import pallas as pl
from jax.experimental.pallas import tpu as pltpu
from jax.sharding import PartitionSpec as P

MESH = pl.DeviceIdType.MESH
F32 = jnp.float32
BF16 = jnp.bfloat16
VMEM = pl.BlockSpec(memory_space=pltpu.VMEM)
HIGHEST = lax.Precision.HIGHEST
LIMIT = 60 * 1024 * 1024

PARTS = ((0, 48, (0, 1, 2)), (48, 48, (1, 2, 0)), (96, 32, (2, 0, 1)))
GATHER = ((0, 32, (2, 1, 0)), (32, 16, (0, 2, 1)), (48, 16, (1, 0, 2)))


def place():
    row, col = lax.axis_index("row"), lax.axis_index("col")
    y, z_lo, core = row // 4, (row // 2) % 2, row % 2
    z_hi, x = col // 4, col % 4
    return (x, y, z_hi * 2 + z_lo), core


def device(at, core):
    x, y, z = at
    return (y * 4 + (z % 2) * 2 + core, (z // 2) * 4 + x)


def moved(at, axis, offset):
    return tuple((c + offset) % 4 if a == axis else c for a, c in enumerate(at))


class Copies:
    def __init__(self, send, recv):
        self.send, self.recv, self.used = send, recv, 0

    def start(self, src, dst, target):
        n = self.used
        self.used += 1
        copy = pltpu.make_async_remote_copy(
            src_ref=src,
            dst_ref=dst,
            send_sem=self.send.at[n],
            recv_sem=self.recv.at[n],
            device_id=target,
            device_id_type=MESH,
        )
        copy.start()
        return copy


def greet(peers):
    barrier = pltpu.get_barrier_semaphore()
    for peer in peers:
        pl.semaphore_signal(barrier, inc=1, device_id=peer, device_id_type=MESH)
    pl.semaphore_wait(barrier, len(peers))


def axis_peers(at, core):
    return [device(moved(at, a, o), core) for a in range(3) for o in (1, 2, 3)]


def pick(axes, at, rows=None):
    index = tuple(at[a] if a in axes else slice(None) for a in range(3))
    return index if rows is None else (*index, rows)


def gram_kernel(
    n_total, x_ref, b_ref, g_ref, s_ref, mean_ref,
    c_ref, local_ref, mhalf, mrecv0, mrecv, daug, gt, half, recv0,
    r1a, r1b, r1c, t1a, t1b, t1c, r2a, r2b, r2c, t2a, t2b, t2c, r3a, r3b, r3c,
    gme, s_half, sr0, sr1, ss1, sr2, ss2, send, recv,
):
    at, core = place()
    x, y, z = at
    other = 1 - core
    copies = Copies(send, recv)
    partner = device(at, other)
    greet([partner, *axis_peers(at, core)])
    n_local, width = x_ref.shape

    @pl.loop(0, width // 256)
    def _(j):
        lanes = pl.ds(pl.multiple_of(j * 256, 256), 256)
        m = jnp.sum(x_ref[:, lanes].astype(F32), 0, keepdims=True) * (1.0 / n_local)
        local_ref[pl.ds(2 * j, 1), :] = m[:, :128]
        local_ref[pl.ds(2 * j + 1, 1), :] = m[:, 128:]

    mine = pl.ds(pl.multiple_of(core * 32, 32), 32)
    theirs = pl.ds(pl.multiple_of(other * 32, 32), 32)
    copy = copies.start(local_ref.at[theirs], mrecv0, partner)

    @pl.loop(0, width // 256)
    def _(j):
        lanes = pl.ds(pl.multiple_of(j * 256, 256), 256)
        rows = local_ref[pl.ds(2 * j, 2), :]
        m = jnp.concatenate([rows[0:1], rows[1:2]], 1)
        c_ref[:, lanes] = (x_ref[:, lanes].astype(F32) - m).astype(BF16)

    first = jnp.zeros((n_local, b_ref.shape[1]), F32)
    pieces = 4
    deep = width // pieces
    copy.wait()
    mhalf[0] = local_ref[mine, :] + mrecv0[...]
    for a in range(3):
        waits = [copies.start(mhalf.at[a], mrecv.at[a, o - 1], device(moved(at, a, o), core)) for o in (1, 2, 3)]
        first += jnp.dot(
            c_ref[:, a * deep : (a + 1) * deep], b_ref[a * deep : (a + 1) * deep, :], preferred_element_type=F32
        )
        for w in waits:
            w.wait()
        mhalf[a + 1] = mhalf[a] + mrecv[a, 0] + mrecv[a, 1] + mrecv[a, 2]
    mhalf[4] = mhalf[3] * (1.0 / 128.0)
    mean_ref[mine, :] = mhalf[4]
    copy = copies.start(mhalf.at[4], mean_ref.at[mine], partner)
    first += jnp.dot(c_ref[:, 3 * deep :], b_ref[3 * deep :, :], preferred_element_type=F32)
    first_t = first.T.astype(BF16)
    copy.wait()

    ids = lax.broadcasted_iota(jnp.int32, (16, 128), 0)

    @pl.loop(0, width // 128)
    def _(j):
        delta = local_ref[pl.ds(j, 1), :] - mean_ref[pl.ds(j, 1), :]
        high = delta.astype(BF16).astype(F32)
        low = delta - high
        tile = jnp.where(ids == 1, low, jnp.where((ids == 0) | (ids == 2), high, 0.0))
        daug[:, pl.ds(pl.multiple_of(j * 128, 128), 128)] = tile.astype(BF16)

    tau = jnp.dot(daug[...], b_ref[...], preferred_element_type=F32)
    tau = (tau[0:1] + tau[1:2]) * float(n_local)
    t_high = tau.astype(BF16).astype(F32)
    ids = lax.broadcasted_iota(jnp.int32, (16, 256), 0)
    taug = jnp.where(ids == 2, tau - t_high, jnp.where(ids < 2, t_high, 0.0))
    taug_t = taug.T.astype(BF16)

    @pl.loop(0, width // 256)
    def _(j):
        lanes = pl.ds(pl.multiple_of(j * 256, 256), 256)
        block = jnp.dot(first_t, c_ref[:, lanes], preferred_element_type=F32)
        block += jnp.dot(taug_t, daug[:, lanes], preferred_element_type=F32)
        block = block.astype(BF16)
        bx, by, bz = j // 8, (j // 2) % 4, (j % 2) * 2
        gt[bx, by, bz] = block[:, :128]
        gt[bx, by, bz + 1] = block[:, 128:]

    near = pl.ds(pl.multiple_of(core * 128, 128), 128)
    far = pl.ds(pl.multiple_of(other * 128, 128), 128)
    copies.start(gt.at[:, :, :, far, :], recv0, partner).wait()

    @pl.loop(0, 64)
    def _(j):
        bx, by, bz = j // 16, (j // 4) % 4, j % 4
        half[bx, by, bz] = (gt[bx, by, bz, near, :].astype(F32) + recv0[bx, by, bz].astype(F32)).astype(BF16)

    parts = list(zip(PARTS, (r1a, r1b, r1c), (t1a, t1b, t1c), (r2a, r2b, r2c), (t2a, t2b, t2c), (r3a, r3b, r3c)))
    waits = []
    for (start, size, order), r1, _, _, _, _ in parts:
        rows = slice(start, start + size)
        for o in (1, 2, 3):
            to = moved(at, order[0], o)
            waits.append(copies.start(half.at[pick(order[:1], to, rows)], r1.at[o - 1], device(to, core)))
    for w in waits:
        w.wait()
    waits = []
    for (start, size, order), r1, t1, r2, _, _ in parts:
        rows = slice(start, start + size)
        own = half.at[pick(order[:1], at, rows)]

        @pl.loop(0, 16)
        def _(j):
            u, v = j // 4, j % 4
            t1[u, v] = (own[u, v].astype(F32) + r1[0, u, v].astype(F32)) + (
                r1[1, u, v].astype(F32) + r1[2, u, v].astype(F32)
            )

        left = [a for a in range(3) if a != order[0]]
        for o in (1, 2, 3):
            to = moved(at, order[1], o)
            index = (to[order[1]],) if left[0] == order[1] else (slice(None), to[order[1]])
            waits.append(copies.start(t1.at[index], r2.at[o - 1], device(to, core)))
    for w in waits:
        w.wait()
    waits = []
    for (start, size, order), _, t1, r2, t2, r3 in parts:
        left = [a for a in range(3) if a != order[0]]
        first_left = left[0] == order[1]
        for k in range(4):
            own = t1[at[order[1]], k] if first_left else t1[k, at[order[1]]]
            t2[k] = (own + r2[0, k]) + (r2[1, k] + r2[2, k])
        for o in (1, 2, 3):
            to = moved(at, order[2], o)
            waits.append(copies.start(t2.at[to[order[2]]], r3.at[o - 1], device(to, core)))
    for w in waits:
        w.wait()
    for (start, size, order), _, _, _, t2, r3 in parts:
        total = (t2[at[order[2]]] + r3[0]) + (r3[1] + r3[2])
        gme[start : start + size, :] = total * (1.0 / n_total)
    g_ref[near, :] = gme[...]
    copies.start(gme, g_ref.at[near], partner).wait()

    square = lax.dot_general(
        gme[...], g_ref[...], (((1,), (1,)), ((), ())), precision=HIGHEST, preferred_element_type=F32
    )
    s_half[0] = square[:, :128]
    s_half[1] = square[:, 128:]
    waits = []
    for o in (1, 2, 3):
        to = moved(at, 0, o)
        rows = pl.ds(pl.multiple_of(to[0] * 32, 32), 32)
        waits.append(copies.start(s_half.at[:, rows, :], sr0.at[o - 1], device(to, core)))
    for w in waits:
        w.wait()
    ss1[...] = (s_half[:, pl.ds(pl.multiple_of(x * 32, 32), 32), :] + sr0[0]) + (sr0[1] + sr0[2])
    waits = []
    for o in (1, 2, 3):
        to = moved(at, 1, o)
        rows = pl.ds(pl.multiple_of(to[1] * 8, 8), 8)
        waits.append(copies.start(ss1.at[:, rows, :], sr1.at[o - 1], device(to, core)))
    for w in waits:
        w.wait()
    ss2[...] = (ss1[:, pl.ds(pl.multiple_of(y * 8, 8), 8), :] + sr1[0]) + (sr1[1] + sr1[2])
    waits = []
    for o in (1, 2, 3):
        waits.append(copies.start(ss2, sr2.at[z], device(moved(at, 2, o), core)))
    sr2[z] = ss2[...]
    for w in waits:
        w.wait()
    base = pl.multiple_of(core * 128 + x * 32 + y * 8, 8)
    s_ref[:, pl.ds(base, 8), :] = (sr2[0] + sr2[1]) + (sr2[2] + sr2[3])
    for axis, rows in (
        (1, pl.ds(base, 8)),
        (0, pl.ds(pl.multiple_of(core * 128 + x * 32, 32), 32)),
    ):
        view = s_ref.at[:, rows, :]
        waits = [copies.start(view, view, device(moved(at, axis, o), core)) for o in (1, 2, 3)]
        for w in waits:
            w.wait()
    view = s_ref.at[:, near, :]
    copies.start(view, view, partner).wait()


def gram_and_square(samples, basis_start, n_total):
    scratch = [
        pltpu.VMEM((256, 8192), BF16),
        pltpu.VMEM((64, 128), F32),
        pltpu.VMEM((5, 32, 128), F32),
        pltpu.VMEM((32, 128), F32),
        pltpu.VMEM((3, 3, 32, 128), F32),
        pltpu.VMEM((16, 8192), BF16),
        pltpu.VMEM((4, 4, 4, 256, 128), BF16),
        pltpu.VMEM((4, 4, 4, 128, 128), BF16),
        pltpu.VMEM((4, 4, 4, 128, 128), BF16),
        *[pltpu.VMEM((3, 4, 4, size, 128), BF16) for _, size, _ in PARTS],
        *[pltpu.VMEM((4, 4, size, 128), F32) for _, size, _ in PARTS],
        *[pltpu.VMEM((3, 4, size, 128), F32) for _, size, _ in PARTS],
        *[pltpu.VMEM((4, size, 128), F32) for _, size, _ in PARTS],
        *[pltpu.VMEM((3, size, 128), F32) for _, size, _ in PARTS],
        pltpu.VMEM((128, 128), F32),
        pltpu.VMEM((2, 128, 128), F32),
        pltpu.VMEM((3, 2, 32, 128), F32),
        pltpu.VMEM((3, 2, 8, 128), F32),
        pltpu.VMEM((2, 32, 128), F32),
        pltpu.VMEM((4, 2, 8, 128), F32),
        pltpu.VMEM((2, 8, 128), F32),
        pltpu.SemaphoreType.DMA((56,)),
        pltpu.SemaphoreType.DMA((56,)),
    ]
    return pl.pallas_call(
        functools.partial(gram_kernel, n_total),
        out_shape=(
            jax.ShapeDtypeStruct((256, 128), F32),
            jax.ShapeDtypeStruct((2, 256, 128), F32),
            jax.ShapeDtypeStruct((64, 128), F32),
        ),
        in_specs=[VMEM, VMEM],
        out_specs=(VMEM, VMEM, VMEM),
        scratch_shapes=scratch,
        compiler_params=pltpu.CompilerParams(collective_id=0, has_side_effects=True, vmem_limit_bytes=LIMIT),
        name="gram",
    )(samples, basis_start)


def small_inverse(t):
    sub = lax.broadcasted_iota(jnp.int32, (8, 128), 0)
    t = list(t)
    for s in range(4):
        rows = [jnp.broadcast_to(t[s][i : i + 1, :], (8, 128)) for i in range(8)]
        e = [[jnp.broadcast_to(rows[i][:, 8 * s + j : 8 * s + j + 1], (8, 128)) for j in range(i + 1)] for i in range(8)]
        inv, low = [], [[None] * 8 for _ in range(8)]
        for j in range(8):
            inv.append(1.0 / e[j][j])
            for i in range(j + 1, 8):
                low[i][j] = e[i][j] * inv[j]
            for i in range(j + 1, 8):
                for m in range(j + 1, i + 1):
                    e[i][m] = e[i][m] - low[i][j] * e[m][j]
        w = []
        for i in range(8):
            v = rows[i]
            for j in range(i):
                v = v - low[i][j] * w[j]
            w.append(v)
        for b in range(s + 1, 4):
            f = []
            for j in range(8):
                v = jnp.broadcast_to(t[b][:, 8 * s + j : 8 * s + j + 1], (8, 128))
                for k in range(j):
                    v = v - f[k] * e[j][k]
                f.append(v * inv[j])
            for j in range(8):
                t[b] = t[b] - f[j] * w[j]
        out = w[0] * lax.rsqrt(e[0][0])
        for i in range(1, 8):
            out = jnp.where(sub == i, w[i] * lax.rsqrt(e[i][i]), out)
        t[s] = out
    return t


def inverse_factor(s_ref, m_ref):
    r = lax.broadcasted_iota(jnp.int32, (256, 256), 0)
    c = lax.broadcasted_iota(jnp.int32, (256, 256), 1)
    m_ref[:, 0:128] = s_ref[0]
    m_ref[:, 128:256] = s_ref[1]
    m_ref[:, 256:512] = (r == c).astype(F32)
    lane = lax.broadcasted_iota(jnp.int32, (32, 128), 1)
    unit = (lane == lax.broadcasted_iota(jnp.int32, (32, 128), 0) + 32).astype(F32)
    wide = lax.broadcasted_iota(jnp.int32, (32, 256), 1)

    def panel(b, carry):
        rows = pl.ds(pl.multiple_of(b * 32, 32), 32)
        tile = m_ref[rows, pl.ds(pl.multiple_of((b // 4) * 128, 128), 128)]
        tile = pltpu.roll(tile, (4 - b % 4) % 4 * 32, 1)
        tile = jnp.where(lane < 32, tile, unit)
        t = small_inverse([tile[8 * i : 8 * i + 8] for i in range(4)])
        inv = jnp.concatenate(t, 0)[:, 32:64]
        w = jnp.dot(inv, m_ref[rows, :], precision=HIGHEST, preferred_element_type=F32)
        left = jnp.where(wide >= (b + 1) * 32, w[:, :256], 0.0)
        m_ref[...] -= lax.dot_general(left, w, (((0,), (0,)), ((), ())), precision=HIGHEST, preferred_element_type=F32)
        m_ref[rows, :] = w
        return carry

    lax.fori_loop(0, 8, panel, 0)


def basis_kernel(g_ref, s_ref, out_ref, m_ref, send, recv):
    at, core = place()
    copies = Copies(send, recv)
    partner = device(at, 1 - core)
    greet([partner, *axis_peers(at, core)])
    inverse_factor(s_ref, m_ref)
    block = lax.dot_general(
        g_ref[...], m_ref[:, 256:512], (((0,), (1,)), ((), ())), precision=HIGHEST, preferred_element_type=F32
    ).astype(BF16)
    out_ref[at[0], at[1], at[2], core] = jnp.where(core == 0, block[:64], block[64:])
    for step in range(3):
        waits = []
        for start, size, order in GATHER:
            fixed = order[step:]
            view = out_ref.at[(*pick(fixed, at), core, slice(start, start + size))]
            for o in (1, 2, 3):
                waits.append(copies.start(view, view, device(moved(at, order[step], o), core)))
        for w in waits:
            w.wait()
    waits = []
    for o in range(4):
        bx = (at[0] + o) % 4
        view = out_ref.at[bx, :, :, core]
        waits.append(copies.start(view, view, partner))
    for w in waits:
        w.wait()


def gather_basis(g, square):
    out = pl.pallas_call(
        basis_kernel,
        out_shape=jax.ShapeDtypeStruct((4, 4, 4, 2, 64, 256), BF16),
        in_specs=[VMEM, VMEM],
        out_specs=VMEM,
        scratch_shapes=[pltpu.VMEM((256, 512), F32), pltpu.SemaphoreType.DMA((31,)), pltpu.SemaphoreType.DMA((31,))],
        compiler_params=pltpu.CompilerParams(collective_id=1, has_side_effects=True, vmem_limit_bytes=LIMIT),
        name="basis",
    )(g, square)
    return out.reshape(8192, 256)


def proof_kernel(
    n_total, width_ref, p_ref, label_ref, out_ref,
    rowp, colp, negrow, acc_all, acc_ref, pay, got, send, recv,
):
    at, core = place()
    x, y, z = at
    z_lo, z_hi = z % 2, z // 2
    copies = Copies(send, recv)
    partner = device(at, 1 - core)
    me_row, me_col = lax.axis_index("row"), lax.axis_index("col")
    rows = [((x + o) % 4, (z_hi + h) % 2) for h in (0, 1) for o in (0, 1, 2, 3)]
    cols = [((y + o) % 4, (z_lo + h) % 2) for h in (0, 1) for o in (0, 1, 2, 3)]
    row_devices = [device((rx, y, rh * 2 + z_lo), core) for rx, rh in rows]
    col_devices = [device((x, cy, z_hi * 2 + cl), core) for cy, cl in cols]
    greet([partner, *row_devices[1:], *col_devices[1:]])

    is_ref = (label_ref[...] == 0).astype(F32)
    mine_row, mine_col = rowp.at[me_col], colp.at[me_row]
    tail = jnp.broadcast_to(is_ref, (16, 256)).astype(BF16)
    mine_row[0:256, :] = p_ref[...]
    mine_row[256:272, :] = tail
    mine_col[0:256, :] = p_ref[...]
    mine_col[256:272, :] = tail
    row_waits = [copies.start(mine_row, mine_row, d) for d in row_devices[1:]]
    col_waits = [copies.start(mine_col, mine_col, d) for d in col_devices[1:]]
    core_waits = [copies.start(mine_col, mine_col, partner)]
    for (cy, cl), o, h, w in zip(cols[1:], (1, 2, 3, 0, 1, 2, 3), (0, 0, 0, 1, 1, 1, 1), col_waits):
        w.wait()
        slot = ((y + 4 - o) % 4) * 4 + ((z_lo + h) % 2) * 2 + core
        view = colp.at[slot]
        core_waits.append(copies.start(view, view, partner))
    for w in row_waits:
        w.wait()

    scale = 1.4426950408889634 / (128.0 * jnp.exp2(jnp.full((1, 256), width_ref[0], jnp.int32).astype(F32)))
    ones = jnp.ones((8, 256), F32)
    for q in range(8):
        p = rowp[q, 0:256, :].astype(F32)
        norm = lax.dot_general(ones, p * p, (((1,), (1,)), ((), ())), precision=HIGHEST, preferred_element_type=F32)
        negrow[q] = norm * -0.5
        acc_all[q] = jnp.zeros((8, 256), F32)
        acc_ref[q] = jnp.zeros((8, 256), F32)
    for w in core_waits:
        w.wait()

    def column(r, count):
        block = colp[r, 0:256, :]
        p = block.astype(F32)
        half_norm = jnp.sum(p * p, 1, keepdims=True) * -0.5
        mark_row = colp[r, 256:272, :].astype(F32)[0:1]
        mark = jnp.concatenate(
            [jnp.broadcast_to(mark_row[:, :128], (128, 128)).T, jnp.broadcast_to(mark_row[:, 128:], (128, 128)).T], 0
        )
        mark = jnp.concatenate([mark, mark], 1)

        def row_block(q, carry):
            inner = lax.dot_general(
                block, rowp[q, 0:256, :], (((1,), (1,)), ((), ())), preferred_element_type=F32
            )
            value = jnp.exp2(((inner + half_norm) + negrow[q][0:1]) * scale)
            acc_all[q] += jnp.sum(value.reshape(32, 8, 256), 0)
            acc_ref[q] += jnp.sum((value * mark).reshape(32, 8, 256), 0)
            return carry

        lax.fori_loop(0, 8, row_block, 0)
        return count + mark_row

    count = lax.fori_loop(0, 16, column, jnp.zeros((1, 256), F32))
    ids = lax.broadcasted_iota(jnp.int32, (8, 256), 0)
    for q in range(8):
        total = jnp.sum(acc_all[q], 0, keepdims=True)
        refs = jnp.sum(acc_ref[q], 0, keepdims=True)
        pay[q] = jnp.where(ids == 0, total, jnp.where(ids == 1, refs, count))
    waits = []
    for (rx, rh), d in zip(rows[1:], row_devices[1:]):
        waits.append(copies.start(pay.at[rh * 4 + rx], got.at[me_col], d))
    got[me_col] = pay[me_col]
    for w in waits:
        w.wait()
    total = jnp.sum(got[...], 0)
    row_sums, ref_sums = total[0:1], total[1:2]
    n_ref = jnp.sum(total[2:3], 1, keepdims=True)
    n_cur = n_total - n_ref
    proof = (ref_sums / n_ref - (row_sums - ref_sums) / n_cur) / (row_sums / n_total)
    out_ref[...] = jnp.broadcast_to(proof, (8, 256))


def proof_values(projected, labels, width_index, n_total):
    out = pl.pallas_call(
        functools.partial(proof_kernel, n_total),
        out_shape=jax.ShapeDtypeStruct((8, 256), F32),
        in_specs=[pl.BlockSpec(memory_space=pltpu.SMEM), VMEM, VMEM],
        out_specs=VMEM,
        scratch_shapes=[
            pltpu.VMEM((8, 272, 256), BF16),
            pltpu.VMEM((16, 272, 256), BF16),
            pltpu.VMEM((8, 8, 256), F32),
            pltpu.VMEM((8, 8, 256), F32),
            pltpu.VMEM((8, 8, 256), F32),
            pltpu.VMEM((8, 8, 256), F32),
            pltpu.VMEM((8, 8, 256), F32),
            pltpu.SemaphoreType.DMA((29,)),
            pltpu.SemaphoreType.DMA((29,)),
        ],
        compiler_params=pltpu.CompilerParams(collective_id=2, has_side_effects=True, vmem_limit_bytes=LIMIT),
        name="proof",
    )(width_index.reshape(1), projected, labels.reshape(1, 256))
    return out[0]


def local(n_total, samples, labels, basis_start, width_index):
    g, square, mean = gram_and_square(samples, basis_start, n_total)
    basis = gather_basis(g, square)
    centred = (samples - mean.reshape(1, 8192)).astype(BF16)
    projected = jnp.dot(centred, basis, preferred_element_type=F32).astype(BF16)
    proof = proof_values(projected, labels, width_index, n_total)
    return projected, proof, basis


def solution(mesh):
    n_total = float(256 * mesh.size)
    placed = (P(("row", "col"), None), P(("row", "col")), P(), P())
    return jax.shard_map(
        functools.partial(local, n_total),
        mesh=mesh,
        in_specs=placed,
        out_specs=(P(("row", "col"), None), P(("row", "col")), P()),
        check_vma=False,
    )
```

```python
import functools

import jax
import jax.numpy as jnp
from jax import lax
from jax.experimental import pallas as pl
from jax.experimental.pallas import tpu as pltpu
from jax.sharding import PartitionSpec as P

MESH = pl.DeviceIdType.MESH
F32 = jnp.float32
BF16 = jnp.bfloat16
VMEM = pl.BlockSpec(memory_space=pltpu.VMEM)
HIGHEST = lax.Precision.HIGHEST
LIMIT = 60 * 1024 * 1024

PARTS = ((0, 48, (0, 1, 2)), (48, 48, (1, 2, 0)), (96, 32, (2, 0, 1)))
GATHER = ((0, 32, (2, 1, 0)), (32, 16, (0, 2, 1)), (48, 16, (1, 0, 2)))


def place():
    row, col = lax.axis_index("row"), lax.axis_index("col")
    y, z_lo, core = row // 4, (row // 2) % 2, row % 2
    z_hi, x = col // 4, col % 4
    return (x, y, z_hi * 2 + z_lo), core


def device(at, core):
    x, y, z = at
    return (y * 4 + (z % 2) * 2 + core, (z // 2) * 4 + x)


def moved(at, axis, offset):
    return tuple((c + offset) % 4 if a == axis else c for a, c in enumerate(at))


class Copies:
    def __init__(self, send, recv):
        self.send, self.recv, self.used = send, recv, 0

    def start(self, src, dst, target):
        n = self.used
        self.used += 1
        copy = pltpu.make_async_remote_copy(
            src_ref=src,
            dst_ref=dst,
            send_sem=self.send.at[n],
            recv_sem=self.recv.at[n],
            device_id=target,
            device_id_type=MESH,
        )
        copy.start()
        return copy


def greet(peers):
    barrier = pltpu.get_barrier_semaphore()
    for peer in peers:
        pl.semaphore_signal(barrier, inc=1, device_id=peer, device_id_type=MESH)
    pl.semaphore_wait(barrier, len(peers))


def axis_peers(at, core):
    return [device(moved(at, a, o), core) for a in range(3) for o in (1, 2, 3)]


def pick(axes, at, rows=None):
    index = tuple(at[a] if a in axes else slice(None) for a in range(3))
    return index if rows is None else (*index, rows)


def gram_kernel(
    n_total, x_ref, b_ref, label_ref, g_ref, s_ref, mean_ref, count_ref,
    c_ref, local_ref, count, crecv, mhalf, mrecv0, mrecv, daug, gt, half, recv0,
    r1a, r1b, r1c, t1a, t1b, t1c, r2a, r2b, r2c, t2a, t2b, t2c, r3a, r3b, r3c,
    gme, s_half, sr0, sr1, ss1, sr2, ss2, send, recv,
):
    at, core = place()
    x, y, z = at
    other = 1 - core
    copies = Copies(send, recv)
    partner = device(at, other)
    greet([partner, *axis_peers(at, core)])
    n_local, width = x_ref.shape

    @pl.loop(0, width // 256)
    def _(j):
        lanes = pl.ds(pl.multiple_of(j * 256, 256), 256)
        m = jnp.sum(x_ref[:, lanes].astype(F32), 0, keepdims=True) * (1.0 / n_local)
        local_ref[pl.ds(2 * j, 1), :] = m[:, :128]
        local_ref[pl.ds(2 * j + 1, 1), :] = m[:, 128:]

    mine = pl.ds(pl.multiple_of(core * 32, 32), 32)
    theirs = pl.ds(pl.multiple_of(other * 32, 32), 32)
    copy = copies.start(local_ref.at[theirs], mrecv0, partner)
    is_ref = (label_ref[...] == 0).astype(F32)
    count[...] = jnp.broadcast_to(jnp.sum(is_ref, 1, keepdims=True), (8, 128))
    copy_count = copies.start(count, crecv, partner)

    @pl.loop(0, width // 256)
    def _(j):
        lanes = pl.ds(pl.multiple_of(j * 256, 256), 256)
        rows = local_ref[pl.ds(2 * j, 2), :]
        m = jnp.concatenate([rows[0:1], rows[1:2]], 1)
        c_ref[:, lanes] = (x_ref[:, lanes].astype(F32) - m).astype(BF16)

    first = jnp.zeros((n_local, b_ref.shape[1]), F32)
    pieces = 4
    deep = width // pieces
    copy.wait()
    copy_count.wait()
    mhalf[0, 0:32] = local_ref[mine, :] + mrecv0[...]
    mhalf[0, 32:40] = count[...] + crecv[...]
    for a in range(3):
        waits = [copies.start(mhalf.at[a], mrecv.at[a, o - 1], device(moved(at, a, o), core)) for o in (1, 2, 3)]
        first += jnp.dot(
            c_ref[:, a * deep : (a + 1) * deep], b_ref[a * deep : (a + 1) * deep, :], preferred_element_type=F32
        )
        for w in waits:
            w.wait()
        mhalf[a + 1] = mhalf[a] + mrecv[a, 0] + mrecv[a, 1] + mrecv[a, 2]
    count_ref[...] = mhalf[3, 32:40]
    mhalf[4, 0:32] = mhalf[3, 0:32] * (1.0 / 128.0)
    mean_ref[mine, :] = mhalf[4, 0:32]
    copy = copies.start(mhalf.at[4, pl.ds(0, 32)], mean_ref.at[mine], partner)
    first += jnp.dot(c_ref[:, 3 * deep :], b_ref[3 * deep :, :], preferred_element_type=F32)
    first_t = first.T.astype(BF16)
    copy.wait()

    ids = lax.broadcasted_iota(jnp.int32, (16, 128), 0)

    @pl.loop(0, width // 128)
    def _(j):
        delta = local_ref[pl.ds(j, 1), :] - mean_ref[pl.ds(j, 1), :]
        high = delta.astype(BF16).astype(F32)
        low = delta - high
        tile = jnp.where(ids == 1, low, jnp.where((ids == 0) | (ids == 2), high, 0.0))
        daug[:, pl.ds(pl.multiple_of(j * 128, 128), 128)] = tile.astype(BF16)

    tau = jnp.dot(daug[...], b_ref[...], preferred_element_type=F32)
    tau = (tau[0:1] + tau[1:2]) * float(n_local)
    t_high = tau.astype(BF16).astype(F32)
    ids = lax.broadcasted_iota(jnp.int32, (16, 256), 0)
    taug = jnp.where(ids == 2, tau - t_high, jnp.where(ids < 2, t_high, 0.0))
    taug_t = taug.T.astype(BF16)

    @pl.loop(0, width // 256)
    def _(j):
        lanes = pl.ds(pl.multiple_of(j * 256, 256), 256)
        block = jnp.dot(first_t, c_ref[:, lanes], preferred_element_type=F32)
        block += jnp.dot(taug_t, daug[:, lanes], preferred_element_type=F32)
        block = block.astype(BF16)
        bx, by, bz = j // 8, (j // 2) % 4, (j % 2) * 2
        gt[bx, by, bz] = block[:, :128]
        gt[bx, by, bz + 1] = block[:, 128:]

    near = pl.ds(pl.multiple_of(core * 128, 128), 128)
    far = pl.ds(pl.multiple_of(other * 128, 128), 128)
    copies.start(gt.at[:, :, :, far, :], recv0, partner).wait()

    @pl.loop(0, 64)
    def _(j):
        bx, by, bz = j // 16, (j // 4) % 4, j % 4
        half[bx, by, bz] = (gt[bx, by, bz, near, :].astype(F32) + recv0[bx, by, bz].astype(F32)).astype(BF16)

    parts = list(zip(PARTS, (r1a, r1b, r1c), (t1a, t1b, t1c), (r2a, r2b, r2c), (t2a, t2b, t2c), (r3a, r3b, r3c)))
    waits = []
    for (start, size, order), r1, _, _, _, _ in parts:
        rows = slice(start, start + size)
        for o in (1, 2, 3):
            to = moved(at, order[0], o)
            waits.append(copies.start(half.at[pick(order[:1], to, rows)], r1.at[o - 1], device(to, core)))
    for w in waits:
        w.wait()
    waits = []
    for (start, size, order), r1, t1, r2, _, _ in parts:
        rows = slice(start, start + size)
        own = half.at[pick(order[:1], at, rows)]

        @pl.loop(0, 16)
        def _(j):
            u, v = j // 4, j % 4
            t1[u, v] = (own[u, v].astype(F32) + r1[0, u, v].astype(F32)) + (
                r1[1, u, v].astype(F32) + r1[2, u, v].astype(F32)
            )

        left = [a for a in range(3) if a != order[0]]
        for o in (1, 2, 3):
            to = moved(at, order[1], o)
            index = (to[order[1]],) if left[0] == order[1] else (slice(None), to[order[1]])
            waits.append(copies.start(t1.at[index], r2.at[o - 1], device(to, core)))
    for w in waits:
        w.wait()
    waits = []
    for (start, size, order), _, t1, r2, t2, r3 in parts:
        left = [a for a in range(3) if a != order[0]]
        first_left = left[0] == order[1]
        for k in range(4):
            own = t1[at[order[1]], k] if first_left else t1[k, at[order[1]]]
            t2[k] = (own + r2[0, k]) + (r2[1, k] + r2[2, k])
        for o in (1, 2, 3):
            to = moved(at, order[2], o)
            waits.append(copies.start(t2.at[to[order[2]]], r3.at[o - 1], device(to, core)))
    for w in waits:
        w.wait()
    for (start, size, order), _, _, _, t2, r3 in parts:
        total = (t2[at[order[2]]] + r3[0]) + (r3[1] + r3[2])
        gme[start : start + size, :] = total * (1.0 / n_total)
    g_ref[near, :] = gme[...]
    copies.start(gme, g_ref.at[near], partner).wait()

    square = lax.dot_general(
        gme[...], g_ref[...], (((1,), (1,)), ((), ())), precision=HIGHEST, preferred_element_type=F32
    )
    s_half[0] = square[:, :128]
    s_half[1] = square[:, 128:]
    waits = []
    for o in (1, 2, 3):
        to = moved(at, 0, o)
        rows = pl.ds(pl.multiple_of(to[0] * 32, 32), 32)
        waits.append(copies.start(s_half.at[:, rows, :], sr0.at[o - 1], device(to, core)))
    for w in waits:
        w.wait()
    ss1[...] = (s_half[:, pl.ds(pl.multiple_of(x * 32, 32), 32), :] + sr0[0]) + (sr0[1] + sr0[2])
    waits = []
    for o in (1, 2, 3):
        to = moved(at, 1, o)
        rows = pl.ds(pl.multiple_of(to[1] * 8, 8), 8)
        waits.append(copies.start(ss1.at[:, rows, :], sr1.at[o - 1], device(to, core)))
    for w in waits:
        w.wait()
    ss2[...] = (ss1[:, pl.ds(pl.multiple_of(y * 8, 8), 8), :] + sr1[0]) + (sr1[1] + sr1[2])
    waits = []
    for o in (1, 2, 3):
        waits.append(copies.start(ss2, sr2.at[z], device(moved(at, 2, o), core)))
    sr2[z] = ss2[...]
    for w in waits:
        w.wait()
    base = pl.multiple_of(core * 128 + x * 32 + y * 8, 8)
    s_ref[:, pl.ds(base, 8), :] = (sr2[0] + sr2[1]) + (sr2[2] + sr2[3])
    for axis, rows in (
        (1, pl.ds(base, 8)),
        (0, pl.ds(pl.multiple_of(core * 128 + x * 32, 32), 32)),
    ):
        view = s_ref.at[:, rows, :]
        waits = [copies.start(view, view, device(moved(at, axis, o), core)) for o in (1, 2, 3)]
        for w in waits:
            w.wait()
    view = s_ref.at[:, near, :]
    copies.start(view, view, partner).wait()


def gram_and_square(samples, basis_start, labels, n_total):
    scratch = [
        pltpu.VMEM((256, 8192), BF16),
        pltpu.VMEM((64, 128), F32),
        pltpu.VMEM((8, 128), F32),
        pltpu.VMEM((8, 128), F32),
        pltpu.VMEM((5, 40, 128), F32),
        pltpu.VMEM((32, 128), F32),
        pltpu.VMEM((3, 3, 40, 128), F32),
        pltpu.VMEM((16, 8192), BF16),
        pltpu.VMEM((4, 4, 4, 256, 128), BF16),
        pltpu.VMEM((4, 4, 4, 128, 128), BF16),
        pltpu.VMEM((4, 4, 4, 128, 128), BF16),
        *[pltpu.VMEM((3, 4, 4, size, 128), BF16) for _, size, _ in PARTS],
        *[pltpu.VMEM((4, 4, size, 128), F32) for _, size, _ in PARTS],
        *[pltpu.VMEM((3, 4, size, 128), F32) for _, size, _ in PARTS],
        *[pltpu.VMEM((4, size, 128), F32) for _, size, _ in PARTS],
        *[pltpu.VMEM((3, size, 128), F32) for _, size, _ in PARTS],
        pltpu.VMEM((128, 128), F32),
        pltpu.VMEM((2, 128, 128), F32),
        pltpu.VMEM((3, 2, 32, 128), F32),
        pltpu.VMEM((3, 2, 8, 128), F32),
        pltpu.VMEM((2, 32, 128), F32),
        pltpu.VMEM((4, 2, 8, 128), F32),
        pltpu.VMEM((2, 8, 128), F32),
        pltpu.SemaphoreType.DMA((57,)),
        pltpu.SemaphoreType.DMA((57,)),
    ]
    return pl.pallas_call(
        functools.partial(gram_kernel, n_total),
        out_shape=(
            jax.ShapeDtypeStruct((256, 128), F32),
            jax.ShapeDtypeStruct((2, 256, 128), F32),
            jax.ShapeDtypeStruct((64, 128), F32),
            jax.ShapeDtypeStruct((8, 128), F32),
        ),
        in_specs=[VMEM, VMEM, VMEM],
        out_specs=(VMEM, VMEM, VMEM, VMEM),
        scratch_shapes=scratch,
        compiler_params=pltpu.CompilerParams(collective_id=0, has_side_effects=True, vmem_limit_bytes=LIMIT),
        name="gram",
    )(samples, basis_start, labels.reshape(1, 256))


def small_inverse(t):
    sub = lax.broadcasted_iota(jnp.int32, (8, 128), 0)
    t = list(t)
    for s in range(4):
        rows = [jnp.broadcast_to(t[s][i : i + 1, :], (8, 128)) for i in range(8)]
        e = [[jnp.broadcast_to(rows[i][:, 8 * s + j : 8 * s + j + 1], (8, 128)) for j in range(i + 1)] for i in range(8)]
        inv, low = [], [[None] * 8 for _ in range(8)]
        for j in range(8):
            inv.append(1.0 / e[j][j])
            for i in range(j + 1, 8):
                low[i][j] = e[i][j] * inv[j]
            for i in range(j + 1, 8):
                for m in range(j + 1, i + 1):
                    e[i][m] = e[i][m] - low[i][j] * e[m][j]
        w = []
        for i in range(8):
            v = rows[i]
            for j in range(i):
                v = v - low[i][j] * w[j]
            w.append(v)
        for b in range(s + 1, 4):
            f = []
            for j in range(8):
                v = jnp.broadcast_to(t[b][:, 8 * s + j : 8 * s + j + 1], (8, 128))
                for k in range(j):
                    v = v - f[k] * e[j][k]
                f.append(v * inv[j])
            for j in range(8):
                t[b] = t[b] - f[j] * w[j]
        out = w[0] * lax.rsqrt(e[0][0])
        for i in range(1, 8):
            out = jnp.where(sub == i, w[i] * lax.rsqrt(e[i][i]), out)
        t[s] = out
    return t


def inverse_factor(s_ref, m_ref):
    r = lax.broadcasted_iota(jnp.int32, (256, 256), 0)
    c = lax.broadcasted_iota(jnp.int32, (256, 256), 1)
    m_ref[:, 0:128] = s_ref[0]
    m_ref[:, 128:256] = s_ref[1]
    m_ref[:, 256:512] = (r == c).astype(F32)
    lane = lax.broadcasted_iota(jnp.int32, (32, 128), 1)
    unit = (lane == lax.broadcasted_iota(jnp.int32, (32, 128), 0) + 32).astype(F32)
    wide = lax.broadcasted_iota(jnp.int32, (32, 256), 1)

    def panel(b, carry):
        rows = pl.ds(pl.multiple_of(b * 32, 32), 32)
        tile = m_ref[rows, pl.ds(pl.multiple_of((b // 4) * 128, 128), 128)]
        tile = pltpu.roll(tile, (4 - b % 4) % 4 * 32, 1)
        tile = jnp.where(lane < 32, tile, unit)
        t = small_inverse([tile[8 * i : 8 * i + 8] for i in range(4)])
        inv = jnp.concatenate(t, 0)[:, 32:64]
        w = jnp.dot(inv, m_ref[rows, :], precision=HIGHEST, preferred_element_type=F32)
        left = jnp.where(wide >= (b + 1) * 32, w[:, :256], 0.0)
        m_ref[...] -= lax.dot_general(left, w, (((0,), (0,)), ((), ())), precision=HIGHEST, preferred_element_type=F32)
        m_ref[rows, :] = w
        return carry

    lax.fori_loop(0, 8, panel, 0)


def basis_kernel(g_ref, s_ref, out_ref, m_ref, send, recv):
    at, core = place()
    copies = Copies(send, recv)
    partner = device(at, 1 - core)
    greet([partner, *axis_peers(at, core)])
    inverse_factor(s_ref, m_ref)
    block = lax.dot_general(
        g_ref[...], m_ref[:, 256:512], (((0,), (1,)), ((), ())), precision=HIGHEST, preferred_element_type=F32
    ).astype(BF16)
    out_ref[at[0], at[1], at[2], core] = jnp.where(core == 0, block[:64], block[64:])
    for step in range(3):
        waits = []
        for start, size, order in GATHER:
            fixed = order[step:]
            view = out_ref.at[(*pick(fixed, at), core, slice(start, start + size))]
            for o in (1, 2, 3):
                waits.append(copies.start(view, view, device(moved(at, order[step], o), core)))
        for w in waits:
            w.wait()
    waits = []
    for o in range(4):
        bx = (at[0] + o) % 4
        view = out_ref.at[bx, :, :, core]
        waits.append(copies.start(view, view, partner))
    for w in waits:
        w.wait()


def gather_basis(g, square):
    out = pl.pallas_call(
        basis_kernel,
        out_shape=jax.ShapeDtypeStruct((4, 4, 4, 2, 64, 256), BF16),
        in_specs=[VMEM, VMEM],
        out_specs=VMEM,
        scratch_shapes=[pltpu.VMEM((256, 512), F32), pltpu.SemaphoreType.DMA((31,)), pltpu.SemaphoreType.DMA((31,))],
        compiler_params=pltpu.CompilerParams(collective_id=1, has_side_effects=True, vmem_limit_bytes=LIMIT),
        name="basis",
    )(g, square)
    return out.reshape(8192, 256)


STEPS = ((0, 0, 0), (3, 0, 0), (0, 0, 3), (0, 1, 0), (2, 0, 0), (0, 3, 3), (3, 0, 1), (1, 1, 0), (0, 2, 3), (0, 0, 2), (2, 0, 1), (0, 2, 0))
PARENTS = ((0, 0, 0), (0, 0, 0), (0, 0, 0), (3, 0, 0), (0, 0, 3), (3, 0, 0), (0, 1, 0), (0, 3, 3), (0, 0, 3), (2, 0, 0), (0, 1, 0))


def difference(a, b):
    return tuple((i - j) % 4 for i, j in zip(a, b))


def panel_plan():
    parent = [None, *[STEPS.index(p) for p in PARENTS]]
    depth = [0] * len(STEPS)
    for s in range(1, len(STEPS)):
        depth[s] = depth[parent[s]] + 1
    best = {}
    for r, row in enumerate(STEPS):
        for c, column in enumerate(STEPS):
            d = difference(row, column)
            cost = (max(depth[r], depth[c]), depth[r] + depth[c], r)
            if d not in best or cost < best[d][0]:
                best[d] = (cost, r, c)
    units = sorted((cost[0], r, c) for cost, r, c in best.values())
    assert len(units) == 64
    return parent, depth, units


def proof_kernel(
    n_total, width_ref, n_ref_ref, p_ref, label_ref, out_ref,
    blocks, columns, rows_ref, acc, got, send, recv,
):
    at, core = place()
    other = 1 - core
    copies = Copies(send, recv)
    partner = device(at, other)
    parent, depth, units = panel_plan()
    neighbours = [device(moved(at, a, o), core) for a in range(3) for o in (1, 3)]
    greet([partner, *neighbours])

    def toward(step):
        return device(tuple((c + i) % 4 for c, i in zip(at, step)), core)

    p = p_ref[...]
    wide = p.astype(F32)
    norm = jnp.broadcast_to(jnp.sum(wide * wide, 1, keepdims=True) * -0.5, (256, 128)).T
    norm = jnp.concatenate([norm[:128, :128], norm[:128, 128:]], 1)[0:1]
    high = norm.astype(BF16).astype(F32)
    middle = (norm - high).astype(BF16).astype(F32)
    low = (norm - high) - middle
    is_ref = (label_ref[...] == 0).astype(F32)
    ids = lax.broadcasted_iota(jnp.int32, (16, 256), 0)
    tail = jnp.where(ids == 0, is_ref, jnp.where(ids == 1, high, jnp.where(ids == 2, middle, jnp.where(ids == 3, low, 0.0))))
    blocks[0, core, 0:256, :] = p
    blocks[0, core, 256:272, :] = tail.astype(BF16)

    edges, cores = {}, {}

    def hand_on(s):
        view = blocks.at[s, core]
        for child in range(1, len(STEPS)):
            if parent[child] == s:
                target = toward(difference(STEPS[s], STEPS[child]))
                edges[child] = copies.start(view, blocks.at[child, core], target)
        cores[s] = copies.start(view, view, partner)

    scale = 1.4426950408889634 / (128.0 * jnp.exp2(jnp.full((1, 256), width_ref[0], jnp.int32).astype(F32)))
    ids = lax.broadcasted_iota(jnp.int32, (16, 256), 0)
    lanes = lax.broadcasted_iota(jnp.int32, (16, 256), 1)
    select = jnp.where(lanes < 128, jnp.where((ids > 0) & (ids < 4), 1.0, 0.0), jnp.where(ids == 0, 1.0, 0.0)).astype(BF16)

    def prepare(s):
        for k in range(2):
            ends = blocks[s, k, 256:272, :].astype(F32).T.astype(BF16)
            columns[s, k] = jnp.dot(ends, select, preferred_element_type=F32)
        ends = blocks[s, core, 256:272, :].astype(F32)
        rows_ref[s] = jnp.broadcast_to((ends[1:2] + ends[2:3]) + ends[3:4], (8, 256))

    for s in range(len(STEPS)):
        acc[s, 0] = jnp.zeros((8, 256), F32)
        acc[s, 1] = jnp.zeros((8, 256), F32)
    hand_on(0)
    for level in range(max(depth) + 1):
        here = [s for s in range(len(STEPS)) if depth[s] == level]
        for s in here:
            if s:
                edges[s].wait()
                hand_on(s)
        for s in here:
            cores[s].wait()
            prepare(s)
        for _, r, c in [u for u in units if u[0] == level]:
            row_norm = rows_ref[r][0:1]
            rows = blocks[r, core, 0:256, :]
            total, refs = acc[r, 0], acc[r, 1]
            for k in range(2):
                inner = lax.dot_general(
                    blocks[c, k, 0:256, :], rows, (((1,), (1,)), ((), ())), preferred_element_type=F32
                )
                norm, mark = columns[c, k, :, :128], columns[c, k, :, 128:]
                norm, mark = jnp.concatenate([norm, norm], 1), jnp.concatenate([mark, mark], 1)
                value = jnp.exp2(((inner + norm) + row_norm) * scale)
                total += jnp.sum(value.reshape(32, 8, 256), 0)
                refs += jnp.sum((value * mark).reshape(32, 8, 256), 0)
            acc[r, 0], acc[r, 1] = total, refs

    for level in range(max(depth), 0, -1):
        here = [s for s in range(1, len(STEPS)) if depth[s] == level]
        waits = [copies.start(acc.at[s], got.at[s], toward(difference(STEPS[s], STEPS[parent[s]]))) for s in here]
        for s, w in zip(here, waits):
            w.wait()
            acc[parent[s]] += got[s]
    row_sums = jnp.sum(acc[0, 0], 0, keepdims=True)
    ref_sums = jnp.sum(acc[0, 1], 0, keepdims=True)
    n_ref = n_ref_ref[0:1, 0:1]
    n_cur = n_total - n_ref
    proof = (ref_sums / n_ref - (row_sums - ref_sums) / n_cur) / (row_sums / n_total)
    out_ref[...] = jnp.broadcast_to(proof, (8, 256))


def proof_values(projected, labels, width_index, n_ref, n_total):
    count = len(STEPS)
    out = pl.pallas_call(
        functools.partial(proof_kernel, n_total),
        out_shape=jax.ShapeDtypeStruct((8, 256), F32),
        in_specs=[pl.BlockSpec(memory_space=pltpu.SMEM), VMEM, VMEM, VMEM],
        out_specs=VMEM,
        scratch_shapes=[
            pltpu.VMEM((count, 2, 272, 256), BF16),
            pltpu.VMEM((count, 2, 256, 256), F32),
            pltpu.VMEM((count, 8, 256), F32),
            pltpu.VMEM((count, 2, 8, 256), F32),
            pltpu.VMEM((count, 2, 8, 256), F32),
            pltpu.SemaphoreType.DMA((3 * count - 2,)),
            pltpu.SemaphoreType.DMA((3 * count - 2,)),
        ],
        compiler_params=pltpu.CompilerParams(collective_id=2, has_side_effects=True, vmem_limit_bytes=LIMIT),
        name="proof",
    )(width_index.reshape(1), n_ref, projected, labels.reshape(1, 256))
    return out[0]


def local(n_total, samples, labels, basis_start, width_index):
    g, square, mean, n_ref = gram_and_square(samples, basis_start, labels, n_total)
    basis = gather_basis(g, square)
    centred = (samples - mean.reshape(1, 8192)).astype(BF16)
    projected = jnp.dot(centred, basis, preferred_element_type=F32).astype(BF16)
    proof = proof_values(projected, labels, width_index, n_ref, n_total)
    return projected, proof, basis


def solution(mesh):
    n_total = float(256 * mesh.size)
    placed = (P(("row", "col"), None), P(("row", "col")), P(), P())
    return jax.shard_map(
        functools.partial(local, n_total),
        mesh=mesh,
        in_specs=placed,
        out_specs=(P(("row", "col"), None), P(("row", "col")), P()),
        check_vma=False,
    )
```

```python
import functools
import itertools

import jax
import jax.numpy as jnp
from jax import lax
from jax.experimental import pallas as pl
from jax.experimental.pallas import tpu as pltpu
from jax.sharding import PartitionSpec as P

MESH = pl.DeviceIdType.MESH
F32 = jnp.float32
BF16 = jnp.bfloat16
VMEM = pl.BlockSpec(memory_space=pltpu.VMEM)
HIGHEST = lax.Precision.HIGHEST
LIMIT = 60 * 1024 * 1024

PARTS = ((0, 48, (0, 1, 2)), (48, 48, (1, 2, 0)), (96, 32, (2, 0, 1)))


def place():
    row, col = lax.axis_index("row"), lax.axis_index("col")
    y, z_lo, core = row // 4, (row // 2) % 2, row % 2
    z_hi, x = col // 4, col % 4
    return (x, y, z_hi * 2 + z_lo), core


def device(at, core):
    x, y, z = at
    return (y * 4 + (z % 2) * 2 + core, (z // 2) * 4 + x)


def moved(at, axis, offset):
    return tuple((c + offset) % 4 if a == axis else c for a, c in enumerate(at))


class Copies:
    def __init__(self, send, recv):
        self.send, self.recv, self.used = send, recv, 0

    def start(self, src, dst, target):
        n = self.used
        self.used += 1
        copy = pltpu.make_async_remote_copy(
            src_ref=src,
            dst_ref=dst,
            send_sem=self.send.at[n],
            recv_sem=self.recv.at[n],
            device_id=target,
            device_id_type=MESH,
        )
        copy.start()
        return copy


def greet(peers):
    barrier = pltpu.get_barrier_semaphore()
    for peer in peers:
        pl.semaphore_signal(barrier, inc=1, device_id=peer, device_id_type=MESH)
    pl.semaphore_wait(barrier, len(peers))


def axis_peers(at, core):
    return [device(moved(at, a, o), core) for a in range(3) for o in (1, 2, 3)]


def pick(axes, at, rows=None):
    index = tuple(at[a] if a in axes else slice(None) for a in range(3))
    return index if rows is None else (*index, rows)


def gram_kernel(
    n_total, x_ref, b_ref, label_ref, g_ref, s_ref, mean_ref, count_ref,
    c_ref, local_ref, count, crecv, mhalf, mrecv0, mrecv, daug, gt, half, recv0,
    r1a, r1b, r1c, t1a, t1b, t1c, r2a, r2b, r2c, t2a, t2b, t2c, r3a, r3b, r3c,
    gme, s_half, sr0, sr1, ss1, sr2, ss2, send, recv,
):
    at, core = place()
    x, y, z = at
    other = 1 - core
    copies = Copies(send, recv)
    partner = device(at, other)
    greet([partner, *axis_peers(at, core)])
    n_local, width = x_ref.shape

    @pl.loop(0, width // 256)
    def _(j):
        lanes = pl.ds(pl.multiple_of(j * 256, 256), 256)
        m = jnp.sum(x_ref[:, lanes].astype(F32), 0, keepdims=True) * (1.0 / n_local)
        local_ref[pl.ds(2 * j, 1), :] = m[:, :128]
        local_ref[pl.ds(2 * j + 1, 1), :] = m[:, 128:]

    mine = pl.ds(pl.multiple_of(core * 32, 32), 32)
    theirs = pl.ds(pl.multiple_of(other * 32, 32), 32)
    copy = copies.start(local_ref.at[theirs], mrecv0, partner)
    is_ref = (label_ref[...] == 0).astype(F32)
    count[...] = jnp.broadcast_to(jnp.sum(is_ref, 1, keepdims=True), (8, 128))
    copy_count = copies.start(count, crecv, partner)

    @pl.loop(0, width // 256)
    def _(j):
        lanes = pl.ds(pl.multiple_of(j * 256, 256), 256)
        rows = local_ref[pl.ds(2 * j, 2), :]
        m = jnp.concatenate([rows[0:1], rows[1:2]], 1)
        c_ref[:, lanes] = (x_ref[:, lanes].astype(F32) - m).astype(BF16)

    first = jnp.zeros((n_local, b_ref.shape[1]), F32)
    pieces = 4
    deep = width // pieces
    copy.wait()
    copy_count.wait()
    mhalf[0, 0:32] = local_ref[mine, :] + mrecv0[...]
    mhalf[0, 32:40] = count[...] + crecv[...]
    for a in range(3):
        waits = [copies.start(mhalf.at[a], mrecv.at[a, o - 1], device(moved(at, a, o), core)) for o in (1, 2, 3)]
        first += jnp.dot(
            c_ref[:, a * deep : (a + 1) * deep], b_ref[a * deep : (a + 1) * deep, :], preferred_element_type=F32
        )
        for w in waits:
            w.wait()
        mhalf[a + 1] = mhalf[a] + mrecv[a, 0] + mrecv[a, 1] + mrecv[a, 2]
    count_ref[...] = mhalf[3, 32:40]
    mhalf[4, 0:32] = mhalf[3, 0:32] * (1.0 / 128.0)
    mean_ref[mine, :] = mhalf[4, 0:32]
    copy = copies.start(mhalf.at[4, pl.ds(0, 32)], mean_ref.at[mine], partner)
    first += jnp.dot(c_ref[:, 3 * deep :], b_ref[3 * deep :, :], preferred_element_type=F32)
    first_t = first.T.astype(BF16)
    copy.wait()

    ids = lax.broadcasted_iota(jnp.int32, (16, 128), 0)

    @pl.loop(0, width // 128)
    def _(j):
        delta = local_ref[pl.ds(j, 1), :] - mean_ref[pl.ds(j, 1), :]
        high = delta.astype(BF16).astype(F32)
        low = delta - high
        tile = jnp.where(ids == 1, low, jnp.where((ids == 0) | (ids == 2), high, 0.0))
        daug[:, pl.ds(pl.multiple_of(j * 128, 128), 128)] = tile.astype(BF16)

    tau = jnp.dot(daug[...], b_ref[...], preferred_element_type=F32)
    tau = (tau[0:1] + tau[1:2]) * float(n_local)
    t_high = tau.astype(BF16).astype(F32)
    ids = lax.broadcasted_iota(jnp.int32, (16, 256), 0)
    taug = jnp.where(ids == 2, tau - t_high, jnp.where(ids < 2, t_high, 0.0))
    taug_t = taug.T.astype(BF16)

    @pl.loop(0, width // 256)
    def _(j):
        lanes = pl.ds(pl.multiple_of(j * 256, 256), 256)
        block = jnp.dot(first_t, c_ref[:, lanes], preferred_element_type=F32)
        block += jnp.dot(taug_t, daug[:, lanes], preferred_element_type=F32)
        block = block.astype(BF16)
        bx, by, bz = j // 8, (j // 2) % 4, (j % 2) * 2
        gt[bx, by, bz] = block[:, :128]
        gt[bx, by, bz + 1] = block[:, 128:]

    near = pl.ds(pl.multiple_of(core * 128, 128), 128)
    far = pl.ds(pl.multiple_of(other * 128, 128), 128)
    copies.start(gt.at[:, :, :, far, :], recv0, partner).wait()

    @pl.loop(0, 64)
    def _(j):
        bx, by, bz = j // 16, (j // 4) % 4, j % 4
        half[bx, by, bz] = (gt[bx, by, bz, near, :].astype(F32) + recv0[bx, by, bz].astype(F32)).astype(BF16)

    parts = list(zip(PARTS, (r1a, r1b, r1c), (t1a, t1b, t1c), (r2a, r2b, r2c), (t2a, t2b, t2c), (r3a, r3b, r3c)))
    waits = []
    for (start, size, order), r1, _, _, _, _ in parts:
        rows = slice(start, start + size)
        for o in (1, 2, 3):
            to = moved(at, order[0], o)
            waits.append(copies.start(half.at[pick(order[:1], to, rows)], r1.at[o - 1], device(to, core)))
    for w in waits:
        w.wait()
    waits = []
    for (start, size, order), r1, t1, r2, _, _ in parts:
        rows = slice(start, start + size)
        own = half.at[pick(order[:1], at, rows)]

        @pl.loop(0, 16)
        def _(j):
            u, v = j // 4, j % 4
            t1[u, v] = (own[u, v].astype(F32) + r1[0, u, v].astype(F32)) + (
                r1[1, u, v].astype(F32) + r1[2, u, v].astype(F32)
            )

        left = [a for a in range(3) if a != order[0]]
        for o in (1, 2, 3):
            to = moved(at, order[1], o)
            index = (to[order[1]],) if left[0] == order[1] else (slice(None), to[order[1]])
            waits.append(copies.start(t1.at[index], r2.at[o - 1], device(to, core)))
    for w in waits:
        w.wait()
    waits = []
    for (start, size, order), _, t1, r2, t2, r3 in parts:
        left = [a for a in range(3) if a != order[0]]
        first_left = left[0] == order[1]
        for k in range(4):
            own = t1[at[order[1]], k] if first_left else t1[k, at[order[1]]]
            t2[k] = (own + r2[0, k]) + (r2[1, k] + r2[2, k])
        for o in (1, 2, 3):
            to = moved(at, order[2], o)
            waits.append(copies.start(t2.at[to[order[2]]], r3.at[o - 1], device(to, core)))
    for w in waits:
        w.wait()
    for (start, size, order), _, _, _, t2, r3 in parts:
        total = (t2[at[order[2]]] + r3[0]) + (r3[1] + r3[2])
        gme[start : start + size, :] = total * (1.0 / n_total)
    g_ref[near, :] = gme[...]
    copies.start(gme, g_ref.at[near], partner).wait()

    square = lax.dot_general(
        gme[...], g_ref[...], (((1,), (1,)), ((), ())), precision=HIGHEST, preferred_element_type=F32
    )
    s_half[0] = square[:, :128]
    s_half[1] = square[:, 128:]
    waits = []
    for o in (1, 2, 3):
        to = moved(at, 0, o)
        rows = pl.ds(pl.multiple_of(to[0] * 32, 32), 32)
        waits.append(copies.start(s_half.at[:, rows, :], sr0.at[o - 1], device(to, core)))
    for w in waits:
        w.wait()
    ss1[...] = (s_half[:, pl.ds(pl.multiple_of(x * 32, 32), 32), :] + sr0[0]) + (sr0[1] + sr0[2])
    waits = []
    for o in (1, 2, 3):
        to = moved(at, 1, o)
        rows = pl.ds(pl.multiple_of(to[1] * 8, 8), 8)
        waits.append(copies.start(ss1.at[:, rows, :], sr1.at[o - 1], device(to, core)))
    for w in waits:
        w.wait()
    ss2[...] = (ss1[:, pl.ds(pl.multiple_of(y * 8, 8), 8), :] + sr1[0]) + (sr1[1] + sr1[2])
    waits = []
    for o in (1, 2, 3):
        waits.append(copies.start(ss2, sr2.at[z], device(moved(at, 2, o), core)))
    sr2[z] = ss2[...]
    for w in waits:
        w.wait()
    base = pl.multiple_of(core * 128 + x * 32 + y * 8, 8)
    s_ref[:, pl.ds(base, 8), :] = (sr2[0] + sr2[1]) + (sr2[2] + sr2[3])
    for axis, rows in (
        (1, pl.ds(base, 8)),
        (0, pl.ds(pl.multiple_of(core * 128 + x * 32, 32), 32)),
    ):
        view = s_ref.at[:, rows, :]
        waits = [copies.start(view, view, device(moved(at, axis, o), core)) for o in (1, 2, 3)]
        for w in waits:
            w.wait()
    view = s_ref.at[:, near, :]
    copies.start(view, view, partner).wait()


def gram_and_square(samples, basis_start, labels, n_total):
    scratch = [
        pltpu.VMEM((256, 8192), BF16),
        pltpu.VMEM((64, 128), F32),
        pltpu.VMEM((8, 128), F32),
        pltpu.VMEM((8, 128), F32),
        pltpu.VMEM((5, 40, 128), F32),
        pltpu.VMEM((32, 128), F32),
        pltpu.VMEM((3, 3, 40, 128), F32),
        pltpu.VMEM((16, 8192), BF16),
        pltpu.VMEM((4, 4, 4, 256, 128), BF16),
        pltpu.VMEM((4, 4, 4, 128, 128), BF16),
        pltpu.VMEM((4, 4, 4, 128, 128), BF16),
        *[pltpu.VMEM((3, 4, 4, size, 128), BF16) for _, size, _ in PARTS],
        *[pltpu.VMEM((4, 4, size, 128), F32) for _, size, _ in PARTS],
        *[pltpu.VMEM((3, 4, size, 128), F32) for _, size, _ in PARTS],
        *[pltpu.VMEM((4, size, 128), F32) for _, size, _ in PARTS],
        *[pltpu.VMEM((3, size, 128), F32) for _, size, _ in PARTS],
        pltpu.VMEM((128, 128), F32),
        pltpu.VMEM((2, 128, 128), F32),
        pltpu.VMEM((3, 2, 32, 128), F32),
        pltpu.VMEM((3, 2, 8, 128), F32),
        pltpu.VMEM((2, 32, 128), F32),
        pltpu.VMEM((4, 2, 8, 128), F32),
        pltpu.VMEM((2, 8, 128), F32),
        pltpu.SemaphoreType.DMA((57,)),
        pltpu.SemaphoreType.DMA((57,)),
    ]
    return pl.pallas_call(
        functools.partial(gram_kernel, n_total),
        out_shape=(
            jax.ShapeDtypeStruct((256, 128), F32),
            jax.ShapeDtypeStruct((2, 256, 128), F32),
            jax.ShapeDtypeStruct((64, 128), F32),
            jax.ShapeDtypeStruct((8, 128), F32),
        ),
        in_specs=[VMEM, VMEM, VMEM],
        out_specs=(VMEM, VMEM, VMEM, VMEM),
        scratch_shapes=scratch,
        compiler_params=pltpu.CompilerParams(collective_id=0, has_side_effects=True, vmem_limit_bytes=LIMIT),
        name="gram",
    )(samples, basis_start, labels.reshape(1, 256))


def small_inverse(t):
    sub = lax.broadcasted_iota(jnp.int32, (8, 128), 0)
    t = list(t)
    for s in range(4):
        rows = [jnp.broadcast_to(t[s][i : i + 1, :], (8, 128)) for i in range(8)]
        e = [[jnp.broadcast_to(rows[i][:, 8 * s + j : 8 * s + j + 1], (8, 128)) for j in range(i + 1)] for i in range(8)]
        inv, low = [], [[None] * 8 for _ in range(8)]
        for j in range(8):
            inv.append(1.0 / e[j][j])
            for i in range(j + 1, 8):
                low[i][j] = e[i][j] * inv[j]
            for i in range(j + 1, 8):
                for m in range(j + 1, i + 1):
                    e[i][m] = e[i][m] - low[i][j] * e[m][j]
        w = []
        for i in range(8):
            v = rows[i]
            for j in range(i):
                v = v - low[i][j] * w[j]
            w.append(v)
        for b in range(s + 1, 4):
            f = []
            for j in range(8):
                v = jnp.broadcast_to(t[b][:, 8 * s + j : 8 * s + j + 1], (8, 128))
                for k in range(j):
                    v = v - f[k] * e[j][k]
                f.append(v * inv[j])
            for j in range(8):
                t[b] = t[b] - f[j] * w[j]
        out = w[0] * lax.rsqrt(e[0][0])
        for i in range(1, 8):
            out = jnp.where(sub == i, w[i] * lax.rsqrt(e[i][i]), out)
        t[s] = out
    return t


def inverse_factor(s_ref, m_ref):
    r = lax.broadcasted_iota(jnp.int32, (256, 256), 0)
    c = lax.broadcasted_iota(jnp.int32, (256, 256), 1)
    m_ref[:, 0:128] = s_ref[0]
    m_ref[:, 128:256] = s_ref[1]
    m_ref[:, 256:512] = (r == c).astype(F32)
    lane = lax.broadcasted_iota(jnp.int32, (32, 128), 1)
    unit = (lane == lax.broadcasted_iota(jnp.int32, (32, 128), 0) + 32).astype(F32)
    wide = lax.broadcasted_iota(jnp.int32, (32, 256), 1)

    def panel(b, carry):
        rows = pl.ds(pl.multiple_of(b * 32, 32), 32)
        tile = m_ref[rows, pl.ds(pl.multiple_of((b // 4) * 128, 128), 128)]
        tile = pltpu.roll(tile, (4 - b % 4) % 4 * 32, 1)
        tile = jnp.where(lane < 32, tile, unit)
        t = small_inverse([tile[8 * i : 8 * i + 8] for i in range(4)])
        inv = jnp.concatenate(t, 0)[:, 32:64]
        w = jnp.dot(inv, m_ref[rows, :], precision=HIGHEST, preferred_element_type=F32)
        left = jnp.where(wide >= (b + 1) * 32, w[:, :256], 0.0)
        m_ref[...] -= lax.dot_general(left, w, (((0,), (0,)), ((), ())), precision=HIGHEST, preferred_element_type=F32)
        m_ref[rows, :] = w
        return carry

    lax.fori_loop(0, 8, panel, 0)


STEPS = ((0, 0, 0), (3, 0, 0), (0, 0, 3), (0, 1, 0), (2, 0, 0), (0, 3, 3), (3, 0, 1), (1, 1, 0), (0, 2, 3), (0, 0, 2), (2, 0, 1), (0, 2, 0))
PARENTS = ((0, 0, 0), (0, 0, 0), (0, 0, 0), (3, 0, 0), (0, 0, 3), (3, 0, 0), (0, 1, 0), (0, 3, 3), (0, 0, 3), (2, 0, 0), (0, 1, 0))


def difference(a, b):
    return tuple((i - j) % 4 for i, j in zip(a, b))


def panel_plan():
    parent = [None, *[STEPS.index(p) for p in PARENTS]]
    depth = [0] * len(STEPS)
    for s in range(1, len(STEPS)):
        depth[s] = depth[parent[s]] + 1
    best = {}
    for r, row in enumerate(STEPS):
        for c, column in enumerate(STEPS):
            d = difference(row, column)
            cost = (max(depth[r], depth[c]), depth[r] + depth[c], r)
            if d not in best or cost < best[d][0]:
                best[d] = (cost, r, c)
    units = sorted((cost[0], r, c) for cost, r, c in best.values())
    assert len(units) == 64
    return parent, depth, units


def spanning_tree():
    def far(step):
        return sum(min(c, 4 - c) for c in step)

    steps = sorted(itertools.product(range(4), repeat=3), key=lambda step: (far(step), step))
    load = {(a, o): 0 for a in range(3) for o in (1, 3)}
    parent = [None]
    for step in steps[1:]:
        choices = []
        for (a, o), used in load.items():
            before = moved(step, a, 4 - o)
            if far(before) == far(step) - 1:
                choices.append((used, a, o, steps.index(before)))
        _, a, o, before = min(choices)
        load[a, o] += 1
        parent.append(before)
    return steps, parent, [far(step) for step in steps]


def project_kernel(
    n_total, width_ref, g_ref, s_ref, x_ref, mean_ref, n_ref_ref, label_ref, basis_ref, proj_ref, out_ref,
    m_ref, p_acc, blocks, columns, rows_ref, acc, got, send, recv,
):
    at, core = place()
    other = 1 - core
    copies = Copies(send, recv)
    partner = device(at, other)
    parent, depth, units = panel_plan()
    neighbours = [device(moved(at, a, o), core) for a in range(3) for o in (1, 3)]
    greet([partner, *neighbours])

    def moved_by(step):
        return tuple((c + i) % 4 for c, i in zip(at, step))

    def toward(step):
        return device(moved_by(step), core)

    inverse_factor(s_ref, m_ref)
    block = lax.dot_general(
        g_ref[...], m_ref[:, 256:512], (((0,), (1,)), ((), ())), precision=HIGHEST, preferred_element_type=F32
    ).astype(BF16)
    basis_ref[(at[0] * 4 + at[1]) * 4 + at[2]] = block

    steps, source, level_of = spanning_tree()
    half = pl.ds(pl.multiple_of(core * 64, 64), 64)

    def chip(s):
        x, y, z = moved_by(steps[s])
        return (x * 4 + y) * 4 + z

    links, across = {}, {}
    p_acc[...] = jnp.zeros_like(p_acc)

    def add_level(level):
        total = p_acc[...]
        for s in range(64):
            if level_of[s] == level:
                if s:
                    across[s].wait()
                b = chip(s)
                lanes = pl.ds(pl.multiple_of(b * 128, 128), 128)
                centred = (x_ref[:, lanes].astype(F32) - mean_ref[pl.ds(b, 1), :]).astype(BF16)
                total += jnp.dot(centred, basis_ref[b], preferred_element_type=F32)
        p_acc[...] = total

    for level in range(7):
        for s in range(64):
            if level_of[s] != level:
                continue
            if s:
                links[s].wait()
            view = basis_ref.at[chip(s), half, :]
            for child in range(1, 64):
                if source[child] == s:
                    links[child] = copies.start(view, view, toward(difference(steps[s], steps[child])))
            if s:
                across[s] = copies.start(view, view, partner)
        if level:
            add_level(level - 1)
    add_level(6)
    p = p_acc[...].astype(BF16)
    proj_ref[...] = p
    wide = p.astype(F32)
    norm = jnp.broadcast_to(jnp.sum(wide * wide, 1, keepdims=True) * -0.5, (256, 128)).T
    norm = jnp.concatenate([norm[:128, :128], norm[:128, 128:]], 1)[0:1]
    high = norm.astype(BF16).astype(F32)
    middle = (norm - high).astype(BF16).astype(F32)
    low = (norm - high) - middle
    is_ref = (label_ref[...] == 0).astype(F32)
    ids = lax.broadcasted_iota(jnp.int32, (16, 256), 0)
    tail = jnp.where(ids == 0, is_ref, jnp.where(ids == 1, high, jnp.where(ids == 2, middle, jnp.where(ids == 3, low, 0.0))))
    blocks[0, core, 0:256, :] = p
    blocks[0, core, 256:272, :] = tail.astype(BF16)

    edges, cores = {}, {}

    def hand_on(s):
        view = blocks.at[s, core]
        for child in range(1, len(STEPS)):
            if parent[child] == s:
                target = toward(difference(STEPS[s], STEPS[child]))
                edges[child] = copies.start(view, blocks.at[child, core], target)
        cores[s] = copies.start(view, view, partner)

    scale = 1.4426950408889634 / (128.0 * jnp.exp2(jnp.full((1, 256), width_ref[0], jnp.int32).astype(F32)))
    ids = lax.broadcasted_iota(jnp.int32, (16, 256), 0)
    lanes = lax.broadcasted_iota(jnp.int32, (16, 256), 1)
    select = jnp.where(lanes < 128, jnp.where((ids > 0) & (ids < 4), 1.0, 0.0), jnp.where(ids == 0, 1.0, 0.0)).astype(BF16)

    def prepare(s):
        for k in range(2):
            ends = blocks[s, k, 256:272, :].astype(F32).T.astype(BF16)
            columns[s, k] = jnp.dot(ends, select, preferred_element_type=F32)
        ends = blocks[s, core, 256:272, :].astype(F32)
        rows_ref[s] = jnp.broadcast_to((ends[1:2] + ends[2:3]) + ends[3:4], (8, 256))

    for s in range(len(STEPS)):
        acc[s, 0] = jnp.zeros((8, 256), F32)
        acc[s, 1] = jnp.zeros((8, 256), F32)
    hand_on(0)
    for level in range(max(depth) + 1):
        here = [s for s in range(len(STEPS)) if depth[s] == level]
        for s in here:
            if s:
                edges[s].wait()
                hand_on(s)
        for s in here:
            cores[s].wait()
            prepare(s)
        for _, r, c in [u for u in units if u[0] == level]:
            row_norm = rows_ref[r][0:1]
            rows = blocks[r, core, 0:256, :]
            total, refs = acc[r, 0], acc[r, 1]
            for k in range(2):
                inner = lax.dot_general(
                    blocks[c, k, 0:256, :], rows, (((1,), (1,)), ((), ())), preferred_element_type=F32
                )
                norm, mark = columns[c, k, :, :128], columns[c, k, :, 128:]
                norm, mark = jnp.concatenate([norm, norm], 1), jnp.concatenate([mark, mark], 1)
                value = jnp.exp2(((inner + norm) + row_norm) * scale)
                total += jnp.sum(value.reshape(32, 8, 256), 0)
                refs += jnp.sum((value * mark).reshape(32, 8, 256), 0)
            acc[r, 0], acc[r, 1] = total, refs

    for level in range(max(depth), 0, -1):
        here = [s for s in range(1, len(STEPS)) if depth[s] == level]
        waits = [copies.start(acc.at[s], got.at[s], toward(difference(STEPS[s], STEPS[parent[s]]))) for s in here]
        for s, w in zip(here, waits):
            w.wait()
            acc[parent[s]] += got[s]
    row_sums = jnp.sum(acc[0, 0], 0, keepdims=True)
    ref_sums = jnp.sum(acc[0, 1], 0, keepdims=True)
    n_ref = n_ref_ref[0:1, 0:1]
    n_cur = n_total - n_ref
    proof = (ref_sums / n_ref - (row_sums - ref_sums) / n_cur) / (row_sums / n_total)
    out_ref[...] = jnp.broadcast_to(proof, (8, 256))


def project_and_prove(g, square, samples, mean, n_ref, labels, width_index, n_total):
    count = len(STEPS)
    copies = 126 + 3 * count - 2
    basis, projected, proof = pl.pallas_call(
        functools.partial(project_kernel, n_total),
        out_shape=(
            jax.ShapeDtypeStruct((64, 128, 256), BF16),
            jax.ShapeDtypeStruct((256, 256), BF16),
            jax.ShapeDtypeStruct((8, 256), F32),
        ),
        in_specs=[pl.BlockSpec(memory_space=pltpu.SMEM), *[VMEM] * 6],
        out_specs=(VMEM, VMEM, VMEM),
        scratch_shapes=[
            pltpu.VMEM((256, 512), F32),
            pltpu.VMEM((256, 256), F32),
            pltpu.VMEM((count, 2, 272, 256), BF16),
            pltpu.VMEM((count, 2, 256, 256), F32),
            pltpu.VMEM((count, 8, 256), F32),
            pltpu.VMEM((count, 2, 8, 256), F32),
            pltpu.VMEM((count, 2, 8, 256), F32),
            pltpu.SemaphoreType.DMA((copies,)),
            pltpu.SemaphoreType.DMA((copies,)),
        ],
        compiler_params=pltpu.CompilerParams(collective_id=1, has_side_effects=True, vmem_limit_bytes=LIMIT),
        name="project",
    )(width_index.reshape(1), g, square, samples, mean, n_ref, labels.reshape(1, 256))
    return basis.reshape(8192, 256), projected, proof[0]


def local(n_total, samples, labels, basis_start, width_index):
    g, square, mean, n_ref = gram_and_square(samples, basis_start, labels, n_total)
    basis, projected, proof = project_and_prove(g, square, samples, mean, n_ref, labels, width_index, n_total)
    return projected, proof, basis


def solution(mesh):
    n_total = float(256 * mesh.size)
    placed = (P(("row", "col"), None), P(("row", "col")), P(), P())
    return jax.shard_map(
        functools.partial(local, n_total),
        mesh=mesh,
        in_specs=placed,
        out_specs=(P(("row", "col"), None), P(("row", "col")), P()),
        check_vma=False,
    )
```

```python
import functools
import itertools

import jax
import jax.numpy as jnp
from jax import lax
from jax.experimental import pallas as pl
from jax.experimental.pallas import tpu as pltpu
from jax.sharding import PartitionSpec as P

MESH = pl.DeviceIdType.MESH
F32 = jnp.float32
BF16 = jnp.bfloat16
VMEM = pl.BlockSpec(memory_space=pltpu.VMEM)
HIGHEST = lax.Precision.HIGHEST
LIMIT = 60 * 1024 * 1024

PARTS = ((0, 48, (0, 1, 2)), (48, 48, (1, 2, 0)), (96, 32, (2, 0, 1)))


def place():
    row, col = lax.axis_index("row"), lax.axis_index("col")
    y, z_lo, core = row // 4, (row // 2) % 2, row % 2
    z_hi, x = col // 4, col % 4
    return (x, y, z_hi * 2 + z_lo), core


def device(at, core):
    x, y, z = at
    return (y * 4 + (z % 2) * 2 + core, (z // 2) * 4 + x)


def moved(at, axis, offset):
    return tuple((c + offset) % 4 if a == axis else c for a, c in enumerate(at))


class Copies:
    def __init__(self, send, recv):
        self.send, self.recv, self.used = send, recv, 0

    def start(self, src, dst, target):
        n = self.used
        self.used += 1
        copy = pltpu.make_async_remote_copy(
            src_ref=src,
            dst_ref=dst,
            send_sem=self.send.at[n],
            recv_sem=self.recv.at[n],
            device_id=target,
            device_id_type=MESH,
        )
        copy.start()
        return copy


def greet(peers):
    barrier = pltpu.get_barrier_semaphore()
    for peer in peers:
        pl.semaphore_signal(barrier, inc=1, device_id=peer, device_id_type=MESH)
    pl.semaphore_wait(barrier, len(peers))


def axis_peers(at, core):
    return [device(moved(at, a, o), core) for a in range(3) for o in (1, 2, 3)]


def pick(axes, at, rows=None):
    index = tuple(at[a] if a in axes else slice(None) for a in range(3))
    return index if rows is None else (*index, rows)


def gram_kernel(
    n_total, x_ref, b_ref, label_ref, g_ref, s_ref, mean_ref, count_ref,
    c_ref, local_ref, theirs_ref, note, note_recv, mhalf, mrecv, delta_ref, daug, gt, half, recv0,
    q1a, q1b, q1c, o1a, o1b, o1c, t1a, t1b, t1c, q2a, q2b, q2c, o2a, o2b, o2c, t2a, t2b, t2c, r3a, r3b, r3c,
    gme, s_half, sr0, sr1, ss1, sr2, ss2, send, recv,
):
    at, core = place()
    x, y, z = at
    other = 1 - core
    copies = Copies(send, recv)
    partner = device(at, other)
    greet([partner, *axis_peers(at, core)])
    n_local, width = x_ref.shape
    step = 512

    @pl.loop(0, width // step)
    def _(j):
        lanes = pl.ds(pl.multiple_of(j * step, step), step)
        m = jnp.sum(x_ref[:, lanes].astype(F32), 0, keepdims=True) * (1.0 / n_local)
        for i in range(step // 128):
            local_ref[pl.ds(step // 128 * j + i, 1), :] = m[:, i * 128 : (i + 1) * 128]

    copy = copies.start(local_ref, theirs_ref, partner)
    ids = lax.broadcasted_iota(jnp.int32, (16, step), 0)

    @pl.loop(0, width // step)
    def _(j):
        lanes = pl.ds(pl.multiple_of(j * step, step), step)
        m = jnp.concatenate([local_ref[pl.ds(step // 128 * j + i, 1), :] for i in range(step // 128)], 1)
        c_ref[0:n_local, lanes] = (x_ref[:, lanes].astype(F32) - m).astype(BF16)
        high = m.astype(BF16).astype(F32)
        middle = (m - high).astype(BF16).astype(F32)
        low = (m - high) - middle
        tile = jnp.where(ids == 0, high, jnp.where(ids == 1, middle, jnp.where(ids == 2, low, 0.0)))
        c_ref[n_local : n_local + 16, lanes] = tile.astype(BF16)

    first = jnp.dot(c_ref[...], b_ref[...], preferred_element_type=F32)
    t_local = (first[n_local : n_local + 1] + first[n_local + 1 : n_local + 2]) + first[n_local + 2 : n_local + 3]
    is_ref = (label_ref[...] == 0).astype(F32)
    ids = lax.broadcasted_iota(jnp.int32, (8, 128), 0)
    count = jnp.sum(is_ref, 1, keepdims=True)
    note[...] = jnp.where(ids == 0, count, jnp.where(ids == 1, t_local[:, :128], jnp.where(ids == 2, t_local[:, 128:], 0.0)))
    copy_note = copies.start(note, note_recv, partner)
    first_t = first[:n_local].T.astype(BF16)
    far = pl.ds(pl.multiple_of(other * 128, 128), 128)
    near = pl.ds(pl.multiple_of(core * 128, 128), 128)
    halves = []

    def gram_blocks(bx):
        @pl.loop(0, 4)
        def _(by):
            lanes = pl.ds(pl.multiple_of((bx * 4 + by) * 512, 512), 512)
            block = jnp.dot(first_t, c_ref[0:n_local, lanes], preferred_element_type=F32).astype(BF16)
            for bz in range(4):
                gt[bx, by, bz] = block[:, bz * 128 : (bz + 1) * 128]

        halves.append(copies.start(gt.at[bx, :, :, far, :], recv0.at[bx], partner))

    mine = pl.ds(pl.multiple_of(core * 32, 32), 32)
    copy.wait()
    copy_note.wait()
    mhalf[0, 0:32] = local_ref[mine, :] + theirs_ref[mine, :]
    mhalf[0, 32:40] = note[...] + note_recv[...]
    for a in range(3):
        waits = [copies.start(mhalf.at[a], mrecv.at[a, o - 1], device(moved(at, a, o), core)) for o in (1, 2, 3)]
        gram_blocks(a)
        if a == 2:
            gram_blocks(3)
        for w in waits:
            w.wait()
        mhalf[a + 1] = mhalf[a] + mrecv[a, 0] + mrecv[a, 1] + mrecv[a, 2]
    totals = mhalf[3, 32:40]
    count_ref[...] = totals
    mhalf[4, 0:32] = mhalf[3, 0:32] * (1.0 / 128.0)
    mean_ref[mine, :] = mhalf[4, 0:32]
    copy = copies.start(mhalf.at[4, pl.ds(0, 32)], mean_ref.at[mine], partner)

    mean_t = totals * (1.0 / 128.0)
    ids = lax.broadcasted_iota(jnp.int32, (16, 256), 0)
    taug = jnp.zeros((16, 256), F32)
    for k, tile in enumerate((note[...], note_recv[...])):
        tau = (tile - mean_t) * float(n_local)
        tau = jnp.concatenate([tau[1:2], tau[2:3]], 1)
        high = tau.astype(BF16).astype(F32)
        taug = jnp.where((ids == 3 * k) | (ids == 3 * k + 1), high, jnp.where(ids == 3 * k + 2, tau - high, taug))
    taug_t = taug.T
    taug_t = jnp.where(core == 0, taug_t[:128], taug_t[128:]).astype(BF16)
    copy.wait()
    delta_ref[...] = jnp.zeros_like(delta_ref)
    for k, source in enumerate((local_ref, theirs_ref)):
        delta = source[...] - mean_ref[...]
        high = delta.astype(BF16).astype(F32)
        delta_ref[:, 3 * k, :] = high
        delta_ref[:, 3 * k + 1, :] = delta - high
        delta_ref[:, 3 * k + 2, :] = high
    daug[...] = delta_ref[...].astype(BF16)

    for bx in range(4):
        halves[bx].wait()

        @pl.loop(0, 4)
        def _(by):
            for bz in range(4):
                extra = jnp.dot(taug_t, daug[(bx * 4 + by) * 4 + bz], preferred_element_type=F32)
                both = gt[bx, by, bz, near, :].astype(F32) + recv0[bx, by, bz].astype(F32)
                half[bx, by, bz] = (both + extra).astype(BF16)

    def exchange(parts, dtype, source, incoming, outgoing, result):
        todo = []
        for i, (axis, size) in enumerate(parts):
            up, down = device(moved(at, axis, 1), core), device(moved(at, axis, 3), core)
            chunks = [source(i, (at[axis] + o) % 4) for o in range(4)]
            low, high = pl.ds(0, 2), pl.ds(2, 2)
            box = incoming[i]
            first_up = copies.start(chunks[2].at[low], box.at[0], up)
            first_down = copies.start(chunks[2].at[high], box.at[1], down)
            near_up = copies.start(chunks[1].at[high], box.at[2], up)
            near_down = copies.start(chunks[3].at[low], box.at[3], down)
            todo.append((up, down, chunks, first_up, first_down, near_up, near_down))
        last = []
        for i, (up, down, chunks, first_up, first_down, _, _) in enumerate(todo):
            box, out = incoming[i], outgoing[i]
            first_up.wait()
            out[0] = chunks[1][0:2] + box[0]
            add_up = copies.start(out.at[0], box.at[4], up)
            first_down.wait()
            out[1] = chunks[3][2:4] + box[1]
            add_down = copies.start(out.at[1], box.at[5], down)
            last.append((add_up, add_down))
        for i, (_, _, chunks, _, _, near_up, near_down) in enumerate(todo):
            box = incoming[i]
            near_up.wait()
            near_down.wait()
            for w in last[i]:
                w.wait()
            own = chunks[0]
            result[i][0:2] = (own[0:2].astype(F32) + box[3].astype(F32)) + box[4].astype(F32)
            result[i][2:4] = (own[2:4].astype(F32) + box[2].astype(F32)) + box[5].astype(F32)

    orders = [order for _, _, order in PARTS]
    t1s, t2s = (t1a, t1b, t1c), (t2a, t2b, t2c)

    def stage_one(i, k):
        start, size, order = PARTS[i]
        to = tuple(k for _ in range(3))
        return half.at[pick(order[:1], to, slice(start, start + size))]

    def stage_two(i, k):
        _, _, order = PARTS[i]
        left = [a for a in range(3) if a != order[0]]
        return t1s[i].at[k] if left[0] == order[1] else t1s[i].at[:, k]

    exchange([(o[0], 0) for o in orders], BF16, stage_one, (q1a, q1b, q1c), (o1a, o1b, o1c), t1s)
    exchange([(o[1], 0) for o in orders], F32, stage_two, (q2a, q2b, q2c), (o2a, o2b, o2c), t2s)
    waits = []
    for (start, size, order), t2, r3 in zip(PARTS, t2s, (r3a, r3b, r3c)):
        for o in (1, 2, 3):
            to = moved(at, order[2], o)
            waits.append(copies.start(t2.at[to[order[2]]], r3.at[o - 1], device(to, core)))
    for w in waits:
        w.wait()
    for (start, size, order), t2, r3 in zip(PARTS, t2s, (r3a, r3b, r3c)):
        total = (t2[at[order[2]]] + r3[0]) + (r3[1] + r3[2])
        gme[start : start + size, :] = total * (1.0 / n_total)
    g_ref[near, :] = gme[...]
    copies.start(gme, g_ref.at[near], partner).wait()

    square = lax.dot_general(
        gme[...], g_ref[...], (((1,), (1,)), ((), ())), precision=HIGHEST, preferred_element_type=F32
    )
    s_half[0] = square[:, :128]
    s_half[1] = square[:, 128:]
    waits = []
    for o in (1, 2, 3):
        to = moved(at, 0, o)
        rows = pl.ds(pl.multiple_of(to[0] * 32, 32), 32)
        waits.append(copies.start(s_half.at[:, rows, :], sr0.at[o - 1], device(to, core)))
    for w in waits:
        w.wait()
    ss1[...] = (s_half[:, pl.ds(pl.multiple_of(x * 32, 32), 32), :] + sr0[0]) + (sr0[1] + sr0[2])
    waits = []
    for o in (1, 2, 3):
        to = moved(at, 1, o)
        rows = pl.ds(pl.multiple_of(to[1] * 8, 8), 8)
        waits.append(copies.start(ss1.at[:, rows, :], sr1.at[o - 1], device(to, core)))
    for w in waits:
        w.wait()
    ss2[...] = (ss1[:, pl.ds(pl.multiple_of(y * 8, 8), 8), :] + sr1[0]) + (sr1[1] + sr1[2])
    waits = []
    for o in (1, 2, 3):
        waits.append(copies.start(ss2, sr2.at[z], device(moved(at, 2, o), core)))
    sr2[z] = ss2[...]
    for w in waits:
        w.wait()
    base = pl.multiple_of(core * 128 + x * 32 + y * 8, 8)
    s_ref[:, pl.ds(base, 8), :] = (sr2[0] + sr2[1]) + (sr2[2] + sr2[3])
    for axis, rows in (
        (1, pl.ds(base, 8)),
        (0, pl.ds(pl.multiple_of(core * 128 + x * 32, 32), 32)),
    ):
        view = s_ref.at[:, rows, :]
        waits = [copies.start(view, view, device(moved(at, axis, o), core)) for o in (1, 2, 3)]
        for w in waits:
            w.wait()
    view = s_ref.at[:, near, :]
    copies.start(view, view, partner).wait()


def gram_and_square(samples, basis_start, labels, n_total):
    scratch = [
        pltpu.VMEM((272, 8192), BF16),
        pltpu.VMEM((64, 128), F32),
        pltpu.VMEM((64, 128), F32),
        pltpu.VMEM((8, 128), F32),
        pltpu.VMEM((8, 128), F32),
        pltpu.VMEM((5, 40, 128), F32),
        pltpu.VMEM((3, 3, 40, 128), F32),
        pltpu.VMEM((64, 16, 128), F32),
        pltpu.VMEM((64, 16, 128), BF16),
        pltpu.VMEM((4, 4, 4, 256, 128), BF16),
        pltpu.VMEM((4, 4, 4, 128, 128), BF16),
        pltpu.VMEM((4, 4, 4, 128, 128), BF16),
        *[pltpu.VMEM((6, 2, 4, size, 128), BF16) for _, size, _ in PARTS],
        *[pltpu.VMEM((2, 2, 4, size, 128), BF16) for _, size, _ in PARTS],
        *[pltpu.VMEM((4, 4, size, 128), F32) for _, size, _ in PARTS],
        *[pltpu.VMEM((6, 2, size, 128), F32) for _, size, _ in PARTS],
        *[pltpu.VMEM((2, 2, size, 128), F32) for _, size, _ in PARTS],
        *[pltpu.VMEM((4, size, 128), F32) for _, size, _ in PARTS],
        *[pltpu.VMEM((3, size, 128), F32) for _, size, _ in PARTS],
        pltpu.VMEM((128, 128), F32),
        pltpu.VMEM((2, 128, 128), F32),
        pltpu.VMEM((3, 2, 32, 128), F32),
        pltpu.VMEM((3, 2, 8, 128), F32),
        pltpu.VMEM((2, 32, 128), F32),
        pltpu.VMEM((4, 2, 8, 128), F32),
        pltpu.VMEM((2, 8, 128), F32),
        pltpu.SemaphoreType.DMA((78,)),
        pltpu.SemaphoreType.DMA((78,)),
    ]
    return pl.pallas_call(
        functools.partial(gram_kernel, n_total),
        out_shape=(
            jax.ShapeDtypeStruct((256, 128), F32),
            jax.ShapeDtypeStruct((2, 256, 128), F32),
            jax.ShapeDtypeStruct((64, 128), F32),
            jax.ShapeDtypeStruct((8, 128), F32),
        ),
        in_specs=[VMEM, VMEM, VMEM],
        out_specs=(VMEM, VMEM, VMEM, VMEM),
        scratch_shapes=scratch,
        compiler_params=pltpu.CompilerParams(collective_id=0, has_side_effects=True, vmem_limit_bytes=LIMIT),
        name="gram",
    )(samples, basis_start, labels.reshape(1, 256))


def small_inverse(t):
    sub = lax.broadcasted_iota(jnp.int32, (8, 128), 0)
    t = list(t)
    for s in range(4):
        rows = [jnp.broadcast_to(t[s][i : i + 1, :], (8, 128)) for i in range(8)]
        e = [[jnp.broadcast_to(rows[i][:, 8 * s + j : 8 * s + j + 1], (8, 128)) for j in range(i + 1)] for i in range(8)]
        inv, low = [], [[None] * 8 for _ in range(8)]
        for j in range(8):
            inv.append(1.0 / e[j][j])
            for i in range(j + 1, 8):
                low[i][j] = e[i][j] * inv[j]
            for i in range(j + 1, 8):
                for m in range(j + 1, i + 1):
                    e[i][m] = e[i][m] - low[i][j] * e[m][j]
        w = []
        for i in range(8):
            v = rows[i]
            for j in range(i):
                v = v - low[i][j] * w[j]
            w.append(v)
        for b in range(s + 1, 4):
            f = []
            for j in range(8):
                v = jnp.broadcast_to(t[b][:, 8 * s + j : 8 * s + j + 1], (8, 128))
                for k in range(j):
                    v = v - f[k] * e[j][k]
                f.append(v * inv[j])
            for j in range(8):
                t[b] = t[b] - f[j] * w[j]
        out = w[0] * lax.rsqrt(e[0][0])
        for i in range(1, 8):
            out = jnp.where(sub == i, w[i] * lax.rsqrt(e[i][i]), out)
        t[s] = out
    return t


def inverse_factor(s_ref, m_ref):
    r = lax.broadcasted_iota(jnp.int32, (256, 256), 0)
    c = lax.broadcasted_iota(jnp.int32, (256, 256), 1)
    m_ref[:, 0:128] = s_ref[0]
    m_ref[:, 128:256] = s_ref[1]
    m_ref[:, 256:512] = (r == c).astype(F32)
    lane = lax.broadcasted_iota(jnp.int32, (32, 128), 1)
    unit = (lane == lax.broadcasted_iota(jnp.int32, (32, 128), 0) + 32).astype(F32)
    wide = lax.broadcasted_iota(jnp.int32, (32, 256), 1)

    def panel(b, carry):
        rows = pl.ds(pl.multiple_of(b * 32, 32), 32)
        tile = m_ref[rows, pl.ds(pl.multiple_of((b // 4) * 128, 128), 128)]
        tile = pltpu.roll(tile, (4 - b % 4) % 4 * 32, 1)
        tile = jnp.where(lane < 32, tile, unit)
        t = small_inverse([tile[8 * i : 8 * i + 8] for i in range(4)])
        inv = jnp.concatenate(t, 0)[:, 32:64]
        w = jnp.dot(inv, m_ref[rows, :], precision=HIGHEST, preferred_element_type=F32)
        left = jnp.where(wide >= (b + 1) * 32, w[:, :256], 0.0)
        m_ref[...] -= lax.dot_general(left, w, (((0,), (0,)), ((), ())), precision=HIGHEST, preferred_element_type=F32)
        m_ref[rows, :] = w
        return carry

    lax.fori_loop(0, 8, panel, 0)


STEPS = ((0, 0, 0), (3, 0, 0), (0, 0, 3), (0, 1, 0), (2, 0, 0), (0, 3, 3), (3, 0, 1), (1, 1, 0), (0, 2, 3), (0, 0, 2), (2, 0, 1), (0, 2, 0))
PARENTS = ((0, 0, 0), (0, 0, 0), (0, 0, 0), (3, 0, 0), (0, 0, 3), (3, 0, 0), (0, 1, 0), (0, 3, 3), (0, 0, 3), (2, 0, 0), (0, 1, 0))


def difference(a, b):
    return tuple((i - j) % 4 for i, j in zip(a, b))


def panel_plan():
    parent = [None, *[STEPS.index(p) for p in PARENTS]]
    depth = [0] * len(STEPS)
    for s in range(1, len(STEPS)):
        depth[s] = depth[parent[s]] + 1
    best = {}
    for r, row in enumerate(STEPS):
        for c, column in enumerate(STEPS):
            d = difference(row, column)
            cost = (max(depth[r], depth[c]), depth[r] + depth[c], r)
            if d not in best or cost < best[d][0]:
                best[d] = (cost, r, c)
    units = sorted((cost[0], r, c) for cost, r, c in best.values())
    assert len(units) == 64
    return parent, depth, units


def spanning_tree():
    def far(step):
        return sum(min(c, 4 - c) for c in step)

    steps = sorted(itertools.product(range(4), repeat=3), key=lambda step: (far(step), step))
    load = {(a, o): 0 for a in range(3) for o in (1, 3)}
    parent = [None]
    for step in steps[1:]:
        choices = []
        for (a, o), used in load.items():
            before = moved(step, a, 4 - o)
            if far(before) == far(step) - 1:
                choices.append((used, a, o, steps.index(before)))
        _, a, o, before = min(choices)
        load[a, o] += 1
        parent.append(before)
    return steps, parent, [far(step) for step in steps]


def project_kernel(
    n_total, width_ref, g_ref, s_ref, x_ref, mean_ref, n_ref_ref, label_ref, basis_ref, proj_ref, out_ref,
    m_ref, p_acc, blocks, columns, rows_ref, acc, got, send, recv,
):
    at, core = place()
    other = 1 - core
    copies = Copies(send, recv)
    partner = device(at, other)
    parent, depth, units = panel_plan()
    neighbours = [device(moved(at, a, o), core) for a in range(3) for o in (1, 3)]
    greet([partner, *neighbours])

    def moved_by(step):
        return tuple((c + i) % 4 for c, i in zip(at, step))

    def toward(step):
        return device(moved_by(step), core)

    inverse_factor(s_ref, m_ref)
    block = lax.dot_general(
        g_ref[...], m_ref[:, 256:512], (((0,), (1,)), ((), ())), precision=HIGHEST, preferred_element_type=F32
    ).astype(BF16)
    basis_ref[(at[0] * 4 + at[1]) * 4 + at[2]] = block

    steps, source, level_of = spanning_tree()
    half = pl.ds(pl.multiple_of(core * 64, 64), 64)

    def chip(s):
        x, y, z = moved_by(steps[s])
        return (x * 4 + y) * 4 + z

    links, across = {}, {}
    p_acc[...] = jnp.zeros_like(p_acc)

    def add_level(level):
        total = p_acc[...]
        for s in range(64):
            if level_of[s] == level:
                if s:
                    across[s].wait()
                b = chip(s)
                lanes = pl.ds(pl.multiple_of(b * 128, 128), 128)
                centred = (x_ref[:, lanes].astype(F32) - mean_ref[pl.ds(b, 1), :]).astype(BF16)
                total += jnp.dot(centred, basis_ref[b], preferred_element_type=F32)
        p_acc[...] = total

    for level in range(7):
        for s in range(64):
            if level_of[s] != level:
                continue
            if s:
                links[s].wait()
            view = basis_ref.at[chip(s), half, :]
            for child in range(1, 64):
                if source[child] == s:
                    links[child] = copies.start(view, view, toward(difference(steps[s], steps[child])))
            if s:
                across[s] = copies.start(view, view, partner)
        if level:
            add_level(level - 1)
    add_level(6)
    p = p_acc[...].astype(BF16)
    proj_ref[...] = p
    wide = p.astype(F32)
    norm = jnp.broadcast_to(jnp.sum(wide * wide, 1, keepdims=True) * -0.5, (256, 128)).T
    norm = jnp.concatenate([norm[:128, :128], norm[:128, 128:]], 1)[0:1]
    high = norm.astype(BF16).astype(F32)
    middle = (norm - high).astype(BF16).astype(F32)
    low = (norm - high) - middle
    is_ref = (label_ref[...] == 0).astype(F32)
    ids = lax.broadcasted_iota(jnp.int32, (16, 256), 0)
    tail = jnp.where(ids == 0, is_ref, jnp.where(ids == 1, high, jnp.where(ids == 2, middle, jnp.where(ids == 3, low, 0.0))))
    blocks[0, core, 0:256, :] = p
    blocks[0, core, 256:272, :] = tail.astype(BF16)

    edges, cores = {}, {}

    def hand_on(s):
        view = blocks.at[s, core]
        for child in range(1, len(STEPS)):
            if parent[child] == s:
                target = toward(difference(STEPS[s], STEPS[child]))
                edges[child] = copies.start(view, blocks.at[child, core], target)
        cores[s] = copies.start(view, view, partner)

    scale = 1.4426950408889634 / (128.0 * jnp.exp2(jnp.full((1, 256), width_ref[0], jnp.int32).astype(F32)))
    ids = lax.broadcasted_iota(jnp.int32, (16, 256), 0)
    lanes = lax.broadcasted_iota(jnp.int32, (16, 256), 1)
    select = jnp.where(lanes < 128, jnp.where((ids > 0) & (ids < 4), 1.0, 0.0), jnp.where(ids == 0, 1.0, 0.0)).astype(BF16)

    def prepare(s):
        for k in range(2):
            ends = blocks[s, k, 256:272, :].astype(F32).T.astype(BF16)
            columns[s, k] = jnp.dot(ends, select, preferred_element_type=F32)
        ends = blocks[s, core, 256:272, :].astype(F32)
        rows_ref[s] = jnp.broadcast_to((ends[1:2] + ends[2:3]) + ends[3:4], (8, 256))

    for s in range(len(STEPS)):
        acc[s, 0] = jnp.zeros((8, 256), F32)
        acc[s, 1] = jnp.zeros((8, 256), F32)
    hand_on(0)
    for level in range(max(depth) + 1):
        here = [s for s in range(len(STEPS)) if depth[s] == level]
        for s in here:
            if s:
                edges[s].wait()
                hand_on(s)
        for s in here:
            cores[s].wait()
            prepare(s)
        for _, r, c in [u for u in units if u[0] == level]:
            row_norm = rows_ref[r][0:1]
            rows = blocks[r, core, 0:256, :]
            total, refs = acc[r, 0], acc[r, 1]
            for k in range(2):
                inner = lax.dot_general(
                    blocks[c, k, 0:256, :], rows, (((1,), (1,)), ((), ())), preferred_element_type=F32
                )
                norm, mark = columns[c, k, :, :128], columns[c, k, :, 128:]
                norm, mark = jnp.concatenate([norm, norm], 1), jnp.concatenate([mark, mark], 1)
                value = jnp.exp2(((inner + norm) + row_norm) * scale)
                total += jnp.sum(value.reshape(32, 8, 256), 0)
                refs += jnp.sum((value * mark).reshape(32, 8, 256), 0)
            acc[r, 0], acc[r, 1] = total, refs

    for level in range(max(depth), 0, -1):
        here = [s for s in range(1, len(STEPS)) if depth[s] == level]
        waits = [copies.start(acc.at[s], got.at[s], toward(difference(STEPS[s], STEPS[parent[s]]))) for s in here]
        for s, w in zip(here, waits):
            w.wait()
            acc[parent[s]] += got[s]
    row_sums = jnp.sum(acc[0, 0], 0, keepdims=True)
    ref_sums = jnp.sum(acc[0, 1], 0, keepdims=True)
    n_ref = n_ref_ref[0:1, 0:1]
    n_cur = n_total - n_ref
    proof = (ref_sums / n_ref - (row_sums - ref_sums) / n_cur) / (row_sums / n_total)
    out_ref[...] = jnp.broadcast_to(proof, (8, 256))


def project_and_prove(g, square, samples, mean, n_ref, labels, width_index, n_total):
    count = len(STEPS)
    copies = 126 + 3 * count - 2
    basis, projected, proof = pl.pallas_call(
        functools.partial(project_kernel, n_total),
        out_shape=(
            jax.ShapeDtypeStruct((64, 128, 256), BF16),
            jax.ShapeDtypeStruct((256, 256), BF16),
            jax.ShapeDtypeStruct((8, 256), F32),
        ),
        in_specs=[pl.BlockSpec(memory_space=pltpu.SMEM), *[VMEM] * 6],
        out_specs=(VMEM, VMEM, VMEM),
        scratch_shapes=[
            pltpu.VMEM((256, 512), F32),
            pltpu.VMEM((256, 256), F32),
            pltpu.VMEM((count, 2, 272, 256), BF16),
            pltpu.VMEM((count, 2, 256, 256), F32),
            pltpu.VMEM((count, 8, 256), F32),
            pltpu.VMEM((count, 2, 8, 256), F32),
            pltpu.VMEM((count, 2, 8, 256), F32),
            pltpu.SemaphoreType.DMA((copies,)),
            pltpu.SemaphoreType.DMA((copies,)),
        ],
        compiler_params=pltpu.CompilerParams(collective_id=1, has_side_effects=True, vmem_limit_bytes=LIMIT),
        name="project",
    )(width_index.reshape(1), g, square, samples, mean, n_ref, labels.reshape(1, 256))
    return basis.reshape(8192, 256), projected, proof[0]


def local(n_total, samples, labels, basis_start, width_index):
    g, square, mean, n_ref = gram_and_square(samples, basis_start, labels, n_total)
    basis, projected, proof = project_and_prove(g, square, samples, mean, n_ref, labels, width_index, n_total)
    return projected, proof, basis


def solution(mesh):
    n_total = float(256 * mesh.size)
    placed = (P(("row", "col"), None), P(("row", "col")), P(), P())
    return jax.shard_map(
        functools.partial(local, n_total),
        mesh=mesh,
        in_specs=placed,
        out_specs=(P(("row", "col"), None), P(("row", "col")), P()),
        check_vma=False,
    )
```

```python
import functools
import itertools

import jax
import jax.numpy as jnp
from jax import lax
from jax.experimental import pallas as pl
from jax.experimental.pallas import tpu as pltpu
from jax.sharding import PartitionSpec as P

MESH = pl.DeviceIdType.MESH
F32 = jnp.float32
BF16 = jnp.bfloat16
VMEM = pl.BlockSpec(memory_space=pltpu.VMEM)
HIGHEST = lax.Precision.HIGHEST
LIMIT = 60 * 1024 * 1024

PARTS = ((0, 48, (0, 1, 2)), (48, 48, (1, 2, 0)), (96, 32, (2, 0, 1)))


def place():
    row, col = lax.axis_index("row"), lax.axis_index("col")
    y, z_lo, core = row // 4, (row // 2) % 2, row % 2
    z_hi, x = col // 4, col % 4
    return (x, y, z_hi * 2 + z_lo), core


def device(at, core):
    x, y, z = at
    return (y * 4 + (z % 2) * 2 + core, (z // 2) * 4 + x)


def moved(at, axis, offset):
    return tuple((c + offset) % 4 if a == axis else c for a, c in enumerate(at))


class Copies:
    def __init__(self, send, recv):
        self.send, self.recv, self.used = send, recv, 0

    def start(self, src, dst, target):
        n = self.used
        self.used += 1
        copy = pltpu.make_async_remote_copy(
            src_ref=src,
            dst_ref=dst,
            send_sem=self.send.at[n],
            recv_sem=self.recv.at[n],
            device_id=target,
            device_id_type=MESH,
        )
        copy.start()
        return copy


def greet(peers):
    barrier = pltpu.get_barrier_semaphore()
    for peer in peers:
        pl.semaphore_signal(barrier, inc=1, device_id=peer, device_id_type=MESH)
    pl.semaphore_wait(barrier, len(peers))


def axis_peers(at, core):
    return [device(moved(at, a, o), core) for a in range(3) for o in (1, 2, 3)]


def pick(axes, at, rows=None):
    index = tuple(at[a] if a in axes else slice(None) for a in range(3))
    return index if rows is None else (*index, rows)


def gram_part(
    n_total, at, core, copies, x_loads, b_load, x_ref, b_ref, label_ref, g_ref, s_ref, mean_ref, count_ref,
    c_ref, local_ref, theirs_ref, note, note_recv, mhalf, mrecv, notes, nrecv, delta_ref, daug, gt, half, recv0,
    q1a, q1b, q1c, o1a, o1b, o1c, t1a, t1b, t1c, q2a, q2b, q2c, o2a, o2b, o2c, t2a, t2b, t2c, r3a, r3b, r3c,
    gme, s_half, sr0, sr1, ss1, sr2, ss2,
):
    other = 1 - core
    partner = device(at, other)
    n_local, width = x_ref.shape
    step = 512
    turns = width // step // len(x_loads)

    for chunk, load in enumerate(x_loads):
        load.wait()

        @pl.loop(chunk * turns, (chunk + 1) * turns)
        def _(j):
            lanes = pl.ds(pl.multiple_of(j * step, step), step)
            m = jnp.sum(x_ref[:, lanes].astype(F32), 0, keepdims=True) * (1.0 / n_local)
            for i in range(step // 128):
                local_ref[pl.ds(step // 128 * j + i, 1), :] = m[:, i * 128 : (i + 1) * 128]

    copy = copies.start(local_ref, theirs_ref, partner)
    ids = lax.broadcasted_iota(jnp.int32, (16, step), 0)

    @pl.loop(0, width // step)
    def _(j):
        lanes = pl.ds(pl.multiple_of(j * step, step), step)
        m = jnp.concatenate([local_ref[pl.ds(step // 128 * j + i, 1), :] for i in range(step // 128)], 1)
        c_ref[0:n_local, lanes] = (x_ref[:, lanes].astype(F32) - m).astype(BF16)
        high = m.astype(BF16).astype(F32)
        middle = (m - high).astype(BF16).astype(F32)
        low = (m - high) - middle
        tile = jnp.where(ids == 0, high, jnp.where(ids == 1, middle, jnp.where(ids == 2, low, 0.0)))
        c_ref[n_local : n_local + 16, lanes] = tile.astype(BF16)

    def start_axis(values, landing, a):
        return [copies.start(values.at[a], landing.at[a, o - 1], device(moved(at, a, o), core)) for o in (1, 2, 3)]

    def end_axis(values, landing, a, waits):
        for w in waits:
            w.wait()
        values[a + 1] = values[a] + landing[a, 0] + landing[a, 1] + landing[a, 2]

    mine = pl.ds(pl.multiple_of(core * 32, 32), 32)
    copy.wait()
    mhalf[0] = local_ref[mine, :] + theirs_ref[mine, :]
    mean_waits = start_axis(mhalf, mrecv, 0)
    b_load.wait()

    first = jnp.dot(c_ref[...], b_ref[...], preferred_element_type=F32)
    t_local = (first[n_local : n_local + 1] + first[n_local + 1 : n_local + 2]) + first[n_local + 2 : n_local + 3]
    is_ref = (label_ref[...] == 0).astype(F32)
    ids = lax.broadcasted_iota(jnp.int32, (8, 128), 0)
    count = jnp.sum(is_ref, 1, keepdims=True)
    note[...] = jnp.where(ids == 0, count, jnp.where(ids == 1, t_local[:, :128], jnp.where(ids == 2, t_local[:, 128:], 0.0)))
    copy_note = copies.start(note, note_recv, partner)
    first_t = first[:n_local].T.astype(BF16)
    far = pl.ds(pl.multiple_of(other * 128, 128), 128)
    near = pl.ds(pl.multiple_of(core * 128, 128), 128)
    halves = []

    def gram_blocks(bx):
        @pl.loop(0, 4)
        def _(by):
            lanes = pl.ds(pl.multiple_of((bx * 4 + by) * 512, 512), 512)
            block = jnp.dot(first_t, c_ref[0:n_local, lanes], preferred_element_type=F32).astype(BF16)
            for bz in range(4):
                gt[bx, by, bz] = block[:, bz * 128 : (bz + 1) * 128]

        halves.append(copies.start(gt.at[bx, :, :, far, :], recv0.at[bx], partner))

    end_axis(mhalf, mrecv, 0, mean_waits)
    mean_waits = start_axis(mhalf, mrecv, 1)
    copy_note.wait()
    notes[0] = note[...] + note_recv[...]
    note_waits = start_axis(notes, nrecv, 0)
    gram_blocks(0)
    end_axis(mhalf, mrecv, 1, mean_waits)
    mean_waits = start_axis(mhalf, mrecv, 2)
    end_axis(notes, nrecv, 0, note_waits)
    note_waits = start_axis(notes, nrecv, 1)
    gram_blocks(1)
    end_axis(mhalf, mrecv, 2, mean_waits)
    mhalf[4] = mhalf[3] * (1.0 / 128.0)
    mean_ref[mine, :] = mhalf[4]
    copy = copies.start(mhalf.at[4], mean_ref.at[mine], partner)
    end_axis(notes, nrecv, 1, note_waits)
    note_waits = start_axis(notes, nrecv, 2)
    gram_blocks(2)
    gram_blocks(3)
    end_axis(notes, nrecv, 2, note_waits)
    totals = notes[3]
    count_ref[...] = totals

    mean_t = totals * (1.0 / 128.0)
    ids = lax.broadcasted_iota(jnp.int32, (16, 256), 0)
    taug = jnp.zeros((16, 256), F32)
    for k, tile in enumerate((note[...], note_recv[...])):
        tau = (tile - mean_t) * float(n_local)
        tau = jnp.concatenate([tau[1:2], tau[2:3]], 1)
        high = tau.astype(BF16).astype(F32)
        taug = jnp.where((ids == 3 * k) | (ids == 3 * k + 1), high, jnp.where(ids == 3 * k + 2, tau - high, taug))
    taug_t = taug.T
    taug_t = jnp.where(core == 0, taug_t[:128], taug_t[128:]).astype(BF16)
    copy.wait()
    delta_ref[...] = jnp.zeros_like(delta_ref)
    for k, source in enumerate((local_ref, theirs_ref)):
        delta = source[...] - mean_ref[...]
        high = delta.astype(BF16).astype(F32)
        delta_ref[:, 3 * k, :] = high
        delta_ref[:, 3 * k + 1, :] = delta - high
        delta_ref[:, 3 * k + 2, :] = high
    daug[...] = delta_ref[...].astype(BF16)

    for bx in range(4):
        halves[bx].wait()

        @pl.loop(0, 4)
        def _(by):
            for bz in range(4):
                extra = jnp.dot(taug_t, daug[(bx * 4 + by) * 4 + bz], preferred_element_type=F32)
                both = gt[bx, by, bz, near, :].astype(F32) + recv0[bx, by, bz].astype(F32)
                half[bx, by, bz] = (both + extra).astype(BF16)

    def exchange(parts, dtype, source, incoming, outgoing, result):
        todo = []
        for i, (axis, size) in enumerate(parts):
            up, down = device(moved(at, axis, 1), core), device(moved(at, axis, 3), core)
            chunks = [source(i, (at[axis] + o) % 4) for o in range(4)]
            low, high = pl.ds(0, 2), pl.ds(2, 2)
            box = incoming[i]
            first_up = copies.start(chunks[2].at[low], box.at[0], up)
            first_down = copies.start(chunks[2].at[high], box.at[1], down)
            near_up = copies.start(chunks[1].at[high], box.at[2], up)
            near_down = copies.start(chunks[3].at[low], box.at[3], down)
            todo.append((up, down, chunks, first_up, first_down, near_up, near_down))
        last = []
        for i, (up, down, chunks, first_up, first_down, _, _) in enumerate(todo):
            box, out = incoming[i], outgoing[i]
            first_up.wait()
            out[0] = chunks[1][0:2] + box[0]
            add_up = copies.start(out.at[0], box.at[4], up)
            first_down.wait()
            out[1] = chunks[3][2:4] + box[1]
            add_down = copies.start(out.at[1], box.at[5], down)
            last.append((add_up, add_down))
        for i, (_, _, chunks, _, _, near_up, near_down) in enumerate(todo):
            box = incoming[i]
            near_up.wait()
            near_down.wait()
            for w in last[i]:
                w.wait()
            own = chunks[0]
            result[i][0:2] = (own[0:2].astype(F32) + box[3].astype(F32)) + box[4].astype(F32)
            result[i][2:4] = (own[2:4].astype(F32) + box[2].astype(F32)) + box[5].astype(F32)

    orders = [order for _, _, order in PARTS]
    t1s, t2s = (t1a, t1b, t1c), (t2a, t2b, t2c)

    def stage_one(i, k):
        start, size, order = PARTS[i]
        to = tuple(k for _ in range(3))
        return half.at[pick(order[:1], to, slice(start, start + size))]

    def stage_two(i, k):
        _, _, order = PARTS[i]
        left = [a for a in range(3) if a != order[0]]
        return t1s[i].at[k] if left[0] == order[1] else t1s[i].at[:, k]

    exchange([(o[0], 0) for o in orders], BF16, stage_one, (q1a, q1b, q1c), (o1a, o1b, o1c), t1s)
    exchange([(o[1], 0) for o in orders], F32, stage_two, (q2a, q2b, q2c), (o2a, o2b, o2c), t2s)
    waits = []
    for (start, size, order), t2, r3 in zip(PARTS, t2s, (r3a, r3b, r3c)):
        for o in (1, 2, 3):
            to = moved(at, order[2], o)
            waits.append(copies.start(t2.at[to[order[2]]], r3.at[o - 1], device(to, core)))
    for w in waits:
        w.wait()
    for (start, size, order), t2, r3 in zip(PARTS, t2s, (r3a, r3b, r3c)):
        total = (t2[at[order[2]]] + r3[0]) + (r3[1] + r3[2])
        gme[start : start + size, :] = total * (1.0 / n_total)
    g_ref[near, :] = gme[...]
    copies.start(gme, g_ref.at[near], partner).wait()

    square = lax.dot_general(
        gme[...], g_ref[...], (((1,), (1,)), ((), ())), precision=HIGHEST, preferred_element_type=F32
    )
    s_half[0] = square[:, :128]
    s_half[1] = square[:, 128:]
    plans = ((0, (0, 1, 2)), (1, (1, 2, 0)))

    def band(h, position, size):
        return pl.ds(pl.multiple_of(position * size, size), size)

    waits = []
    for h, order in plans:
        for o in (1, 2, 3):
            to = moved(at, order[0], o)
            waits.append(
                copies.start(s_half.at[h, band(h, to[order[0]], 32), :], sr0.at[h, o - 1], device(to, core))
            )
    for w in waits:
        w.wait()
    waits = []
    for h, order in plans:
        ss1[h] = (s_half[h, band(h, at[order[0]], 32), :] + sr0[h, 0]) + (sr0[h, 1] + sr0[h, 2])
        for o in (1, 2, 3):
            to = moved(at, order[1], o)
            waits.append(copies.start(ss1.at[h, band(h, to[order[1]], 8), :], sr1.at[h, o - 1], device(to, core)))
    for w in waits:
        w.wait()
    waits = []
    for h, order in plans:
        ss2[h] = (ss1[h, band(h, at[order[1]], 8), :] + sr1[h, 0]) + (sr1[h, 1] + sr1[h, 2])
        for o in (1, 2, 3):
            waits.append(copies.start(ss2.at[h], sr2.at[h, at[order[2]]], device(moved(at, order[2], o), core)))
        sr2[h, at[order[2]]] = ss2[h]
    for w in waits:
        w.wait()
    bases = [core * 128 + at[order[0]] * 32 + at[order[1]] * 8 for _, order in plans]
    for (h, order), base in zip(plans, bases):
        s_ref[h, pl.ds(pl.multiple_of(base, 8), 8), :] = (sr2[h, 0] + sr2[h, 1]) + (sr2[h, 2] + sr2[h, 3])
    for level in (1, 0):
        waits = []
        for (h, order), base in zip(plans, bases):
            if level:
                rows = pl.ds(pl.multiple_of(base, 8), 8)
            else:
                rows = pl.ds(pl.multiple_of(core * 128 + at[order[0]] * 32, 32), 32)
            view = s_ref.at[h, rows, :]
            waits += [copies.start(view, view, device(moved(at, order[level], o), core)) for o in (1, 2, 3)]
        for w in waits:
            w.wait()
    view = s_ref.at[:, near, :]
    copies.start(view, view, partner).wait()


def gram_scratch():
    return [
        pltpu.VMEM((272, 8192), BF16),
        pltpu.VMEM((64, 128), F32),
        pltpu.VMEM((64, 128), F32),
        pltpu.VMEM((8, 128), F32),
        pltpu.VMEM((8, 128), F32),
        pltpu.VMEM((5, 32, 128), F32),
        pltpu.VMEM((3, 3, 32, 128), F32),
        pltpu.VMEM((4, 8, 128), F32),
        pltpu.VMEM((3, 3, 8, 128), F32),
        pltpu.VMEM((64, 16, 128), F32),
        pltpu.VMEM((64, 16, 128), BF16),
        pltpu.VMEM((4, 4, 4, 256, 128), BF16),
        pltpu.VMEM((4, 4, 4, 128, 128), BF16),
        pltpu.VMEM((4, 4, 4, 128, 128), BF16),
        *[pltpu.VMEM((6, 2, 4, size, 128), BF16) for _, size, _ in PARTS],
        *[pltpu.VMEM((2, 2, 4, size, 128), BF16) for _, size, _ in PARTS],
        *[pltpu.VMEM((4, 4, size, 128), F32) for _, size, _ in PARTS],
        *[pltpu.VMEM((6, 2, size, 128), F32) for _, size, _ in PARTS],
        *[pltpu.VMEM((2, 2, size, 128), F32) for _, size, _ in PARTS],
        *[pltpu.VMEM((4, size, 128), F32) for _, size, _ in PARTS],
        *[pltpu.VMEM((3, size, 128), F32) for _, size, _ in PARTS],
        pltpu.VMEM((128, 128), F32),
        pltpu.VMEM((2, 128, 128), F32),
        pltpu.VMEM((2, 3, 32, 128), F32),
        pltpu.VMEM((2, 3, 8, 128), F32),
        pltpu.VMEM((2, 32, 128), F32),
        pltpu.VMEM((2, 4, 8, 128), F32),
        pltpu.VMEM((2, 8, 128), F32),
    ]


def small_inverse(t):
    sub = lax.broadcasted_iota(jnp.int32, (8, 128), 0)
    t = list(t)
    for s in range(4):
        rows = [jnp.broadcast_to(t[s][i : i + 1, :], (8, 128)) for i in range(8)]
        e = [[jnp.broadcast_to(rows[i][:, 8 * s + j : 8 * s + j + 1], (8, 128)) for j in range(i + 1)] for i in range(8)]
        inv, low = [], [[None] * 8 for _ in range(8)]
        for j in range(8):
            inv.append(1.0 / e[j][j])
            for i in range(j + 1, 8):
                low[i][j] = e[i][j] * inv[j]
            for i in range(j + 1, 8):
                for m in range(j + 1, i + 1):
                    e[i][m] = e[i][m] - low[i][j] * e[m][j]
        w = []
        for i in range(8):
            v = rows[i]
            for j in range(i):
                v = v - low[i][j] * w[j]
            w.append(v)
        for b in range(s + 1, 4):
            f = []
            for j in range(8):
                v = jnp.broadcast_to(t[b][:, 8 * s + j : 8 * s + j + 1], (8, 128))
                for k in range(j):
                    v = v - f[k] * e[j][k]
                f.append(v * inv[j])
            for j in range(8):
                t[b] = t[b] - f[j] * w[j]
        out = w[0] * lax.rsqrt(e[0][0])
        for i in range(1, 8):
            out = jnp.where(sub == i, w[i] * lax.rsqrt(e[i][i]), out)
        t[s] = out
    return t


def inverse_factor(s_ref, m_ref):
    r = lax.broadcasted_iota(jnp.int32, (256, 256), 0)
    c = lax.broadcasted_iota(jnp.int32, (256, 256), 1)
    m_ref[:, 0:128] = s_ref[0]
    m_ref[:, 128:256] = s_ref[1]
    m_ref[:, 256:512] = (r == c).astype(F32)
    lane = lax.broadcasted_iota(jnp.int32, (32, 128), 1)
    unit = (lane == lax.broadcasted_iota(jnp.int32, (32, 128), 0) + 32).astype(F32)
    for b in range(8):
        left = 128 * (b // 4)
        rows, window = slice(32 * b, 32 * b + 32), slice(left, left + 384)
        tile = m_ref[rows, left : left + 128]
        if b % 4:
            tile = pltpu.roll(tile, 128 - 32 * (b % 4), 1)
        tile = jnp.where(lane < 32, tile, unit)
        t = small_inverse([tile[8 * i : 8 * i + 8] for i in range(4)])
        inv = jnp.concatenate(t, 0)[:, 32:64]
        w = jnp.dot(inv, m_ref[rows, window], precision=HIGHEST, preferred_element_type=F32)
        if b < 7:
            update = lax.dot_general(
                w[:, : 256 - left], w, (((0,), (0,)), ((), ())), precision=HIGHEST, preferred_element_type=F32
            )
            m_ref[32 * b + 32 :, window] -= update[32 * b + 32 - left :]
        m_ref[rows, window] = w


STEPS = ((0, 0, 0), (3, 0, 0), (0, 0, 3), (0, 1, 0), (2, 0, 0), (0, 3, 3), (3, 0, 1), (1, 1, 0), (0, 2, 3), (0, 0, 2), (2, 0, 1), (0, 2, 0))
PARENTS = ((0, 0, 0), (0, 0, 0), (0, 0, 0), (3, 0, 0), (0, 0, 3), (3, 0, 0), (0, 1, 0), (0, 3, 3), (0, 0, 3), (2, 0, 0), (0, 1, 0))


def difference(a, b):
    return tuple((i - j) % 4 for i, j in zip(a, b))


def panel_plan():
    parent = [None, *[STEPS.index(p) for p in PARENTS]]
    depth = [0] * len(STEPS)
    for s in range(1, len(STEPS)):
        depth[s] = depth[parent[s]] + 1
    best = {}
    for r, row in enumerate(STEPS):
        for c, column in enumerate(STEPS):
            d = difference(row, column)
            cost = (max(depth[r], depth[c]), depth[r] + depth[c], r)
            if d not in best or cost < best[d][0]:
                best[d] = (cost, r, c)
    units = sorted((cost[0], r, c) for cost, r, c in best.values())
    assert len(units) == 64
    return parent, depth, units


def spanning_tree():
    def far(step):
        return sum(min(c, 4 - c) for c in step)

    steps = sorted(itertools.product(range(4), repeat=3), key=lambda step: (far(step), step))
    load = {(a, o): 0 for a in range(3) for o in (1, 3)}
    parent = [None]
    for step in steps[1:]:
        choices = []
        for (a, o), used in load.items():
            before = moved(step, a, 4 - o)
            if far(before) == far(step) - 1:
                choices.append((used, a, o, steps.index(before)))
        _, a, o, before = min(choices)
        load[a, o] += 1
        parent.append(before)
    return steps, parent, [far(step) for step in steps]


def project_part(
    n_total, at, core, copies, width_ref, label_ref, x_ref, g_ref, s_ref, mean_ref, n_ref_ref,
    basis_out, proj_ref, out_ref, basis_sem,
    basis_ref, m_ref, p_acc, blocks, columns, rows_ref, acc, got,
):
    other = 1 - core
    partner = device(at, other)
    parent, depth, units = panel_plan()

    def moved_by(step):
        return tuple((c + i) % 4 for c, i in zip(at, step))

    def toward(step):
        return device(moved_by(step), core)

    inverse_factor(s_ref, m_ref)
    block = lax.dot_general(
        g_ref[...], m_ref[:, 256:512], (((0,), (1,)), ((), ())), precision=HIGHEST, preferred_element_type=F32
    ).astype(BF16)
    basis_ref[(at[0] * 4 + at[1]) * 4 + at[2]] = block

    steps, source, level_of = spanning_tree()
    half = pl.ds(pl.multiple_of(core * 64, 64), 64)

    def chip(s):
        x, y, z = moved_by(steps[s])
        return (x * 4 + y) * 4 + z

    links, across = {}, {}
    p_acc[...] = jnp.zeros_like(p_acc)

    def add_level(level):
        total = p_acc[...]
        for s in range(64):
            if level_of[s] == level:
                if s:
                    across[s].wait()
                b = chip(s)
                lanes = pl.ds(pl.multiple_of(b * 128, 128), 128)
                centred = (x_ref[:, lanes].astype(F32) - mean_ref[pl.ds(b, 1), :]).astype(BF16)
                total += jnp.dot(centred, basis_ref[b], preferred_element_type=F32)
        p_acc[...] = total

    for level in range(7):
        for s in range(64):
            if level_of[s] != level:
                continue
            if s:
                links[s].wait()
            view = basis_ref.at[chip(s), half, :]
            for child in range(1, 64):
                if source[child] == s:
                    links[child] = copies.start(view, view, toward(difference(steps[s], steps[child])))
            if s:
                across[s] = copies.start(view, view, partner)
        if level:
            add_level(level - 1)
    add_level(6)
    basis_copy = pltpu.make_async_copy(basis_ref, basis_out, basis_sem)
    basis_copy.start()
    p = p_acc[...].astype(BF16)
    proj_ref[...] = p
    wide = p.astype(F32)
    norm = jnp.broadcast_to(jnp.sum(wide * wide, 1, keepdims=True) * -0.5, (256, 128)).T
    norm = jnp.concatenate([norm[:128, :128], norm[:128, 128:]], 1)[0:1]
    high = norm.astype(BF16).astype(F32)
    middle = (norm - high).astype(BF16).astype(F32)
    low = (norm - high) - middle
    is_ref = (label_ref[...] == 0).astype(F32)
    ids = lax.broadcasted_iota(jnp.int32, (16, 256), 0)
    tail = jnp.where(ids == 0, is_ref, jnp.where(ids == 1, high, jnp.where(ids == 2, middle, jnp.where(ids == 3, low, 0.0))))
    blocks[0, core, 0:256, :] = p
    blocks[0, core, 256:272, :] = tail.astype(BF16)

    edges, cores = {}, {}

    def hand_on(s):
        view = blocks.at[s, core]
        for child in range(1, len(STEPS)):
            if parent[child] == s:
                target = toward(difference(STEPS[s], STEPS[child]))
                edges[child] = copies.start(view, blocks.at[child, core], target)
        cores[s] = copies.start(view, view, partner)

    scale = 1.4426950408889634 / (128.0 * jnp.exp2(jnp.full((1, 256), width_ref[0], jnp.int32).astype(F32)))
    ids = lax.broadcasted_iota(jnp.int32, (16, 256), 0)
    lanes = lax.broadcasted_iota(jnp.int32, (16, 256), 1)
    select = jnp.where(lanes < 128, jnp.where((ids > 0) & (ids < 4), 1.0, 0.0), jnp.where(ids == 0, 1.0, 0.0)).astype(BF16)

    def prepare(s):
        for k in range(2):
            ends = blocks[s, k, 256:272, :].astype(F32).T.astype(BF16)
            columns[s, k] = jnp.dot(ends, select, preferred_element_type=F32)
        ends = blocks[s, core, 256:272, :].astype(F32)
        rows_ref[s] = jnp.broadcast_to((ends[1:2] + ends[2:3]) + ends[3:4], (8, 256))

    for s in range(len(STEPS)):
        acc[s, 0] = jnp.zeros((8, 256), F32)
        acc[s, 1] = jnp.zeros((8, 256), F32)
    hand_on(0)
    for level in range(max(depth) + 1):
        here = [s for s in range(len(STEPS)) if depth[s] == level]
        for s in here:
            if s:
                edges[s].wait()
                hand_on(s)
        for s in here:
            cores[s].wait()
            prepare(s)
        for _, r, c in [u for u in units if u[0] == level]:
            row_norm = rows_ref[r][0:1]
            rows = blocks[r, core, 0:256, :]
            total, refs = acc[r, 0], acc[r, 1]
            for k in range(2):
                inner = lax.dot_general(
                    blocks[c, k, 0:256, :], rows, (((1,), (1,)), ((), ())), preferred_element_type=F32
                )
                norm, mark = columns[c, k, :, :128], columns[c, k, :, 128:]
                norm, mark = jnp.concatenate([norm, norm], 1), jnp.concatenate([mark, mark], 1)
                value = jnp.exp2(((inner + norm) + row_norm) * scale)
                total += jnp.sum(value.reshape(32, 8, 256), 0)
                refs += jnp.sum((value * mark).reshape(32, 8, 256), 0)
            acc[r, 0], acc[r, 1] = total, refs

    for level in range(max(depth), 0, -1):
        here = [s for s in range(1, len(STEPS)) if depth[s] == level]
        waits = [copies.start(acc.at[s], got.at[s], toward(difference(STEPS[s], STEPS[parent[s]]))) for s in here]
        for s, w in zip(here, waits):
            w.wait()
            acc[parent[s]] += got[s]
    row_sums = jnp.sum(acc[0, 0], 0, keepdims=True)
    ref_sums = jnp.sum(acc[0, 1], 0, keepdims=True)
    n_ref = n_ref_ref[0:1, 0:1]
    n_cur = n_total - n_ref
    proof = (ref_sums / n_ref - (row_sums - ref_sums) / n_cur) / (row_sums / n_total)
    out_ref[...] = jnp.broadcast_to(proof, (8, 256))
    basis_copy.wait()


def project_scratch():
    count = len(STEPS)
    return [
        pltpu.VMEM((64, 128, 256), BF16),
        pltpu.VMEM((256, 512), F32),
        pltpu.VMEM((256, 256), F32),
        pltpu.VMEM((count, 2, 272, 256), BF16),
        pltpu.VMEM((count, 2, 256, 256), F32),
        pltpu.VMEM((count, 8, 256), F32),
        pltpu.VMEM((count, 2, 8, 256), F32),
        pltpu.VMEM((count, 2, 8, 256), F32),
    ]


def drift_kernel(
    n_total, n_gram, width_ref, x_hbm, b_hbm, label_ref, basis_out, proj_ref, out_ref,
    x_ref, b_ref, g_ref, s_ref, mean_ref, count_ref, load_sem, send, recv, *scratch,
):
    chunks = 4
    lanes = x_ref.shape[1] // chunks
    loads = []
    for i in range(chunks):
        part = slice(i * lanes, (i + 1) * lanes)
        loads.append(pltpu.make_async_copy(x_hbm.at[:, part], x_ref.at[:, part], load_sem.at[i]))
    b_load = pltpu.make_async_copy(b_hbm, b_ref, load_sem.at[chunks])
    for load in (*loads, b_load):
        load.start()
    at, core = place()
    copies = Copies(send, recv)
    greet([device(at, 1 - core), *axis_peers(at, core)])
    gram_part(
        n_total, at, core, copies, loads, b_load, x_ref, b_ref, label_ref, g_ref, s_ref, mean_ref, count_ref,
        *scratch[:n_gram],
    )
    project_part(
        n_total, at, core, copies, width_ref, label_ref, x_ref, g_ref, s_ref, mean_ref, count_ref,
        basis_out, proj_ref, out_ref, load_sem.at[chunks + 1],
        *scratch[n_gram:],
    )


def hand_out_kernel(basis, projected, proof, basis_out, projected_out, proof_out):
    basis_out[...] = basis[...]

    @pl.when(pl.program_id(0) == 0)
    def _():
        projected_out[...] = projected[...]
        proof_out[...] = proof[0:1, :]


def hand_out(basis, projected, proof):
    tiles = 8
    tile = pl.BlockSpec((basis.shape[0] // tiles, basis.shape[1]), lambda i: (i, 0))
    whole = [pl.BlockSpec(a.shape, lambda i: (0, 0)) for a in (projected, proof)]
    basis, projected, proof = pl.pallas_call(
        hand_out_kernel,
        grid=(tiles,),
        out_shape=(
            jax.ShapeDtypeStruct(basis.shape, basis.dtype),
            jax.ShapeDtypeStruct(projected.shape, projected.dtype),
            jax.ShapeDtypeStruct((1, 256), F32),
        ),
        in_specs=[tile, *whole],
        out_specs=(tile, whole[0], pl.BlockSpec((1, 256), lambda i: (0, 0))),
        name="hand_out",
    )(basis, projected, proof)
    return projected, proof.reshape(256), basis


def local(n_total, samples, labels, basis_start, width_index):
    gram, project = gram_scratch(), project_scratch()
    n_copies = 102 + 126 + 3 * len(STEPS) - 2
    basis, projected, proof = pl.pallas_call(
        functools.partial(drift_kernel, n_total, len(gram)),
        out_shape=(
            jax.ShapeDtypeStruct((64, 128, 256), BF16),
            jax.ShapeDtypeStruct((256, 256), BF16),
            jax.ShapeDtypeStruct((8, 256), F32),
        ),
        in_specs=[
            pl.BlockSpec(memory_space=pltpu.SMEM),
            pl.BlockSpec(memory_space=pl.ANY),
            pl.BlockSpec(memory_space=pl.ANY),
            VMEM,
        ],
        out_specs=(pl.BlockSpec(memory_space=pl.ANY), VMEM, VMEM),
        scratch_shapes=[
            pltpu.VMEM((256, 8192), BF16),
            pltpu.VMEM((8192, 256), BF16),
            pltpu.VMEM((256, 128), F32),
            pltpu.VMEM((2, 256, 128), F32),
            pltpu.VMEM((64, 128), F32),
            pltpu.VMEM((8, 128), F32),
            pltpu.SemaphoreType.DMA((6,)),
            pltpu.SemaphoreType.DMA((n_copies,)),
            pltpu.SemaphoreType.DMA((n_copies,)),
            *gram,
            *project,
        ],
        compiler_params=pltpu.CompilerParams(collective_id=0, has_side_effects=True, vmem_limit_bytes=LIMIT),
        name="drift",
    )(width_index.reshape(1), samples, basis_start, labels.reshape(1, 256))
    return hand_out(basis.reshape(8192, 256), projected, proof)


def solution(mesh):
    n_total = float(256 * mesh.size)
    placed = (P(("row", "col"), None), P(("row", "col")), P(), P())
    return jax.shard_map(
        functools.partial(local, n_total),
        mesh=mesh,
        in_specs=placed,
        out_specs=(P(("row", "col"), None), P(("row", "col")), P()),
        check_vma=False,
    )
```

```python
import functools
import itertools

import jax
import jax.numpy as jnp
from jax import lax
from jax.experimental import pallas as pl
from jax.experimental.pallas import tpu as pltpu
from jax.sharding import PartitionSpec as P

MESH = pl.DeviceIdType.MESH
F32 = jnp.float32
BF16 = jnp.bfloat16
VMEM = pl.BlockSpec(memory_space=pltpu.VMEM)
HIGHEST = lax.Precision.HIGHEST
LIMIT = 48 * 1024 * 1024

PARTS = ((0, 48, (0, 1, 2)), (48, 48, (1, 2, 0)), (96, 32, (2, 0, 1)))


def place():
    row, col = lax.axis_index("row"), lax.axis_index("col")
    y, z_lo, core = row // 4, (row // 2) % 2, row % 2
    z_hi, x = col // 4, col % 4
    return (x, y, z_hi * 2 + z_lo), core


def device(at, core):
    x, y, z = at
    return (y * 4 + (z % 2) * 2 + core, (z // 2) * 4 + x)


def moved(at, axis, offset):
    return tuple((c + offset) % 4 if a == axis else c for a, c in enumerate(at))


class Copies:
    def __init__(self, send, recv):
        self.send, self.recv, self.used = send, recv, 0

    def start(self, src, dst, target):
        n = self.used
        self.used += 1
        copy = pltpu.make_async_remote_copy(
            src_ref=src,
            dst_ref=dst,
            send_sem=self.send.at[n],
            recv_sem=self.recv.at[n],
            device_id=target,
            device_id_type=MESH,
        )
        copy.start()
        return copy


def greet(peers):
    barrier = pltpu.get_barrier_semaphore()
    for peer in peers:
        pl.semaphore_signal(barrier, inc=1, device_id=peer, device_id_type=MESH)
    pl.semaphore_wait(barrier, len(peers))


def axis_peers(at, core):
    return [device(moved(at, a, o), core) for a in range(3) for o in (1, 2, 3)]


def pick(axes, at, rows=None):
    index = tuple(at[a] if a in axes else slice(None) for a in range(3))
    return index if rows is None else (*index, rows)


def gram_part(
    n_total, at, core, copies, gathering, gram_all, x_loads, b_load, x_ref, b_ref, label_ref, g_ref, s_ref, mean_ref, count_ref,
    c_ref, local_ref, theirs_ref, note, note_recv, mhalf, mrecv, notes, nrecv, delta_ref, daug, gt, half, recv0,
    q1a, q1b, q1c, o1a, o1b, o1c, t1a, t1b, t1c, q2a, q2b, q2c, o2a, o2b, o2c, t2a, t2b, t2c, r3a, r3b, r3c,
    gme, s_half, sr0, sr1, ss1, sr2, ss2,
):
    other = 1 - core
    partner = device(at, other)
    n_local, width = x_ref.shape
    step = 512
    turns = width // step // len(x_loads)

    for chunk, load in enumerate(x_loads):
        load.wait()

        @pl.loop(chunk * turns, (chunk + 1) * turns)
        def _(j):
            lanes = pl.ds(pl.multiple_of(j * step, step), step)
            m = jnp.sum(x_ref[:, lanes].astype(F32), 0, keepdims=True) * (1.0 / n_local)
            for i in range(step // 128):
                local_ref[pl.ds(step // 128 * j + i, 1), :] = m[:, i * 128 : (i + 1) * 128]

    copy = copies.start(local_ref, theirs_ref, partner)
    ids = lax.broadcasted_iota(jnp.int32, (16, step), 0)

    @pl.loop(0, width // step)
    def _(j):
        lanes = pl.ds(pl.multiple_of(j * step, step), step)
        m = jnp.concatenate([local_ref[pl.ds(step // 128 * j + i, 1), :] for i in range(step // 128)], 1)
        c_ref[0:n_local, lanes] = (x_ref[:, lanes].astype(F32) - m).astype(BF16)
        high = m.astype(BF16).astype(F32)
        middle = (m - high).astype(BF16).astype(F32)
        low = (m - high) - middle
        tile = jnp.where(ids == 0, high, jnp.where(ids == 1, middle, jnp.where(ids == 2, low, 0.0)))
        c_ref[n_local : n_local + 16, lanes] = tile.astype(BF16)

    def start_axis(values, landing, a):
        return [copies.start(values.at[a], landing.at[a, o - 1], device(moved(at, a, o), core)) for o in (1, 2, 3)]

    def end_axis(values, landing, a, waits):
        for w in waits:
            w.wait()
        values[a + 1] = values[a] + landing[a, 0] + landing[a, 1] + landing[a, 2]

    mine = pl.ds(pl.multiple_of(core * 32, 32), 32)
    copy.wait()
    mhalf[0] = local_ref[mine, :] + theirs_ref[mine, :]
    mean_waits = start_axis(mhalf, mrecv, 0)
    b_load.wait()

    first = jnp.dot(c_ref[...], b_ref[...], preferred_element_type=F32)
    t_local = (first[n_local : n_local + 1] + first[n_local + 1 : n_local + 2]) + first[n_local + 2 : n_local + 3]
    is_ref = (label_ref[...] == 0).astype(F32)
    ids = lax.broadcasted_iota(jnp.int32, (8, 128), 0)
    count = jnp.sum(is_ref, 1, keepdims=True)
    note[...] = jnp.where(ids == 0, count, jnp.where(ids == 1, t_local[:, :128], jnp.where(ids == 2, t_local[:, 128:], 0.0)))
    copy_note = copies.start(note, note_recv, partner)
    first_t = first[:n_local].T.astype(BF16)
    far = pl.ds(pl.multiple_of(other * 128, 128), 128)
    near = pl.ds(pl.multiple_of(core * 128, 128), 128)
    halves = []

    def gram_blocks(bx):
        @pl.loop(0, 4)
        def _(by):
            lanes = pl.ds(pl.multiple_of((bx * 4 + by) * 512, 512), 512)
            block = jnp.dot(first_t, c_ref[0:n_local, lanes], preferred_element_type=F32).astype(BF16)
            for bz in range(4):
                gt[bx, by, bz] = block[:, bz * 128 : (bz + 1) * 128]

        halves.append(copies.start(gt.at[bx, :, :, far, :], recv0.at[bx], partner))

    end_axis(mhalf, mrecv, 0, mean_waits)
    mean_waits = start_axis(mhalf, mrecv, 1)
    copy_note.wait()
    notes[0] = note[...] + note_recv[...]
    note_waits = start_axis(notes, nrecv, 0)
    gram_blocks(0)
    end_axis(mhalf, mrecv, 1, mean_waits)
    mean_waits = start_axis(mhalf, mrecv, 2)
    end_axis(notes, nrecv, 0, note_waits)
    note_waits = start_axis(notes, nrecv, 1)
    gram_blocks(1)
    end_axis(mhalf, mrecv, 2, mean_waits)
    mhalf[4] = mhalf[3] * (1.0 / 128.0)
    mean_ref[mine, :] = mhalf[4]
    copy = copies.start(mhalf.at[4], mean_ref.at[mine], partner)
    end_axis(notes, nrecv, 1, note_waits)
    note_waits = start_axis(notes, nrecv, 2)
    gram_blocks(2)
    gram_blocks(3)
    end_axis(notes, nrecv, 2, note_waits)
    totals = notes[3]
    count_ref[...] = totals

    mean_t = totals * (1.0 / 128.0)
    ids = lax.broadcasted_iota(jnp.int32, (16, 256), 0)
    taug = jnp.zeros((16, 256), F32)
    for k, tile in enumerate((note[...], note_recv[...])):
        tau = (tile - mean_t) * float(n_local)
        tau = jnp.concatenate([tau[1:2], tau[2:3]], 1)
        high = tau.astype(BF16).astype(F32)
        taug = jnp.where((ids == 3 * k) | (ids == 3 * k + 1), high, jnp.where(ids == 3 * k + 2, tau - high, taug))
    taug_t = taug.T
    taug_t = jnp.where(core == 0, taug_t[:128], taug_t[128:]).astype(BF16)
    copy.wait()
    delta_ref[...] = jnp.zeros_like(delta_ref)
    for k, source in enumerate((local_ref, theirs_ref)):
        delta = source[...] - mean_ref[...]
        high = delta.astype(BF16).astype(F32)
        delta_ref[:, 3 * k, :] = high
        delta_ref[:, 3 * k + 1, :] = delta - high
        delta_ref[:, 3 * k + 2, :] = high
    daug[...] = delta_ref[...].astype(BF16)

    for bx in range(4):
        halves[bx].wait()

        @pl.loop(0, 4)
        def _(by):
            for bz in range(4):
                extra = jnp.dot(taug_t, daug[(bx * 4 + by) * 4 + bz], preferred_element_type=F32)
                both = gt[bx, by, bz, near, :].astype(F32) + recv0[bx, by, bz].astype(F32)
                half[bx, by, bz] = (both + extra).astype(BF16)

    def exchange(parts, dtype, source, incoming, outgoing, result):
        todo = []
        for i, (axis, size) in enumerate(parts):
            up, down = device(moved(at, axis, 1), core), device(moved(at, axis, 3), core)
            chunks = [source(i, (at[axis] + o) % 4) for o in range(4)]
            low, high = pl.ds(0, 2), pl.ds(2, 2)
            box = incoming[i]
            first_up = copies.start(chunks[2].at[low], box.at[0], up)
            first_down = copies.start(chunks[2].at[high], box.at[1], down)
            near_up = copies.start(chunks[1].at[high], box.at[2], up)
            near_down = copies.start(chunks[3].at[low], box.at[3], down)
            todo.append((up, down, chunks, first_up, first_down, near_up, near_down))
        last = []
        for i, (up, down, chunks, first_up, first_down, _, _) in enumerate(todo):
            box, out = incoming[i], outgoing[i]
            first_up.wait()
            out[0] = chunks[1][0:2] + box[0]
            add_up = copies.start(out.at[0], box.at[4], up)
            first_down.wait()
            out[1] = chunks[3][2:4] + box[1]
            add_down = copies.start(out.at[1], box.at[5], down)
            last.append((add_up, add_down))
        for i, (_, _, chunks, _, _, near_up, near_down) in enumerate(todo):
            box = incoming[i]
            near_up.wait()
            near_down.wait()
            for w in last[i]:
                w.wait()
            own = chunks[0]
            result[i][0:2] = (own[0:2].astype(F32) + box[3].astype(F32)) + box[4].astype(F32)
            result[i][2:4] = (own[2:4].astype(F32) + box[2].astype(F32)) + box[5].astype(F32)

    orders = [order for _, _, order in PARTS]
    t1s, t2s = (t1a, t1b, t1c), (t2a, t2b, t2c)

    def stage_one(i, k):
        start, size, order = PARTS[i]
        to = tuple(k for _ in range(3))
        return half.at[pick(order[:1], to, slice(start, start + size))]

    def stage_two(i, k):
        _, _, order = PARTS[i]
        left = [a for a in range(3) if a != order[0]]
        return t1s[i].at[k] if left[0] == order[1] else t1s[i].at[:, k]

    exchange([(o[0], 0) for o in orders], BF16, stage_one, (q1a, q1b, q1c), (o1a, o1b, o1c), t1s)
    exchange([(o[1], 0) for o in orders], F32, stage_two, (q2a, q2b, q2c), (o2a, o2b, o2c), t2s)
    waits = []
    for (start, size, order), t2, r3 in zip(PARTS, t2s, (r3a, r3b, r3c)):
        for o in (1, 2, 3):
            to = moved(at, order[2], o)
            waits.append(copies.start(t2.at[to[order[2]]], r3.at[o - 1], device(to, core)))
    for w in waits:
        w.wait()
    for (start, size, order), t2, r3 in zip(PARTS, t2s, (r3a, r3b, r3c)):
        total = (t2[at[order[2]]] + r3[0]) + (r3[1] + r3[2])
        gme[start : start + size, :] = total * (1.0 / n_total)
    g_ref[near, :] = gme[...]
    copies.start(gme, g_ref.at[near], partner).wait()
    gram_all[chip_number(at)] = g_ref[...].T
    next(gathering)

    square = lax.dot_general(
        gme[...], g_ref[...], (((1,), (1,)), ((), ())), precision=HIGHEST, preferred_element_type=F32
    )
    s_half[0] = square[:, :128]
    s_half[1] = square[:, 128:]
    plans = ((0, (0, 1, 2)), (1, (1, 2, 0)))

    def band(h, position, size):
        return pl.ds(pl.multiple_of(position * size, size), size)

    waits = []
    for h, order in plans:
        for o in (1, 2, 3):
            to = moved(at, order[0], o)
            waits.append(
                copies.start(s_half.at[h, band(h, to[order[0]], 32), :], sr0.at[h, o - 1], device(to, core))
            )
    for w in waits:
        w.wait()
    waits = []
    for h, order in plans:
        ss1[h] = (s_half[h, band(h, at[order[0]], 32), :] + sr0[h, 0]) + (sr0[h, 1] + sr0[h, 2])
        for o in (1, 2, 3):
            to = moved(at, order[1], o)
            waits.append(copies.start(ss1.at[h, band(h, to[order[1]], 8), :], sr1.at[h, o - 1], device(to, core)))
    for w in waits:
        w.wait()
    waits = []
    for h, order in plans:
        ss2[h] = (ss1[h, band(h, at[order[1]], 8), :] + sr1[h, 0]) + (sr1[h, 1] + sr1[h, 2])
        for o in (1, 2, 3):
            waits.append(copies.start(ss2.at[h], sr2.at[h, at[order[2]]], device(moved(at, order[2], o), core)))
        sr2[h, at[order[2]]] = ss2[h]
    next(gathering)
    for w in waits:
        w.wait()
    bases = [core * 128 + at[order[0]] * 32 + at[order[1]] * 8 for _, order in plans]
    for (h, order), base in zip(plans, bases):
        s_ref[h, pl.ds(pl.multiple_of(base, 8), 8), :] = (sr2[h, 0] + sr2[h, 1]) + (sr2[h, 2] + sr2[h, 3])
    for level in (1, 0):
        waits = []
        for (h, order), base in zip(plans, bases):
            if level:
                rows = pl.ds(pl.multiple_of(base, 8), 8)
            else:
                rows = pl.ds(pl.multiple_of(core * 128 + at[order[0]] * 32, 32), 32)
            view = s_ref.at[h, rows, :]
            waits += [copies.start(view, view, device(moved(at, order[level], o), core)) for o in (1, 2, 3)]
        for w in waits:
            w.wait()
    view = s_ref.at[:, near, :]
    copy = copies.start(view, view, partner)
    next(gathering)
    copy.wait()


def gram_scratch():
    return [
        pltpu.VMEM((272, 8192), BF16),
        pltpu.VMEM((64, 128), F32),
        pltpu.VMEM((64, 128), F32),
        pltpu.VMEM((8, 128), F32),
        pltpu.VMEM((8, 128), F32),
        pltpu.VMEM((5, 32, 128), F32),
        pltpu.VMEM((3, 3, 32, 128), F32),
        pltpu.VMEM((4, 8, 128), F32),
        pltpu.VMEM((3, 3, 8, 128), F32),
        pltpu.VMEM((64, 16, 128), F32),
        pltpu.VMEM((64, 16, 128), BF16),
        pltpu.VMEM((4, 4, 4, 256, 128), BF16),
        pltpu.VMEM((4, 4, 4, 128, 128), BF16),
        pltpu.VMEM((4, 4, 4, 128, 128), BF16),
        *[pltpu.VMEM((6, 2, 4, size, 128), BF16) for _, size, _ in PARTS],
        *[pltpu.VMEM((2, 2, 4, size, 128), BF16) for _, size, _ in PARTS],
        *[pltpu.VMEM((4, 4, size, 128), F32) for _, size, _ in PARTS],
        *[pltpu.VMEM((6, 2, size, 128), F32) for _, size, _ in PARTS],
        *[pltpu.VMEM((2, 2, size, 128), F32) for _, size, _ in PARTS],
        *[pltpu.VMEM((4, size, 128), F32) for _, size, _ in PARTS],
        *[pltpu.VMEM((3, size, 128), F32) for _, size, _ in PARTS],
        pltpu.VMEM((128, 128), F32),
        pltpu.VMEM((2, 128, 128), F32),
        pltpu.VMEM((2, 3, 32, 128), F32),
        pltpu.VMEM((2, 3, 8, 128), F32),
        pltpu.VMEM((2, 32, 128), F32),
        pltpu.VMEM((2, 4, 8, 128), F32),
        pltpu.VMEM((2, 8, 128), F32),
    ]


def small_inverse(t):
    sub = lax.broadcasted_iota(jnp.int32, (8, 128), 0)
    t = list(t)
    for s in range(4):
        rows = [jnp.broadcast_to(t[s][i : i + 1, :], (8, 128)) for i in range(8)]
        e = [[jnp.broadcast_to(rows[i][:, 8 * s + j : 8 * s + j + 1], (8, 128)) for j in range(i + 1)] for i in range(8)]
        inv, low = [], [[None] * 8 for _ in range(8)]
        for j in range(8):
            inv.append(1.0 / e[j][j])
            for i in range(j + 1, 8):
                low[i][j] = e[i][j] * inv[j]
            for i in range(j + 1, 8):
                for m in range(j + 1, i + 1):
                    e[i][m] = e[i][m] - low[i][j] * e[m][j]
        w = []
        for i in range(8):
            v = rows[i]
            for j in range(i):
                v = v - low[i][j] * w[j]
            w.append(v)
        for b in range(s + 1, 4):
            f = []
            for j in range(8):
                v = jnp.broadcast_to(t[b][:, 8 * s + j : 8 * s + j + 1], (8, 128))
                for k in range(j):
                    v = v - f[k] * e[j][k]
                f.append(v * inv[j])
            for j in range(8):
                t[b] = t[b] - f[j] * w[j]
        out = w[0] * lax.rsqrt(e[0][0])
        for i in range(1, 8):
            out = jnp.where(sub == i, w[i] * lax.rsqrt(e[i][i]), out)
        t[s] = out
    return t


def inverse_factor(s_ref, m_ref, gathering):
    r = lax.broadcasted_iota(jnp.int32, (256, 256), 0)
    c = lax.broadcasted_iota(jnp.int32, (256, 256), 1)
    m_ref[:, 0:128] = s_ref[0]
    m_ref[:, 128:256] = s_ref[1]
    m_ref[:, 256:512] = (r == c).astype(F32)
    lane = lax.broadcasted_iota(jnp.int32, (32, 128), 1)
    unit = (lane == lax.broadcasted_iota(jnp.int32, (32, 128), 0) + 32).astype(F32)
    for b in range(8):
        left = 128 * (b // 4)
        rows, window = slice(32 * b, 32 * b + 32), slice(left, left + 384)
        tile = m_ref[rows, left : left + 128]
        if b % 4:
            tile = pltpu.roll(tile, 128 - 32 * (b % 4), 1)
        tile = jnp.where(lane < 32, tile, unit)
        t = small_inverse([tile[8 * i : 8 * i + 8] for i in range(4)])
        inv = jnp.concatenate(t, 0)[:, 32:64]
        w = jnp.dot(inv, m_ref[rows, window], precision=HIGHEST, preferred_element_type=F32)
        if b < 7:
            update = lax.dot_general(
                w[:, : 256 - left], w, (((0,), (0,)), ((), ())), precision=HIGHEST, preferred_element_type=F32
            )
            m_ref[32 * b + 32 :, window] -= update[32 * b + 32 - left :]
        m_ref[rows, window] = w
        if b in (2, 5, 7):
            next(gathering)


STEPS = ((0, 0, 0), (3, 0, 0), (0, 0, 3), (0, 1, 0), (2, 0, 0), (0, 3, 3), (3, 0, 1), (1, 1, 0), (0, 2, 3), (0, 0, 2), (2, 0, 1), (0, 2, 0))
PARENTS = ((0, 0, 0), (0, 0, 0), (0, 0, 0), (3, 0, 0), (0, 0, 3), (3, 0, 0), (0, 1, 0), (0, 3, 3), (0, 0, 3), (2, 0, 0), (0, 1, 0))


def difference(a, b):
    return tuple((i - j) % 4 for i, j in zip(a, b))


def panel_plan():
    parent = [None, *[STEPS.index(p) for p in PARENTS]]
    depth = [0] * len(STEPS)
    for s in range(1, len(STEPS)):
        depth[s] = depth[parent[s]] + 1
    best = {}
    for r, row in enumerate(STEPS):
        for c, column in enumerate(STEPS):
            d = difference(row, column)
            cost = (max(depth[r], depth[c]), depth[r] + depth[c], r)
            if d not in best or cost < best[d][0]:
                best[d] = (cost, r, c)
    units = sorted((cost[0], r, c) for cost, r, c in best.values())
    assert len(units) == 64
    return parent, depth, units


def spanning_tree():
    def far(step):
        return sum(min(c, 4 - c) for c in step)

    steps = sorted(itertools.product(range(4), repeat=3), key=lambda step: (far(step), step))
    load = {(a, o): 0 for a in range(3) for o in (1, 3)}
    parent = [None]
    for step in steps[1:]:
        choices = []
        for (a, o), used in load.items():
            before = moved(step, a, 4 - o)
            if far(before) == far(step) - 1:
                choices.append((used, a, o, steps.index(before)))
        _, a, o, before = min(choices)
        load[a, o] += 1
        parent.append(before)
    return steps, parent, [far(step) for step in steps]


def chip_number(at):
    return (at[0] * 4 + at[1]) * 4 + at[2]


def gather(at, core, copies, ref):
    steps, source, level_of = spanning_tree()
    partner = device(at, 1 - core)
    half = pl.ds(pl.multiple_of(core * 64, 64), 64)

    def moved_by(step):
        return tuple((c + i) % 4 for c, i in zip(at, step))

    links, across = {}, {}
    for level in range(7):
        for s in range(64):
            if level_of[s] != level:
                continue
            if s:
                links[s].wait()
            view = ref.at[chip_number(moved_by(steps[s])), half, :]
            for child in range(1, 64):
                if source[child] == s:
                    target = device(moved_by(difference(steps[s], steps[child])), core)
                    links[child] = copies.start(view, view, target)
            if s:
                across[s] = copies.start(view, view, partner)
        yield
    for s in range(1, 64):
        across[s].wait()
    yield


def project_part(
    n_total, at, core, copies, gathering, gram_all, basis_ref, width_ref, label_ref, x_ref, s_ref, mean_ref, n_ref_ref,
    basis_out, proj_ref, out_ref, basis_sem,
    m_ref, inv_high, inv_low, p_acc, blocks, columns, rows_ref, acc, got,
):
    other = 1 - core
    partner = device(at, other)
    parent, depth, units = panel_plan()

    def toward(step):
        return device(tuple((c + i) % 4 for c, i in zip(at, step)), core)

    inverse_factor(s_ref, m_ref, gathering)
    for _ in gathering:
        pass
    inverse_t = m_ref[:, 256:512].T
    high = inverse_t.astype(BF16)
    inv_high[...] = high
    inv_low[...] = (inverse_t - high.astype(F32)).astype(BF16)
    p_acc[...] = jnp.zeros_like(p_acc)

    @pl.loop(0, 16)
    def _(j):
        chips = pl.ds(4 * j, 4)
        gram = gram_all[chips].reshape(512, 256)
        high = gram.astype(BF16)
        low = (gram - high.astype(F32)).astype(BF16)
        block = jnp.dot(low, inv_high[...], preferred_element_type=F32)
        block += jnp.dot(high, inv_low[...], preferred_element_type=F32)
        block += jnp.dot(high, inv_high[...], preferred_element_type=F32)
        block = block.astype(BF16)
        lanes = pl.ds(pl.multiple_of(j * 512, 512), 512)
        basis_ref[lanes, :] = block
        mean = jnp.concatenate([mean_ref[pl.ds(4 * j + i, 1), :] for i in range(4)], 1)
        centred = (x_ref[:, lanes].astype(F32) - mean).astype(BF16)
        p_acc[...] += jnp.dot(centred, block, preferred_element_type=F32)

    basis_copy = pltpu.make_async_copy(basis_ref, basis_out, basis_sem)
    basis_copy.start()
    p = p_acc[...].astype(BF16)
    proj_ref[...] = p
    wide = p.astype(F32)
    norm = jnp.broadcast_to(jnp.sum(wide * wide, 1, keepdims=True) * -0.5, (256, 128)).T
    norm = jnp.concatenate([norm[:128, :128], norm[:128, 128:]], 1)[0:1]
    high = norm.astype(BF16).astype(F32)
    middle = (norm - high).astype(BF16).astype(F32)
    low = (norm - high) - middle
    is_ref = (label_ref[...] == 0).astype(F32)
    ids = lax.broadcasted_iota(jnp.int32, (16, 256), 0)
    tail = jnp.where(ids == 0, is_ref, jnp.where(ids == 1, high, jnp.where(ids == 2, middle, jnp.where(ids == 3, low, 0.0))))
    blocks[0, core, 0:256, :] = p
    blocks[0, core, 256:272, :] = tail.astype(BF16)

    edges, cores = {}, {}

    def hand_on(s):
        view = blocks.at[s, core]
        for child in range(1, len(STEPS)):
            if parent[child] == s:
                target = toward(difference(STEPS[s], STEPS[child]))
                edges[child] = copies.start(view, blocks.at[child, core], target)
        cores[s] = copies.start(view, view, partner)

    scale = 1.4426950408889634 / (128.0 * jnp.exp2(jnp.full((1, 256), width_ref[0], jnp.int32).astype(F32)))
    ids = lax.broadcasted_iota(jnp.int32, (16, 256), 0)
    lanes = lax.broadcasted_iota(jnp.int32, (16, 256), 1)
    select = jnp.where(lanes < 128, jnp.where((ids > 0) & (ids < 4), 1.0, 0.0), jnp.where(ids == 0, 1.0, 0.0)).astype(BF16)

    def prepare(s):
        for k in range(2):
            ends = blocks[s, k, 256:272, :].astype(F32).T.astype(BF16)
            columns[s, k] = jnp.dot(ends, select, preferred_element_type=F32)
        ends = blocks[s, core, 256:272, :].astype(F32)
        rows_ref[s] = jnp.broadcast_to((ends[1:2] + ends[2:3]) + ends[3:4], (8, 256))

    for s in range(len(STEPS)):
        acc[s, 0] = jnp.zeros((8, 256), F32)
        acc[s, 1] = jnp.zeros((8, 256), F32)
    hand_on(0)
    for level in range(max(depth) + 1):
        here = [s for s in range(len(STEPS)) if depth[s] == level]
        for s in here:
            if s:
                edges[s].wait()
                hand_on(s)
        for s in here:
            cores[s].wait()
            prepare(s)
        for _, r, c in [u for u in units if u[0] == level]:
            row_norm = rows_ref[r][0:1]
            rows = blocks[r, core, 0:256, :]
            total, refs = acc[r, 0], acc[r, 1]
            for k in range(2):
                inner = lax.dot_general(
                    blocks[c, k, 0:256, :], rows, (((1,), (1,)), ((), ())), preferred_element_type=F32
                )
                norm, mark = columns[c, k, :, :128], columns[c, k, :, 128:]
                norm, mark = jnp.concatenate([norm, norm], 1), jnp.concatenate([mark, mark], 1)
                value = jnp.exp2(((inner + norm) + row_norm) * scale)
                total += jnp.sum(value.reshape(32, 8, 256), 0)
                refs += jnp.sum((value * mark).reshape(32, 8, 256), 0)
            acc[r, 0], acc[r, 1] = total, refs

    for level in range(max(depth), 0, -1):
        here = [s for s in range(1, len(STEPS)) if depth[s] == level]
        waits = [copies.start(acc.at[s], got.at[s], toward(difference(STEPS[s], STEPS[parent[s]]))) for s in here]
        for s, w in zip(here, waits):
            w.wait()
            acc[parent[s]] += got[s]
    row_sums = jnp.sum(acc[0, 0], 0, keepdims=True)
    ref_sums = jnp.sum(acc[0, 1], 0, keepdims=True)
    n_ref = n_ref_ref[0:1, 0:1]
    n_cur = n_total - n_ref
    proof = (ref_sums / n_ref - (row_sums - ref_sums) / n_cur) / (row_sums / n_total)
    out_ref[...] = jnp.broadcast_to(proof, (8, 256))
    basis_copy.wait()


def project_scratch():
    count = len(STEPS)
    return [
        pltpu.VMEM((256, 512), F32),
        pltpu.VMEM((256, 256), BF16),
        pltpu.VMEM((256, 256), BF16),
        pltpu.VMEM((256, 256), F32),
        pltpu.VMEM((count, 2, 272, 256), BF16),
        pltpu.VMEM((count, 2, 256, 256), F32),
        pltpu.VMEM((count, 8, 256), F32),
        pltpu.VMEM((count, 2, 8, 256), F32),
        pltpu.VMEM((count, 2, 8, 256), F32),
    ]


def drift_kernel(
    n_total, n_gram, width_ref, x_hbm, b_hbm, label_ref, basis_out, proj_ref, out_ref,
    x_ref, b_ref, g_ref, s_ref, mean_ref, count_ref, gram_all, load_sem, send, recv, *scratch,
):
    chunks = 4
    lanes = x_ref.shape[1] // chunks
    loads = []
    for i in range(chunks):
        part = slice(i * lanes, (i + 1) * lanes)
        loads.append(pltpu.make_async_copy(x_hbm.at[:, part], x_ref.at[:, part], load_sem.at[i]))
    b_load = pltpu.make_async_copy(b_hbm, b_ref, load_sem.at[chunks])
    for load in (*loads, b_load):
        load.start()
    at, core = place()
    copies = Copies(send, recv)
    greet([device(at, 1 - core), *axis_peers(at, core)])
    gathering = gather(at, core, copies, gram_all)
    gram_part(
        n_total, at, core, copies, gathering, gram_all, loads, b_load, x_ref, b_ref, label_ref, g_ref, s_ref, mean_ref, count_ref,
        *scratch[:n_gram],
    )
    project_part(
        n_total, at, core, copies, gathering, gram_all, b_ref, width_ref, label_ref, x_ref, s_ref, mean_ref, count_ref,
        basis_out, proj_ref, out_ref, load_sem.at[chunks + 1],
        *scratch[n_gram:],
    )


def hand_out_kernel(basis, projected, proof, basis_out, projected_out, proof_out, sems):
    moves = ((basis, basis_out), (projected, projected_out), (proof, proof_out))
    waits = [pltpu.make_async_copy(src, dst, sems.at[i]) for i, (src, dst) in enumerate(moves)]
    for w in waits:
        w.start()
    for w in waits:
        w.wait()


def hand_out(basis, projected, proof):
    arrays = (basis, projected, proof)
    anywhere = [pl.BlockSpec(memory_space=pl.ANY)] * 3
    basis, projected, proof = pl.pallas_call(
        hand_out_kernel,
        out_shape=tuple(jax.ShapeDtypeStruct(a.shape, a.dtype) for a in arrays),
        in_specs=anywhere,
        out_specs=tuple(anywhere),
        scratch_shapes=[pltpu.SemaphoreType.DMA((3,))],
        compiler_params=pltpu.CompilerParams(vmem_limit_bytes=8 * 1024 * 1024),
        name="hand_out",
    )(*arrays)
    return projected, proof[0], basis


def local(n_total, samples, labels, basis_start, width_index):
    gram, project = gram_scratch(), project_scratch()
    n_copies = 102 + 126 + 3 * len(STEPS) - 2
    basis, projected, proof = pl.pallas_call(
        functools.partial(drift_kernel, n_total, len(gram)),
        out_shape=(
            jax.ShapeDtypeStruct((8192, 256), BF16),
            jax.ShapeDtypeStruct((256, 256), BF16),
            jax.ShapeDtypeStruct((8, 256), F32),
        ),
        in_specs=[
            pl.BlockSpec(memory_space=pltpu.SMEM),
            pl.BlockSpec(memory_space=pl.ANY),
            pl.BlockSpec(memory_space=pl.ANY),
            VMEM,
        ],
        out_specs=(pl.BlockSpec(memory_space=pl.ANY), VMEM, VMEM),
        scratch_shapes=[
            pltpu.VMEM((256, 8192), BF16),
            pltpu.VMEM((8192, 256), BF16),
            pltpu.VMEM((256, 128), F32),
            pltpu.VMEM((2, 256, 128), F32),
            pltpu.VMEM((64, 128), F32),
            pltpu.VMEM((8, 128), F32),
            pltpu.VMEM((64, 128, 256), F32),
            pltpu.SemaphoreType.DMA((6,)),
            pltpu.SemaphoreType.DMA((n_copies,)),
            pltpu.SemaphoreType.DMA((n_copies,)),
            *gram,
            *project,
        ],
        compiler_params=pltpu.CompilerParams(collective_id=0, has_side_effects=True, vmem_limit_bytes=LIMIT),
        name="drift",
    )(width_index.reshape(1), samples, basis_start, labels.reshape(1, 256))
    return hand_out(basis, projected, proof)


def solution(mesh):
    n_total = float(256 * mesh.size)
    placed = (P(("row", "col"), None), P(("row", "col")), P(), P())
    return jax.shard_map(
        functools.partial(local, n_total),
        mesh=mesh,
        in_specs=placed,
        out_specs=(P(("row", "col"), None), P(("row", "col")), P()),
        check_vma=False,
    )
```

```python
import functools
import itertools

import jax
import jax.numpy as jnp
from jax import lax
from jax.experimental import pallas as pl
from jax.experimental.pallas import tpu as pltpu
from jax.sharding import PartitionSpec as P

MESH = pl.DeviceIdType.MESH
F32 = jnp.float32
BF16 = jnp.bfloat16
VMEM = pl.BlockSpec(memory_space=pltpu.VMEM)
HIGHEST = lax.Precision.HIGHEST
LIMIT = 48 * 1024 * 1024

PARTS = ((0, 48, (0, 1, 2)), (48, 48, (1, 2, 0)), (96, 32, (2, 0, 1)))


def place():
    row, col = lax.axis_index("row"), lax.axis_index("col")
    y, z_lo, core = row // 4, (row // 2) % 2, row % 2
    z_hi, x = col // 4, col % 4
    return (x, y, z_hi * 2 + z_lo), core


def device(at, core):
    x, y, z = at
    return (y * 4 + (z % 2) * 2 + core, (z // 2) * 4 + x)


def moved(at, axis, offset):
    return tuple((c + offset) % 4 if a == axis else c for a, c in enumerate(at))


class Copies:
    def __init__(self, send, recv):
        self.send, self.recv, self.used = send, recv, 0

    def start(self, src, dst, target):
        n = self.used
        self.used += 1
        copy = pltpu.make_async_remote_copy(
            src_ref=src,
            dst_ref=dst,
            send_sem=self.send.at[n],
            recv_sem=self.recv.at[n],
            device_id=target,
            device_id_type=MESH,
        )
        copy.start()
        return copy


def greet(peers):
    barrier = pltpu.get_barrier_semaphore()
    for peer in peers:
        pl.semaphore_signal(barrier, inc=1, device_id=peer, device_id_type=MESH)
    pl.semaphore_wait(barrier, len(peers))


def axis_peers(at, core):
    return [device(moved(at, a, o), core) for a in range(3) for o in (1, 2, 3)]


def pick(axes, at, rows=None):
    index = tuple(at[a] if a in axes else slice(None) for a in range(3))
    return index if rows is None else (*index, rows)


def gram_part(
    n_total, at, core, copies, gathering, gram_all, x_loads, b_load, x_ref, b_ref, label_ref, g_ref, s_ref, mean_ref, count_ref,
    c_ref, local_ref, theirs_ref, note, note_recv, mhalf, mrecv, notes, nrecv, delta_ref, daug, gt, half, recv0,
    q1a, q1b, q1c, o1a, o1b, o1c, t1a, t1b, t1c, q2a, q2b, q2c, o2a, o2b, o2c, t2a, t2b, t2c, r3a, r3b, r3c,
    gme, s_half, sr0, sr1, ss1, sr2, ss2,
):
    other = 1 - core
    partner = device(at, other)
    n_local, width = x_ref.shape
    step = 512
    turns = width // step // len(x_loads)

    for chunk, load in enumerate(x_loads):
        load.wait()

        @pl.loop(chunk * turns, (chunk + 1) * turns)
        def _(j):
            lanes = pl.ds(pl.multiple_of(j * step, step), step)
            m = jnp.sum(x_ref[:, lanes].astype(F32), 0, keepdims=True) * (1.0 / n_local)
            for i in range(step // 128):
                local_ref[pl.ds(step // 128 * j + i, 1), :] = m[:, i * 128 : (i + 1) * 128]

    copy = copies.start(local_ref, theirs_ref, partner)
    ids = lax.broadcasted_iota(jnp.int32, (16, step), 0)

    @pl.loop(0, width // step)
    def _(j):
        lanes = pl.ds(pl.multiple_of(j * step, step), step)
        m = jnp.concatenate([local_ref[pl.ds(step // 128 * j + i, 1), :] for i in range(step // 128)], 1)
        c_ref[0:n_local, lanes] = (x_ref[:, lanes].astype(F32) - m).astype(BF16)
        high = m.astype(BF16).astype(F32)
        middle = (m - high).astype(BF16).astype(F32)
        low = (m - high) - middle
        tile = jnp.where(ids == 0, high, jnp.where(ids == 1, middle, jnp.where(ids == 2, low, 0.0)))
        c_ref[n_local : n_local + 16, lanes] = tile.astype(BF16)

    def start_axis(values, landing, a):
        return [copies.start(values.at[a], landing.at[a, o - 1], device(moved(at, a, o), core)) for o in (1, 2, 3)]

    def end_axis(values, landing, a, waits):
        for w in waits:
            w.wait()
        values[a + 1] = values[a] + landing[a, 0] + landing[a, 1] + landing[a, 2]

    mine = pl.ds(pl.multiple_of(core * 32, 32), 32)
    copy.wait()
    mhalf[0] = local_ref[mine, :] + theirs_ref[mine, :]
    mean_waits = start_axis(mhalf, mrecv, 0)
    b_load.wait()

    first = jnp.dot(c_ref[...], b_ref[...], preferred_element_type=F32)
    t_local = (first[n_local : n_local + 1] + first[n_local + 1 : n_local + 2]) + first[n_local + 2 : n_local + 3]
    is_ref = (label_ref[...] == 0).astype(F32)
    ids = lax.broadcasted_iota(jnp.int32, (8, 128), 0)
    count = jnp.sum(is_ref, 1, keepdims=True)
    note[...] = jnp.where(ids == 0, count, jnp.where(ids == 1, t_local[:, :128], jnp.where(ids == 2, t_local[:, 128:], 0.0)))
    copy_note = copies.start(note, note_recv, partner)
    first_t = first[:n_local].T.astype(BF16)
    far = pl.ds(pl.multiple_of(other * 128, 128), 128)
    near = pl.ds(pl.multiple_of(core * 128, 128), 128)
    halves = []

    def gram_blocks(bx):
        @pl.loop(0, 4)
        def _(by):
            lanes = pl.ds(pl.multiple_of((bx * 4 + by) * 512, 512), 512)
            block = jnp.dot(first_t, c_ref[0:n_local, lanes], preferred_element_type=F32).astype(BF16)
            for bz in range(4):
                gt[bx, by, bz] = block[:, bz * 128 : (bz + 1) * 128]

        halves.append(copies.start(gt.at[bx, :, :, far, :], recv0.at[bx], partner))

    end_axis(mhalf, mrecv, 0, mean_waits)
    mean_waits = start_axis(mhalf, mrecv, 1)
    copy_note.wait()
    notes[0] = note[...] + note_recv[...]
    note_waits = start_axis(notes, nrecv, 0)
    gram_blocks(0)
    end_axis(mhalf, mrecv, 1, mean_waits)
    mean_waits = start_axis(mhalf, mrecv, 2)
    end_axis(notes, nrecv, 0, note_waits)
    note_waits = start_axis(notes, nrecv, 1)
    gram_blocks(1)
    end_axis(mhalf, mrecv, 2, mean_waits)
    mhalf[4] = mhalf[3] * (1.0 / 128.0)
    mean_ref[mine, :] = mhalf[4]
    copy = copies.start(mhalf.at[4], mean_ref.at[mine], partner)
    end_axis(notes, nrecv, 1, note_waits)
    note_waits = start_axis(notes, nrecv, 2)
    gram_blocks(2)
    gram_blocks(3)
    end_axis(notes, nrecv, 2, note_waits)
    totals = notes[3]
    count_ref[...] = totals

    mean_t = totals * (1.0 / 128.0)
    ids = lax.broadcasted_iota(jnp.int32, (16, 256), 0)
    taug = jnp.zeros((16, 256), F32)
    for k, tile in enumerate((note[...], note_recv[...])):
        tau = (tile - mean_t) * float(n_local)
        tau = jnp.concatenate([tau[1:2], tau[2:3]], 1)
        high = tau.astype(BF16).astype(F32)
        taug = jnp.where((ids == 3 * k) | (ids == 3 * k + 1), high, jnp.where(ids == 3 * k + 2, tau - high, taug))
    taug_t = taug.T
    taug_t = jnp.where(core == 0, taug_t[:128], taug_t[128:]).astype(BF16)
    copy.wait()
    delta_ref[...] = jnp.zeros_like(delta_ref)
    for k, source in enumerate((local_ref, theirs_ref)):
        delta = source[...] - mean_ref[...]
        high = delta.astype(BF16).astype(F32)
        delta_ref[:, 3 * k, :] = high
        delta_ref[:, 3 * k + 1, :] = delta - high
        delta_ref[:, 3 * k + 2, :] = high
    daug[...] = delta_ref[...].astype(BF16)

    for bx in range(4):
        halves[bx].wait()

        @pl.loop(0, 4)
        def _(by):
            for bz in range(4):
                extra = jnp.dot(taug_t, daug[(bx * 4 + by) * 4 + bz], preferred_element_type=F32)
                both = gt[bx, by, bz, near, :].astype(F32) + recv0[bx, by, bz].astype(F32)
                half[bx, by, bz] = (both + extra).astype(BF16)

    def exchange(parts, dtype, source, incoming, outgoing, result):
        todo = []
        for i, (axis, size) in enumerate(parts):
            up, down = device(moved(at, axis, 1), core), device(moved(at, axis, 3), core)
            chunks = [source(i, (at[axis] + o) % 4) for o in range(4)]
            low, high = pl.ds(0, 2), pl.ds(2, 2)
            box = incoming[i]
            first_up = copies.start(chunks[2].at[low], box.at[0], up)
            first_down = copies.start(chunks[2].at[high], box.at[1], down)
            near_up = copies.start(chunks[1].at[high], box.at[2], up)
            near_down = copies.start(chunks[3].at[low], box.at[3], down)
            todo.append((up, down, chunks, first_up, first_down, near_up, near_down))
        last = []
        for i, (up, down, chunks, first_up, first_down, _, _) in enumerate(todo):
            box, out = incoming[i], outgoing[i]
            first_up.wait()
            out[0] = chunks[1][0:2] + box[0]
            add_up = copies.start(out.at[0], box.at[4], up)
            first_down.wait()
            out[1] = chunks[3][2:4] + box[1]
            add_down = copies.start(out.at[1], box.at[5], down)
            last.append((add_up, add_down))
        for i, (_, _, chunks, _, _, near_up, near_down) in enumerate(todo):
            box = incoming[i]
            near_up.wait()
            near_down.wait()
            for w in last[i]:
                w.wait()
            own = chunks[0]
            result[i][0:2] = (own[0:2].astype(F32) + box[3].astype(F32)) + box[4].astype(F32)
            result[i][2:4] = (own[2:4].astype(F32) + box[2].astype(F32)) + box[5].astype(F32)

    orders = [order for _, _, order in PARTS]
    t1s, t2s = (t1a, t1b, t1c), (t2a, t2b, t2c)

    def stage_one(i, k):
        start, size, order = PARTS[i]
        to = tuple(k for _ in range(3))
        return half.at[pick(order[:1], to, slice(start, start + size))]

    def stage_two(i, k):
        _, _, order = PARTS[i]
        left = [a for a in range(3) if a != order[0]]
        return t1s[i].at[k] if left[0] == order[1] else t1s[i].at[:, k]

    exchange([(o[0], 0) for o in orders], BF16, stage_one, (q1a, q1b, q1c), (o1a, o1b, o1c), t1s)
    exchange([(o[1], 0) for o in orders], F32, stage_two, (q2a, q2b, q2c), (o2a, o2b, o2c), t2s)
    waits = []
    for (start, size, order), t2, r3 in zip(PARTS, t2s, (r3a, r3b, r3c)):
        for o in (1, 2, 3):
            to = moved(at, order[2], o)
            waits.append(copies.start(t2.at[to[order[2]]], r3.at[o - 1], device(to, core)))
    for w in waits:
        w.wait()
    for (start, size, order), t2, r3 in zip(PARTS, t2s, (r3a, r3b, r3c)):
        total = (t2[at[order[2]]] + r3[0]) + (r3[1] + r3[2])
        gme[start : start + size, :] = total * (1.0 / n_total)
    g_ref[near, :] = gme[...]
    copies.start(gme, g_ref.at[near], partner).wait()
    gram_all[chip_number(at)] = g_ref[...].T
    next(gathering)

    square = lax.dot_general(
        gme[...], g_ref[...], (((1,), (1,)), ((), ())), precision=HIGHEST, preferred_element_type=F32
    )
    s_half[0] = square[:, :128]
    s_half[1] = square[:, 128:]
    plans = ((0, (0, 1, 2)), (1, (1, 2, 0)))

    def band(h, position, size):
        return pl.ds(pl.multiple_of(position * size, size), size)

    waits = []
    for h, order in plans:
        for o in (1, 2, 3):
            to = moved(at, order[0], o)
            waits.append(
                copies.start(s_half.at[h, band(h, to[order[0]], 32), :], sr0.at[h, o - 1], device(to, core))
            )
    for w in waits:
        w.wait()
    waits = []
    for h, order in plans:
        ss1[h] = (s_half[h, band(h, at[order[0]], 32), :] + sr0[h, 0]) + (sr0[h, 1] + sr0[h, 2])
        for o in (1, 2, 3):
            to = moved(at, order[1], o)
            waits.append(copies.start(ss1.at[h, band(h, to[order[1]], 8), :], sr1.at[h, o - 1], device(to, core)))
    for w in waits:
        w.wait()
    waits = []
    for h, order in plans:
        ss2[h] = (ss1[h, band(h, at[order[1]], 8), :] + sr1[h, 0]) + (sr1[h, 1] + sr1[h, 2])
        for o in (1, 2, 3):
            waits.append(copies.start(ss2.at[h], sr2.at[h, at[order[2]]], device(moved(at, order[2], o), core)))
        sr2[h, at[order[2]]] = ss2[h]
    next(gathering)
    for w in waits:
        w.wait()
    bases = [core * 128 + at[order[0]] * 32 + at[order[1]] * 8 for _, order in plans]
    for (h, order), base in zip(plans, bases):
        s_ref[h, pl.ds(pl.multiple_of(base, 8), 8), :] = (sr2[h, 0] + sr2[h, 1]) + (sr2[h, 2] + sr2[h, 3])
    for level in (1, 0):
        waits = []
        for (h, order), base in zip(plans, bases):
            if level:
                rows = pl.ds(pl.multiple_of(base, 8), 8)
            else:
                rows = pl.ds(pl.multiple_of(core * 128 + at[order[0]] * 32, 32), 32)
            view = s_ref.at[h, rows, :]
            waits += [copies.start(view, view, device(moved(at, order[level], o), core)) for o in (1, 2, 3)]
        for w in waits:
            w.wait()
    view = s_ref.at[:, near, :]
    copy = copies.start(view, view, partner)
    next(gathering)
    copy.wait()


def gram_scratch():
    return [
        pltpu.VMEM((272, 8192), BF16),
        pltpu.VMEM((64, 128), F32),
        pltpu.VMEM((64, 128), F32),
        pltpu.VMEM((8, 128), F32),
        pltpu.VMEM((8, 128), F32),
        pltpu.VMEM((5, 32, 128), F32),
        pltpu.VMEM((3, 3, 32, 128), F32),
        pltpu.VMEM((4, 8, 128), F32),
        pltpu.VMEM((3, 3, 8, 128), F32),
        pltpu.VMEM((64, 16, 128), F32),
        pltpu.VMEM((64, 16, 128), BF16),
        pltpu.VMEM((4, 4, 4, 256, 128), BF16),
        pltpu.VMEM((4, 4, 4, 128, 128), BF16),
        pltpu.VMEM((4, 4, 4, 128, 128), BF16),
        *[pltpu.VMEM((6, 2, 4, size, 128), BF16) for _, size, _ in PARTS],
        *[pltpu.VMEM((2, 2, 4, size, 128), BF16) for _, size, _ in PARTS],
        *[pltpu.VMEM((4, 4, size, 128), F32) for _, size, _ in PARTS],
        *[pltpu.VMEM((6, 2, size, 128), F32) for _, size, _ in PARTS],
        *[pltpu.VMEM((2, 2, size, 128), F32) for _, size, _ in PARTS],
        *[pltpu.VMEM((4, size, 128), F32) for _, size, _ in PARTS],
        *[pltpu.VMEM((3, size, 128), F32) for _, size, _ in PARTS],
        pltpu.VMEM((128, 128), F32),
        pltpu.VMEM((2, 128, 128), F32),
        pltpu.VMEM((2, 3, 32, 128), F32),
        pltpu.VMEM((2, 3, 8, 128), F32),
        pltpu.VMEM((2, 32, 128), F32),
        pltpu.VMEM((2, 4, 8, 128), F32),
        pltpu.VMEM((2, 8, 128), F32),
    ]


def small_inverse(t):
    sub = lax.broadcasted_iota(jnp.int32, (8, 128), 0)
    t = list(t)
    for s in range(4):
        rows = [jnp.broadcast_to(t[s][i : i + 1, :], (8, 128)) for i in range(8)]
        e = [[jnp.broadcast_to(rows[i][:, 8 * s + j : 8 * s + j + 1], (8, 128)) for j in range(i + 1)] for i in range(8)]
        inv, low = [], [[None] * 8 for _ in range(8)]
        for j in range(8):
            inv.append(1.0 / e[j][j])
            for i in range(j + 1, 8):
                low[i][j] = e[i][j] * inv[j]
            for i in range(j + 1, 8):
                for m in range(j + 1, i + 1):
                    e[i][m] = e[i][m] - low[i][j] * e[m][j]
        w = []
        for i in range(8):
            v = rows[i]
            for j in range(i):
                v = v - low[i][j] * w[j]
            w.append(v)
        for b in range(s + 1, 4):
            f = []
            for j in range(8):
                v = jnp.broadcast_to(t[b][:, 8 * s + j : 8 * s + j + 1], (8, 128))
                for k in range(j):
                    v = v - f[k] * e[j][k]
                f.append(v * inv[j])
            for j in range(8):
                t[b] = t[b] - f[j] * w[j]
        out = w[0] * lax.rsqrt(e[0][0])
        for i in range(1, 8):
            out = jnp.where(sub == i, w[i] * lax.rsqrt(e[i][i]), out)
        t[s] = out
    return t


def inverse_factor(s_ref, m_ref, gathering):
    r = lax.broadcasted_iota(jnp.int32, (256, 256), 0)
    c = lax.broadcasted_iota(jnp.int32, (256, 256), 1)
    m_ref[:, 0:128] = s_ref[0]
    m_ref[:, 128:256] = s_ref[1]
    m_ref[:, 256:512] = (r == c).astype(F32)
    lane = lax.broadcasted_iota(jnp.int32, (32, 128), 1)
    unit = (lane == lax.broadcasted_iota(jnp.int32, (32, 128), 0) + 32).astype(F32)
    for b in range(8):
        left = 128 * (b // 4)
        rows, window = slice(32 * b, 32 * b + 32), slice(left, left + 384)
        tile = m_ref[rows, left : left + 128]
        if b % 4:
            tile = pltpu.roll(tile, 128 - 32 * (b % 4), 1)
        tile = jnp.where(lane < 32, tile, unit)
        t = small_inverse([tile[8 * i : 8 * i + 8] for i in range(4)])
        inv = jnp.concatenate(t, 0)[:, 32:64]
        w = jnp.dot(inv, m_ref[rows, window], precision=HIGHEST, preferred_element_type=F32)
        if b < 7:
            update = lax.dot_general(
                w[:, : 256 - left], w, (((0,), (0,)), ((), ())), precision=HIGHEST, preferred_element_type=F32
            )
            m_ref[32 * b + 32 :, window] -= update[32 * b + 32 - left :]
        m_ref[rows, window] = w
        if b in (2, 5, 7):
            next(gathering)


STEPS = ((0, 0, 0), (3, 0, 0), (0, 0, 3), (0, 1, 0), (2, 0, 0), (0, 3, 3), (3, 0, 1), (1, 1, 0), (0, 2, 3), (0, 0, 2), (2, 0, 1), (0, 2, 0))
PARENTS = ((0, 0, 0), (0, 0, 0), (0, 0, 0), (3, 0, 0), (0, 0, 3), (3, 0, 0), (0, 1, 0), (0, 3, 3), (0, 0, 3), (2, 0, 0), (0, 1, 0))


def difference(a, b):
    return tuple((i - j) % 4 for i, j in zip(a, b))


def panel_plan():
    parent = [None, *[STEPS.index(p) for p in PARENTS]]
    depth = [0] * len(STEPS)
    for s in range(1, len(STEPS)):
        depth[s] = depth[parent[s]] + 1
    best = {}
    for r, row in enumerate(STEPS):
        for c, column in enumerate(STEPS):
            d = difference(row, column)
            cost = (max(depth[r], depth[c]), depth[r] + depth[c], r)
            if d not in best or cost < best[d][0]:
                best[d] = (cost, r, c)
    units = sorted((cost[0], r, c) for cost, r, c in best.values())
    assert len(units) == 64
    return parent, depth, units


def spanning_tree():
    def far(step):
        return sum(min(c, 4 - c) for c in step)

    steps = sorted(itertools.product(range(4), repeat=3), key=lambda step: (far(step), step))
    load = {(a, o): 0 for a in range(3) for o in (1, 3)}
    parent = [None]
    for step in steps[1:]:
        choices = []
        for (a, o), used in load.items():
            before = moved(step, a, 4 - o)
            if far(before) == far(step) - 1:
                choices.append((used, a, o, steps.index(before)))
        _, a, o, before = min(choices)
        load[a, o] += 1
        parent.append(before)
    return steps, parent, [far(step) for step in steps]


def chip_number(at):
    return (at[0] * 4 + at[1]) * 4 + at[2]


def gather(at, core, copies, ref):
    steps, source, level_of = spanning_tree()
    partner = device(at, 1 - core)
    half = pl.ds(pl.multiple_of(core * 64, 64), 64)

    def moved_by(step):
        return tuple((c + i) % 4 for c, i in zip(at, step))

    links, across = {}, {}
    for level in range(7):
        for s in range(64):
            if level_of[s] != level:
                continue
            if s:
                links[s].wait()
            view = ref.at[chip_number(moved_by(steps[s])), half, :]
            for child in range(1, 64):
                if source[child] == s:
                    target = device(moved_by(difference(steps[s], steps[child])), core)
                    links[child] = copies.start(view, view, target)
            if s:
                across[s] = copies.start(view, view, partner)
        yield
    for s in range(1, 64):
        across[s].wait()
    yield


def project_part(
    n_total, at, core, copies, gathering, gram_all, basis_ref, width_ref, label_ref, x_ref, s_ref, mean_ref, n_ref_ref,
    basis_out, proj_ref, out_ref, basis_sem,
    m_ref, inv_high, inv_low, p_acc, blocks, columns, rows_ref, acc, got,
):
    other = 1 - core
    partner = device(at, other)
    parent, depth, units = panel_plan()

    def toward(step):
        return device(tuple((c + i) % 4 for c, i in zip(at, step)), core)

    inverse_factor(s_ref, m_ref, gathering)
    for _ in gathering:
        pass
    inverse_t = m_ref[:, 256:512].T
    high = inverse_t.astype(BF16)
    inv_high[...] = high
    inv_low[...] = (inverse_t - high.astype(F32)).astype(BF16)
    p_acc[...] = jnp.zeros_like(p_acc)

    @pl.loop(0, 16)
    def _(j):
        chips = pl.ds(4 * j, 4)
        gram = gram_all[chips].reshape(512, 256)
        high = gram.astype(BF16)
        low = (gram - high.astype(F32)).astype(BF16)
        block = jnp.dot(low, inv_high[...], preferred_element_type=F32)
        block += jnp.dot(high, inv_low[...], preferred_element_type=F32)
        block += jnp.dot(high, inv_high[...], preferred_element_type=F32)
        block = block.astype(BF16)
        lanes = pl.ds(pl.multiple_of(j * 512, 512), 512)
        basis_ref[lanes, :] = block
        mean = jnp.concatenate([mean_ref[pl.ds(4 * j + i, 1), :] for i in range(4)], 1)
        centred = (x_ref[:, lanes].astype(F32) - mean).astype(BF16)
        p_acc[...] += jnp.dot(centred, block, preferred_element_type=F32)

    basis_copy = pltpu.make_async_copy(basis_ref, basis_out, basis_sem)
    basis_copy.start()
    p = p_acc[...].astype(BF16)
    proj_ref[...] = p
    wide = p.astype(F32)
    norm = jnp.broadcast_to(jnp.sum(wide * wide, 1, keepdims=True) * -0.5, (256, 128)).T
    norm = jnp.concatenate([norm[:128, :128], norm[:128, 128:]], 1)[0:1]
    high = norm.astype(BF16).astype(F32)
    middle = (norm - high).astype(BF16).astype(F32)
    low = (norm - high) - middle
    is_ref = (label_ref[...] == 0).astype(F32)
    ids = lax.broadcasted_iota(jnp.int32, (16, 256), 0)
    tail = jnp.where(ids == 0, is_ref, jnp.where(ids == 1, high, jnp.where(ids == 2, middle, jnp.where(ids == 3, low, 0.0))))
    blocks[0, core, 0:256, :] = p
    blocks[0, core, 256:272, :] = tail.astype(BF16)

    edges, cores = {}, {}

    def hand_on(s):
        view = blocks.at[s, core]
        for child in range(1, len(STEPS)):
            if parent[child] == s:
                target = toward(difference(STEPS[s], STEPS[child]))
                edges[child] = copies.start(view, blocks.at[child, core], target)
        cores[s] = copies.start(view, view, partner)

    scale = 1.4426950408889634 / (128.0 * jnp.exp2(jnp.full((1, 256), width_ref[0], jnp.int32).astype(F32)))
    ids = lax.broadcasted_iota(jnp.int32, (16, 256), 0)
    lanes = lax.broadcasted_iota(jnp.int32, (16, 256), 1)
    select = jnp.where(lanes < 128, jnp.where((ids > 0) & (ids < 4), 1.0, 0.0), jnp.where(ids == 0, 1.0, 0.0)).astype(BF16)

    def prepare(s):
        for k in range(2):
            ends = blocks[s, k, 256:272, :].astype(F32).T.astype(BF16)
            columns[s, k] = jnp.dot(ends, select, preferred_element_type=F32)
        ends = blocks[s, core, 256:272, :].astype(F32)
        rows_ref[s] = jnp.broadcast_to((ends[1:2] + ends[2:3]) + ends[3:4], (8, 256))

    for s in range(len(STEPS)):
        acc[s, 0] = jnp.zeros((8, 256), F32)
        acc[s, 1] = jnp.zeros((8, 256), F32)
    hand_on(0)
    for level in range(max(depth) + 1):
        here = [s for s in range(len(STEPS)) if depth[s] == level]
        for s in here:
            if s:
                edges[s].wait()
                hand_on(s)
        for s in here:
            cores[s].wait()
            prepare(s)
        for _, r, c in [u for u in units if u[0] == level]:
            row_norm = rows_ref[r][0:1]
            rows = blocks[r, core, 0:256, :]
            total, refs = acc[r, 0], acc[r, 1]
            for k in range(2):
                inner = lax.dot_general(
                    blocks[c, k, 0:256, :], rows, (((1,), (1,)), ((), ())), preferred_element_type=F32
                )
                norm, mark = columns[c, k, :, :128], columns[c, k, :, 128:]
                norm, mark = jnp.concatenate([norm, norm], 1), jnp.concatenate([mark, mark], 1)
                value = jnp.exp2(((inner + norm) + row_norm) * scale)
                total += jnp.sum(value.reshape(32, 8, 256), 0)
                refs += jnp.sum((value * mark).reshape(32, 8, 256), 0)
            acc[r, 0], acc[r, 1] = total, refs

    def axes(step):
        return sum(c != 0 for c in step)

    waits = []
    for s in range(1, len(STEPS)):
        if axes(STEPS[s]) == 2:
            onto = [q for q in range(1, len(STEPS)) if axes(STEPS[q]) == 1 and axes(difference(STEPS[s], STEPS[q])) == 1][0]
            waits.append((s, onto, copies.start(acc.at[s], got.at[s], toward(difference(STEPS[s], STEPS[onto])))))
    for _, _, w in waits:
        w.wait()
    for s, onto, _ in waits:
        acc[onto] += got[s]
    straight = [s for s in range(1, len(STEPS)) if axes(STEPS[s]) == 1]
    waits = [copies.start(acc.at[s], got.at[s], toward(STEPS[s])) for s in straight]
    for w in waits:
        w.wait()
    for s in straight:
        acc[0] += got[s]
    row_sums = jnp.sum(acc[0, 0], 0, keepdims=True)
    ref_sums = jnp.sum(acc[0, 1], 0, keepdims=True)
    n_ref = n_ref_ref[0:1, 0:1]
    n_cur = n_total - n_ref
    proof = (ref_sums / n_ref - (row_sums - ref_sums) / n_cur) / (row_sums / n_total)
    out_ref[...] = jnp.broadcast_to(proof, (8, 256))
    basis_copy.wait()


def project_scratch():
    count = len(STEPS)
    return [
        pltpu.VMEM((256, 512), F32),
        pltpu.VMEM((256, 256), BF16),
        pltpu.VMEM((256, 256), BF16),
        pltpu.VMEM((256, 256), F32),
        pltpu.VMEM((count, 2, 272, 256), BF16),
        pltpu.VMEM((count, 2, 256, 256), F32),
        pltpu.VMEM((count, 8, 256), F32),
        pltpu.VMEM((count, 2, 8, 256), F32),
        pltpu.VMEM((count, 2, 8, 256), F32),
    ]


def drift_kernel(
    n_total, n_gram, width_ref, x_hbm, b_hbm, label_ref, basis_out, proj_ref, out_ref,
    x_ref, b_ref, g_ref, s_ref, mean_ref, count_ref, gram_all, load_sem, send, recv, *scratch,
):
    chunks = 4
    lanes = x_ref.shape[1] // chunks
    loads = []
    for i in range(chunks):
        part = slice(i * lanes, (i + 1) * lanes)
        loads.append(pltpu.make_async_copy(x_hbm.at[:, part], x_ref.at[:, part], load_sem.at[i]))
    b_load = pltpu.make_async_copy(b_hbm, b_ref, load_sem.at[chunks])
    for load in (*loads, b_load):
        load.start()
    at, core = place()
    copies = Copies(send, recv)
    greet([device(at, 1 - core), *axis_peers(at, core)])
    gathering = gather(at, core, copies, gram_all)
    gram_part(
        n_total, at, core, copies, gathering, gram_all, loads, b_load, x_ref, b_ref, label_ref, g_ref, s_ref, mean_ref, count_ref,
        *scratch[:n_gram],
    )
    project_part(
        n_total, at, core, copies, gathering, gram_all, b_ref, width_ref, label_ref, x_ref, s_ref, mean_ref, count_ref,
        basis_out, proj_ref, out_ref, load_sem.at[chunks + 1],
        *scratch[n_gram:],
    )


def hand_out_kernel(basis, projected, proof, basis_out, projected_out, proof_out, sems):
    moves = ((basis, basis_out), (projected, projected_out), (proof, proof_out))
    waits = [pltpu.make_async_copy(src, dst, sems.at[i]) for i, (src, dst) in enumerate(moves)]
    for w in waits:
        w.start()
    for w in waits:
        w.wait()


def hand_out(basis, projected, proof):
    arrays = (basis, projected, proof)
    anywhere = [pl.BlockSpec(memory_space=pl.ANY)] * 3
    basis, projected, proof = pl.pallas_call(
        hand_out_kernel,
        out_shape=tuple(jax.ShapeDtypeStruct(a.shape, a.dtype) for a in arrays),
        in_specs=anywhere,
        out_specs=tuple(anywhere),
        scratch_shapes=[pltpu.SemaphoreType.DMA((3,))],
        compiler_params=pltpu.CompilerParams(vmem_limit_bytes=8 * 1024 * 1024),
        name="hand_out",
    )(*arrays)
    return projected, proof[0], basis


def local(n_total, samples, labels, basis_start, width_index):
    gram, project = gram_scratch(), project_scratch()
    n_copies = 102 + 126 + 3 * len(STEPS) - 2
    basis, projected, proof = pl.pallas_call(
        functools.partial(drift_kernel, n_total, len(gram)),
        out_shape=(
            jax.ShapeDtypeStruct((8192, 256), BF16),
            jax.ShapeDtypeStruct((256, 256), BF16),
            jax.ShapeDtypeStruct((8, 256), F32),
        ),
        in_specs=[
            pl.BlockSpec(memory_space=pltpu.SMEM),
            pl.BlockSpec(memory_space=pl.ANY),
            pl.BlockSpec(memory_space=pl.ANY),
            VMEM,
        ],
        out_specs=(pl.BlockSpec(memory_space=pl.ANY), VMEM, VMEM),
        scratch_shapes=[
            pltpu.VMEM((256, 8192), BF16),
            pltpu.VMEM((8192, 256), BF16),
            pltpu.VMEM((256, 128), F32),
            pltpu.VMEM((2, 256, 128), F32),
            pltpu.VMEM((64, 128), F32),
            pltpu.VMEM((8, 128), F32),
            pltpu.VMEM((64, 128, 256), F32),
            pltpu.SemaphoreType.DMA((6,)),
            pltpu.SemaphoreType.DMA((n_copies,)),
            pltpu.SemaphoreType.DMA((n_copies,)),
            *gram,
            *project,
        ],
        compiler_params=pltpu.CompilerParams(collective_id=0, has_side_effects=True, vmem_limit_bytes=LIMIT),
        name="drift",
    )(width_index.reshape(1), samples, basis_start, labels.reshape(1, 256))
    return hand_out(basis, projected, proof)


def solution(mesh):
    n_total = float(256 * mesh.size)
    placed = (P(("row", "col"), None), P(("row", "col")), P(), P())
    return jax.shard_map(
        functools.partial(local, n_total),
        mesh=mesh,
        in_specs=placed,
        out_specs=(P(("row", "col"), None), P(("row", "col")), P()),
        check_vma=False,
    )
```
